512 devices in a mesh: tm: 32 (over z, core), bat: 16 (over y, x).
Axes of the slice: x: 4, y: 4, z: 16, core: 2. Of those that a mesh axis runs over, the one named last changes fastest.
Arguments:
- power0: float32 [512, 6144], P('tm', 'bat'), may hold values from -0.5 to 0.5
- charge0: float32 [512, 6144], P('tm', 'bat'), may hold values from 0 to 1
- dyn_dual0: float32 [512, 6144], P('tm', 'bat'), may hold values from -3 to 3
- feeder_dual0: float32 [512, 3072], P(('tm', 'bat')), may hold values from 0 to 0.5
- price: float32 [512, 6144], P('tm', 'bat'), may hold values from -12 to 12
- inflow: float32 [512, 6144], P('tm', 'bat'), may hold values from -1.5 to 1.5
- power_limit: float32 [6144], P('bat'), may hold values from 0.5 to 6
- capacity: float32 [6144], P('bat'), may hold values from 0.5 to 8
- feeder_limit: float32 [3072], replicated, may hold values from 0 to 1
- block_values: float32 [72, 128, 128], replicated, may hold values from -0.3125 to 0.3125
- block_cols: int32 [72], replicated, may hold values from 0 to 47, as said below
- block_offsets: int32 [25], replicated, may hold values from 0 to 72, as said below
Outputs:
- power: float32 [512, 6144], P('tm', 'bat')
- charge: float32 [512, 6144], P('tm', 'bat')
- dyn_dual: float32 [512, 6144], P('tm', 'bat')
- feeder_dual: float32 [512, 3072], P(('tm', 'bat'))
The draws below stay inside these ranges and needn't reach their ends.
Inputs may be any that keep to these rules, and one draw needn't show every extreme that they name: `block_cols`: every battery block 0 to 47 appears at least once. block_offsets[0] = 0, strictly rising, block_offsets[24] = 72.
All inputs are finite; a program needn't handle non-finite values.
Results may differ from the reference program's by a relative error of at most 0.0001.
Values sent between devices are 32-bit elements; how exact they have to be, the bound alone decides.
No kernel may reach another device: no remote copies, remote signals or barrier semaphores. Data moves between devices by JAX's collectives and lax.ppermute only.
A program may use at most 64 MiB of HBM per device.

```python
import math
import jax
import jax.numpy as jnp
from jax import lax

BLK = 128
ITERS = 4
T_SIZE = 512
B = 6144
NB = 48
FEED_BLK = 24
NNZB = 72
FR = 3072


def draw_price(key, part):
    ramp = 1.0 + 2.0 * jnp.arange(T_SIZE, dtype=jnp.float32) / max(T_SIZE - 1, 1)
    base = jnp.clip(jax.random.normal(key, (T_SIZE, B), jnp.float32), -3.5, 3.5)
    return base * ramp[:, None]


def draw_power_limit(key, part):
    ramp = 1.0 + 2.0 * jnp.arange(B, dtype=jnp.float32) / max(B - 1, 1)
    base = jnp.exp(jax.random.uniform(key, (B,), jnp.float32, jnp.log(0.5), jnp.log(2.0)))
    return base * ramp


def draw_block_cols(key, part):
    first = jax.random.permutation(jax.random.fold_in(key, 11), NB)
    extra = jax.random.randint(jax.random.fold_in(key, 12), (NNZB - NB,), 0, NB)
    joined = jnp.concatenate([first, extra]).astype(jnp.int32)
    return jax.random.permutation(jax.random.fold_in(key, 13), joined).astype(jnp.int32)


def draw_block_offsets(key, part):
    picks = jax.random.permutation(jax.random.fold_in(key, 21), NNZB - 1)[:FEED_BLK - 1] + 1
    cuts = jnp.sort(picks.astype(jnp.int32))
    head = jnp.zeros((1,), jnp.int32)
    tail = jnp.full((1,), NNZB, jnp.int32)
    return jnp.concatenate([head, cuts, tail]).astype(jnp.int32)


def block_levels(rng, dims, shards, low, high):
    factor_of, own = 1.0, jax.random.fold_in(rng, 6)
    for dim, parts in shards:
        heights = jnp.exp(jax.random.uniform(jax.random.fold_in(own, dim), (parts,), jnp.float32, low / len(shards), high / len(shards)))
        factor_of = factor_of * jnp.repeat(heights, dims[dim] // parts).reshape([-1 if axis == dim else 1 for axis in range(len(dims))])
    return factor_of


def noise(own_key, extent, deviation, reach, pieces=(), kind=jnp.bfloat16):
    loudness = block_levels(own_key, extent, pieces, -0.22, 0.18) if pieces else 1.0
    result = jax.random.normal(own_key, extent, jnp.float32) * deviation * loudness
    return jnp.minimum(jnp.maximum(result, -reach), reach).astype(kind)


def setup_inputs(seed: int = 0) -> dict:
    key_list = jax.random.split(jax.random.key(seed), 13)
    return {
        "power0": jnp.clip(jax.random.uniform(key_list[0], (T_SIZE, B), jnp.float32, -0.5, 0.5) * block_levels(key_list[0], (T_SIZE, B), ((0, 32), (1, 16)), -0.4, 0.0), -0.5, 0.5),
        "charge0": jnp.clip(1.0 * jax.random.uniform(key_list[1], (T_SIZE, B), jnp.float32) ** block_levels(key_list[1], (T_SIZE, B), ((0, 32), (1, 16)), -0.2, 0.2), 0.0, 1.0),
        "dyn_dual0": noise(key_list[2], (T_SIZE, B), 0.5, 3.0, ((0, 32), (1, 16)), jnp.float32),
        "feeder_dual0": jnp.clip(0.5 * jax.random.uniform(key_list[3], (T_SIZE, FR), jnp.float32) ** block_levels(key_list[3], (T_SIZE, FR), ((0, 512),), -0.2, 0.2), 0.0, 0.5),
        "price": draw_price(jax.random.fold_in(key_list[12], 71), 0),
        "inflow": noise(key_list[5], (T_SIZE, B), 0.3, 1.5, ((0, 32), (1, 16)), jnp.float32),
        "power_limit": draw_power_limit(jax.random.fold_in(key_list[12], 71), 0),
        "capacity": jnp.clip(jnp.exp(math.log(8.0) - 2.7725887 * jax.random.uniform(key_list[7], (B,), jnp.float32) ** block_levels(key_list[7], (B,), ((0, 16),), -0.2, 0.2)), 0.5, 8.0),
        "feeder_limit": jnp.clip(jax.random.uniform(key_list[8], (FR,), jnp.float32, 0.0, 1.0), 0.0, 1.0),
        "block_values": noise(key_list[9], (NNZB, BLK, BLK), (3 * BLK) ** -0.5, 0.3125, (), jnp.float32),
        "block_cols": draw_block_cols(jax.random.fold_in(key_list[12], 71), 0),
        "block_offsets": draw_block_offsets(jax.random.fold_in(key_list[12], 71), 0),
    }


HIGH = lax.Precision.HIGHEST
ETA_STEP = 0.4
EPS_NORM = 1e-06

def row_table(block_offsets, count, dtype):
    index_all = jnp.arange(count, dtype=jnp.int32)
    row_of = lax.optimization_barrier(jnp.sum((index_all[:, None] >= block_offsets[None, 1:-1]).astype(jnp.int32), axis=1))
    feed_count = block_offsets.shape[0] - 1
    return (row_of[:, None] == jnp.arange(feed_count, dtype=jnp.int32)[None, :]).astype(dtype)

def column_table(block_cols, battery_blocks, dtype):
    return (block_cols[:, None] == jnp.arange(battery_blocks, dtype=jnp.int32)[None, :]).astype(dtype)

def feeder_apply(field, block_values, rows_tab, cols_tab):
    count_rows = field.shape[0]
    blk = block_values.shape[1]
    blocks = field.reshape(count_rows, -1, blk)
    picked = jnp.einsum('rnk,jn->rjk', blocks, cols_tab, precision=HIGH)
    partial_rows = jnp.einsum('rjk,jmk->rjm', picked, block_values, precision=HIGH)
    summed = jnp.einsum('rjm,jf->rfm', partial_rows, rows_tab, precision=HIGH)
    return summed.reshape(count_rows, -1)

def feeder_adjoint(duals, block_values, rows_tab, cols_tab):
    count_rows = duals.shape[0]
    blk = block_values.shape[1]
    blocks = duals.reshape(count_rows, -1, blk)
    chosen = jnp.einsum('rfm,jf->rjm', blocks, rows_tab, precision=HIGH)
    pushed = jnp.einsum('rjm,jmk->rjk', chosen, block_values, precision=HIGH)
    spread = jnp.einsum('rjk,jn->rnk', pushed, cols_tab, precision=HIGH)
    return spread.reshape(count_rows, -1)

def reference(power0, charge0, dyn_dual0, feeder_dual0, price, inflow, power_limit, capacity, feeder_limit, block_values, block_cols, block_offsets):
    dtype = power0.dtype
    blk = block_values.shape[1]
    rows_tab = row_table(block_offsets, block_values.shape[0], dtype)
    cols_tab = column_table(block_cols, power0.shape[1] // blk, dtype)
    power, charge, dyn_dual, feeder_dual = (power0, charge0, dyn_dual0, feeder_dual0)
    weight = jnp.asarray(1.0, dtype=dtype)
    pushed = feeder_adjoint(feeder_dual, block_values, rows_tab, cols_tab)
    zero_row = jnp.zeros((1, power0.shape[1]), dtype)
    for iteration in range(ITERS):
        step_primal = ETA_STEP / weight
        step_dual = ETA_STEP * weight
        dual_next = jnp.concatenate([dyn_dual[1:], zero_row], axis=0)
        power_new = jnp.clip(power - step_primal * (price - dyn_dual + pushed), -power_limit[None, :], power_limit[None, :])
        charge_new = jnp.clip(charge - step_primal * (dyn_dual - dual_next), 0.0, capacity[None, :])
        power_bar = 2.0 * power_new - power
        charge_bar = 2.0 * charge_new - charge
        charge_prev = jnp.concatenate([zero_row, charge_bar[:-1]], axis=0)
        dyn_new = dyn_dual + step_dual * (charge_bar - charge_prev - power_bar - inflow)
        feeder_new = jnp.maximum(0.0, feeder_dual + step_dual * (feeder_apply(power_bar, block_values, rows_tab, cols_tab) - feeder_limit[None, :]))
        if iteration + 1 < ITERS:
            move_power = power_new - power
            move_charge = charge_new - charge
            primal_sq = jnp.sum(move_power * move_power + move_charge * move_charge)
            move_dyn = dyn_new - dyn_dual
            move_feed = feeder_new - feeder_dual
            dual_sq = jnp.sum(move_dyn * move_dyn) + jnp.sum(move_feed * move_feed)
            weight = jnp.sqrt(weight * jnp.sqrt((dual_sq + EPS_NORM) / (primal_sq + EPS_NORM)))
            pushed = feeder_adjoint(feeder_new, block_values, rows_tab, cols_tab)
        power, charge, dyn_dual, feeder_dual = (power_new, charge_new, dyn_new, feeder_new)
    return (power, charge, dyn_dual, feeder_dual)
```

```python
import functools

import jax
import jax.numpy as jnp
from jax import lax
from jax.experimental import pallas as pl
from jax.experimental.pallas import tpu as pltpu
from jax.sharding import PartitionSpec as P

ITERS = 4
ETA_STEP = 0.4
EPS_NORM = 1e-06
LANES = 128
HALF = LANES // 2
F32 = jnp.float32

VMEM = pl.BlockSpec(memory_space=pltpu.VMEM)
SMEM = pl.BlockSpec(memory_space=pltpu.SMEM)

POWER, CHARGE, DYN, PRICE, INFLOW, DYN_NEXT, DYN_PREV, CHARGE_PREV, LIMIT, CAPACITY = range(10)


def rows_up(count):
    return -(-count // 8) * 8


def lane_iota(shape):
    return lax.broadcasted_iota(jnp.int32, shape, len(shape) - 1)


def clip(value, low, high):
    return jnp.minimum(jnp.maximum(value, low), high)


def total(value):
    return jnp.sum(jnp.sum(value, axis=0, keepdims=True), axis=1, keepdims=True)


def take_row(ref, array, pieces, groups, slot_rows):
    parts = [ref[pl.ds(array * pieces + i, groups, stride=slot_rows), :] for i in range(pieces)]
    return jnp.concatenate(parts, axis=0)


def put_row(ref, array, value, pieces, groups, slot_rows):
    for i in range(pieces):
        ref[pl.ds(array * pieces + i, groups, stride=slot_rows), :] = value[i * groups : (i + 1) * groups]


def row_of_block(block, pieces, groups):
    return (block % pieces) * groups + block // pieces


def feeder_adjoint(values, cols, offsets, duals_t, spread, sums, pieces, groups):
    blk = values.shape[1]
    for f in range(spread.shape[0]):
        spread[f] = jnp.broadcast_to(duals_t[:, f : f + 1], spread.shape[1:])
    sums[...] = jnp.zeros_like(sums)

    def step(j, f):
        f = jnp.where(j == offsets[f + 1], f + 1, f)
        product = values[j] * spread[f]
        c = row_of_block(cols[j], pieces, groups)
        sums[c] = sums[c] + jnp.sum(product.reshape(blk // 8, 8, LANES), axis=0)
        return f

    lax.fori_loop(0, values.shape[0], step, 0, unroll=4)
    return jnp.sum(sums[...], axis=1)


def feeder_apply(values, cols, offsets, field, sums, pieces, groups):
    blk = values.shape[1]

    def step(j, carry):
        f, acc = carry
        fresh = j == offsets[f + 1]
        f = jnp.where(fresh, f + 1, f)
        keep = jnp.where(fresh, 0.0, 1.0).astype(F32)
        c = row_of_block(cols[j], pieces, groups)
        acc = acc * keep + values[j] * field[pl.ds(c, 1), :]
        sums[f] = acc
        return f, acc

    lax.fori_loop(0, values.shape[0], step, (0, jnp.zeros((blk, LANES), F32)), unroll=4)
    lane = lane_iota((blk, LANES))
    out = jnp.zeros((blk, LANES), F32)
    for f in range(sums.shape[0]):
        out = jnp.where(lane == f, jnp.sum(sums[f], axis=1, keepdims=True), out)
    return out


def pack_sums(primal, dual):
    lane = lane_iota(primal.shape)
    return jnp.where(
        lane < HALF, primal + pltpu.roll(primal, HALF, 1), dual + pltpu.roll(dual, HALF, 1)
    )


def next_weight(weight, parts):
    both = jnp.sum(parts, axis=0, keepdims=True)
    lane = lane_iota(both.shape)
    primal_sq = total(jnp.where(lane < HALF, both, 0.0))
    dual_sq = total(jnp.where(lane < HALF, 0.0, both))
    ratio = jnp.sqrt((dual_sq + EPS_NORM) / (primal_sq + EPS_NORM))
    return jnp.broadcast_to(jnp.sqrt(weight[:, :1] * ratio), (1, LANES))


def row_sum(value):
    return jnp.sum(value, axis=0, keepdims=True)


def first_duals_kernel(dims, duals, limits, values, cols, offsets, pushed, duals_t, limits_t, spread, sums):
    blk = values.shape[1]
    feeds = duals.shape[0]
    for source, target in ((duals, duals_t), (limits, limits_t)):
        padded = jnp.concatenate([source[...], jnp.zeros((blk - feeds, LANES), F32)], axis=0)
        target[...] = jnp.transpose(padded)
    pushed[...] = feeder_adjoint(values, cols, offsets, duals_t[...], spread, sums, *dims[:2])


def slots_kernel(dims, power, charge, dyn, price, inflow, limit, capacity, after, before, slots):
    pieces, groups, slot_rows = dims
    arrays = {POWER: power, CHARGE: charge, DYN: dyn, PRICE: price, INFLOW: inflow}
    for i in range(pieces):
        cut = slice(i * LANES, (i + 1) * LANES)
        for array, ref in arrays.items():
            slots[pl.ds(array * pieces + i, groups, stride=slot_rows), :] = ref[:, cut]
        for array, ref in ((LIMIT, limit), (CAPACITY, capacity)):
            slots[pl.ds(array * pieces + i, groups, stride=slot_rows), :] = jnp.broadcast_to(
                ref[:, cut], (groups, LANES)
            )
        last = (groups - 1) * slot_rows
        slots[pl.ds(DYN_NEXT * pieces + i, groups - 1, stride=slot_rows), :] = dyn[1:, cut]
        slots[last + DYN_NEXT * pieces + i, :] = after[0, cut]
        for array, ref, line in ((DYN_PREV, dyn, 0), (CHARGE_PREV, charge, 1)):
            slots[pl.ds(slot_rows + array * pieces + i, groups - 1, stride=slot_rows), :] = ref[:-1, cut]
            slots[array * pieces + i, :] = before[line, cut]


def row_step(weight, first, power, charge, dyn, dyn_next, dyn_prev, charge_prev, pushed, price, inflow, limit, capacity):
    step_primal = ETA_STEP / weight[:, :1]
    step_dual = ETA_STEP * weight[:, :1]
    power_new = clip(power - step_primal * (price - dyn + pushed), -limit, limit)
    charge_new = clip(charge - step_primal * (dyn - dyn_next), 0.0, capacity)
    prev_new = clip(charge_prev - step_primal * (dyn_prev - dyn), 0.0, capacity)
    power_bar = 2.0 * power_new - power
    charge_bar = 2.0 * charge_new - charge
    prev_bar = jnp.where(first, 0.0, 2.0 * prev_new - charge_prev)
    dyn_new = dyn + step_dual * (charge_bar - prev_bar - power_bar - inflow)
    primal = row_sum((power_new - power) ** 2 + (charge_new - charge) ** 2)
    dual = row_sum((dyn_new - dyn) ** 2)
    return power_new, charge_new, dyn_new, prev_new, power_bar, primal, dual


def first_step():
    return (lax.axis_index("tm") == 0) & (lax.axis_index("bat") == 0)


def first_row_kernel(dims, slots, pushed, weight, power_out, charge_out, dyn_out, prev_out, bar_out, primal_out, dual_out):
    take = lambda array: take_row(slots, array, *dims)
    weight[...] = jnp.ones_like(weight)
    results = row_step(
        weight[...], first_step(), take(POWER), take(CHARGE), take(DYN), take(DYN_NEXT), take(DYN_PREV),
        take(CHARGE_PREV), pushed[...], take(PRICE), take(INFLOW), take(LIMIT), take(CAPACITY),
    )
    for ref, value in zip((power_out, charge_out, dyn_out, prev_out, bar_out, primal_out, dual_out), results):
        ref[...] = value


def row_kernel(dims, slots, parts, weight_in, power, charge, dyn, dyn_next, dyn_prev, charge_prev, pushed,
               weight, power_out, charge_out, dyn_out, prev_out, bar_out, primal_out, dual_out):
    take = lambda array: take_row(slots, array, *dims)
    weight[...] = next_weight(weight_in[...], parts[...])
    results = row_step(
        weight[...], first_step(), power[...], charge[...], dyn[...], dyn_next[...], dyn_prev[...],
        charge_prev[...], pushed[...], take(PRICE), take(INFLOW), take(LIMIT), take(CAPACITY),
    )
    for ref, value in zip((power_out, charge_out, dyn_out, prev_out, bar_out, primal_out, dual_out), results):
        ref[...] = value


def feeder_step(weight, coupled, duals_t, limits_t):
    step_dual = ETA_STEP * weight[:, :1]
    return jnp.maximum(0.0, duals_t + step_dual * (coupled - limits_t))


def feeder_kernel(dims, weight, bar, primal, dual, duals_t, limits_t, values, cols, offsets,
                  pushed, duals_out, parts, spread, sums):
    pieces, groups = dims[:2]
    coupled = feeder_apply(values, cols, offsets, bar, spread, pieces, groups)
    new = feeder_step(weight[...], coupled, duals_t[...], limits_t[...])
    duals_out[...] = new
    parts[...] = pack_sums(primal[...], dual[...] + row_sum((new - duals_t[...]) ** 2))
    pushed[...] = feeder_adjoint(values, cols, offsets, new, spread, sums, pieces, groups)


def back_kernel(dims, back_rows, weight, power, charge, dyn, bar, primal, dual, duals_t, limits_t, values, cols,
                offsets, pushed, duals_out, slots, spread, sums):
    pieces, groups = dims[:2]
    coupled = feeder_apply(values, cols, offsets, bar, spread, pieces, groups)
    new = feeder_step(weight[...], coupled, duals_t[...], limits_t[...])
    duals_out[...] = new
    parts = pack_sums(primal[...], dual[...] + row_sum((new - duals_t[...]) ** 2))
    slots[pl.ds(4 * pieces, groups, stride=back_rows), :] = jnp.broadcast_to(parts, (groups, LANES))
    adjoint = feeder_adjoint(values, cols, offsets, new, spread, sums, pieces, groups)
    pushed[...] = adjoint
    for array, value in enumerate((power[...], charge[...], dyn[...], adjoint)):
        put_row(slots, array, value, pieces, groups, back_rows)


def last_kernel(dims, back_rows, slots, parts, weight_in, power, dyn, pushed, duals_t, limits_t, values, cols,
                offsets, back, price, inflow, limit, capacity, after, before,
                power_out, charge_out, dyn_out, duals_out, bar, sums):
    pieces, groups, slot_rows = dims
    take = lambda array: take_row(slots, array, *dims)
    weight = next_weight(weight_in[...], parts[...])
    step_primal = ETA_STEP / weight[:, :1]
    step_dual = ETA_STEP * weight[:, :1]
    row_limit = take(LIMIT)
    row_new = clip(power[...] - step_primal * (take(PRICE) - dyn[...] + pushed[...]), -row_limit, row_limit)
    bar[...] = 2.0 * row_new - power[...]
    first = lax.axis_index("tm") == 0
    row = lax.broadcasted_iota(jnp.int32, (groups, LANES), 0)
    for i in range(pieces):
        cut = slice(i * LANES, (i + 1) * LANES)
        old = [back[pl.ds(array * pieces + i, groups, stride=back_rows), :] for array in range(4)]
        o_power, o_charge, o_dyn, o_pushed = old
        o_limit, o_capacity = limit[:, cut], capacity[:, cut]
        power_new = clip(o_power - step_primal * (price[:, cut] - o_dyn + o_pushed), -o_limit, o_limit)
        dyn_next = jnp.where(row == groups - 1, after[i : i + 1, :], pltpu.roll(o_dyn, groups - 1, 0))
        charge_new = clip(o_charge - step_primal * (o_dyn - dyn_next), 0.0, o_capacity)
        power_bar = 2.0 * power_new - o_power
        charge_bar = 2.0 * charge_new - o_charge
        edge_charge, edge_dyn = before[i : i + 1, :], before[pieces + i : pieces + i + 1, :]
        edge_new = clip(edge_charge - step_primal * (edge_dyn - o_dyn[:1]), 0.0, o_capacity)
        edge_bar = jnp.where(first, 0.0, 2.0 * edge_new - edge_charge)
        prev_bar = jnp.where(row == 0, edge_bar, pltpu.roll(charge_bar, 1, 0))
        dyn_new = o_dyn + step_dual * (charge_bar - prev_bar - power_bar - inflow[:, cut])
        power_out[:, cut] = power_new
        charge_out[:, cut] = charge_new
        dyn_out[:, cut] = dyn_new
    coupled = feeder_apply(values, cols, offsets, bar, sums, pieces, groups)
    new = feeder_step(weight, coupled, duals_t[...], limits_t[...])
    duals_out[...] = jnp.transpose(new)[: duals_out.shape[0]]


def shapes(*dims):
    return [jax.ShapeDtypeStruct(dim, F32) for dim in dims]


def call(kernel, name, in_specs, out_dims, scratch=(), flops=0, moved=0):
    return pl.pallas_call(
        kernel,
        name=name,
        in_specs=in_specs,
        out_specs=[VMEM] * len(out_dims),
        out_shape=shapes(*out_dims),
        scratch_shapes=[pltpu.VMEM(dim, F32) for dim in scratch],
        compiler_params=pltpu.CompilerParams(vmem_limit_bytes=24 * 1024 * 1024),
        cost_estimate=pl.CostEstimate(flops=flops, bytes_accessed=moved, transcendentals=0),
    )


def moved_to(value, axis, distance):
    count = lax.axis_size(axis)
    return lax.ppermute(value, axis, [(i, i + distance) for i in range(count) if 0 <= i + distance < count])


def exchange(value, axis):
    return lax.all_to_all(value, axis, 0, 0, tiled=True)


def shards(power0, charge0, dyn_dual0, feeder_dual0, price, inflow, power_limit, capacity, feeder_limit,
           block_values, block_cols, block_offsets):
    groups, local = power0.shape
    pieces = local // LANES
    blocks, blk = block_values.shape[:2]
    feeds = block_offsets.shape[0] - 1
    steps = lax.axis_size("tm")
    slot_rows = rows_up(10 * pieces)
    back_rows = rows_up(4 * pieces + 1)
    dims = (pieces, groups, slot_rows)
    row = (pieces * groups, LANES)
    line = (1, LANES)
    square = (blk, LANES)
    spread, sums = (feeds, blk, LANES), (pieces * groups, 8, LANES)
    matrix = (block_values, block_cols, block_offsets)
    matrix_specs = [VMEM, SMEM, SMEM]
    work = 2 * blocks * blk * LANES
    limit_line, capacity_line = power_limit.reshape(1, local), capacity.reshape(1, local)

    after = moved_to(dyn_dual0[:1], "tm", -1)
    before = moved_to(jnp.concatenate([dyn_dual0[-1:], charge0[-1:]], axis=0), "tm", 1)
    pushed, duals_t, limits_t = call(
        functools.partial(first_duals_kernel, dims), "first_duals",
        [VMEM, VMEM] + matrix_specs, [row, square, square], [spread, sums], work, 4 * blocks * blk * LANES,
    )(feeder_dual0.reshape(feeds, blk), feeder_limit.reshape(feeds, blk), *matrix)
    slots = call(
        functools.partial(slots_kernel, dims), "slots", [VMEM] * 9, [(groups * slot_rows, LANES)],
    )(power0, charge0, dyn_dual0, price, inflow, limit_line, capacity_line, after, before)[0]
    slots = exchange(slots.reshape(groups, slot_rows, LANES), "bat").reshape(groups * slot_rows, LANES)

    row_outs = [line] + [row] * 5 + [line] * 2
    weight, power, charge, dyn, charge_prev, bar, primal, dual = call(
        functools.partial(first_row_kernel, dims), "first_row", [VMEM] * 2, row_outs
    )(slots, pushed)

    for iteration in range(1, ITERS):
        if iteration + 1 < ITERS:
            dyn_next = moved_to(dyn, ("tm", "bat"), -1)
            dyn_prev = moved_to(dyn, ("tm", "bat"), 1)
            pushed, duals_t, parts = call(
                functools.partial(feeder_kernel, dims), "feeder",
                [VMEM] * 6 + matrix_specs, [row, square, line], [spread, sums], 2 * work, 4 * blocks * blk * LANES,
            )(weight, bar, primal, dual, duals_t, limits_t, *matrix)
            parts = exchange(jnp.broadcast_to(parts[None], (groups, 1, LANES)), "bat")
            parts = jnp.sum(parts, axis=0, keepdims=True)
            parts = exchange(jnp.broadcast_to(parts, (steps, 1, LANES)), "tm").reshape(steps, LANES)
            weight, power, charge, dyn, charge_prev, bar, primal, dual = call(
                functools.partial(row_kernel, dims), "row", [VMEM] * 10, row_outs
            )(slots, parts, weight, power, charge, dyn, dyn_next, dyn_prev, charge_prev, pushed)
        else:
            pushed, duals_t, back = call(
                functools.partial(back_kernel, dims, back_rows), "feeder_back",
                [VMEM] * 9 + matrix_specs, [row, square, (groups * back_rows, LANES)], [spread, sums], 2 * work,
                4 * blocks * blk * LANES,
            )(weight, power, charge, dyn, bar, primal, dual, duals_t, limits_t, *matrix)
            back = exchange(back.reshape(groups, back_rows, LANES), "bat")
            after = moved_to(back[0, 2 * pieces : 3 * pieces], "tm", -1)
            before = moved_to(back[-1, pieces : 3 * pieces], "tm", 1)
            parts = jnp.sum(back[:, 4 * pieces : 4 * pieces + 1], axis=0, keepdims=True)
            parts = exchange(jnp.broadcast_to(parts, (steps, 1, LANES)), "tm").reshape(steps, LANES)

    power, charge, dyn_dual, feeder_dual = call(
        functools.partial(last_kernel, dims, back_rows), "last",
        [VMEM] * 8 + matrix_specs + [VMEM] * 7,
        [(groups, local)] * 3 + [(feeds, blk)], [row, spread], work, 4 * blocks * blk * LANES,
    )(slots, parts, weight, power, dyn, pushed, duals_t, limits_t, *matrix,
      back.reshape(groups * back_rows, LANES), price, inflow, limit_line, capacity_line, after, before)
    return power, charge, dyn_dual, feeder_dual.reshape(1, feeds * blk)


def solution(mesh):
    split = P("tm", "bat")
    steps = P(("tm", "bat"), None)
    return jax.shard_map(
        shards,
        mesh=mesh,
        in_specs=(split, split, split, steps, split, split, P("bat"), P("bat"), P(), P(), P(), P()),
        out_specs=(split, split, split, steps),
        check_vma=False,
    )
```

```python
import functools

import jax
import jax.numpy as jnp
from jax import lax
from jax.experimental import pallas as pl
from jax.experimental.pallas import tpu as pltpu
from jax.sharding import PartitionSpec as P

ITERS = 4
ETA_STEP = 0.4
EPS_NORM = 1e-06
LANES = 128
HALF = LANES // 2
F32 = jnp.float32

VMEM = pl.BlockSpec(memory_space=pltpu.VMEM)
SMEM = pl.BlockSpec(memory_space=pltpu.SMEM)

POWER, CHARGE, DYN, PRICE, INFLOW, LIMIT, CAPACITY, DYN_NEXT, DYN_PREV, CHARGE_PREV = range(10)


def rows_up(count):
    return -(-count // 8) * 8


def lane_iota(shape):
    return lax.broadcasted_iota(jnp.int32, shape, len(shape) - 1)


def clip(value, low, high):
    return jnp.minimum(jnp.maximum(value, low), high)


def total(value):
    return jnp.sum(jnp.sum(value, axis=0, keepdims=True), axis=1, keepdims=True)


def take_row(ref, array, pieces, groups, slot_rows):
    parts = [ref[pl.ds(array * pieces + i, groups, stride=slot_rows), :] for i in range(pieces)]
    return jnp.concatenate(parts, axis=0)


def put_row(ref, array, value, pieces, groups, slot_rows):
    for i in range(pieces):
        ref[pl.ds(array * pieces + i, groups, stride=slot_rows), :] = value[i * groups : (i + 1) * groups]


def row_of_block(block, pieces, groups):
    return (block % pieces) * groups + block // pieces


def feeder_adjoint(values, table, duals_t, spread, sums, pieces, groups):
    blocks, blk = values.shape[:2]
    for f in range(spread.shape[0]):
        spread[f] = jnp.broadcast_to(duals_t[:, f : f + 1], spread.shape[1:])
    sums[...] = jnp.zeros_like(sums)

    def step(j, f):
        f = jnp.where(j == table[blocks + f + 1], f + 1, f)
        product = values[j] * spread[f]
        c = row_of_block(table[j], pieces, groups)
        sums[c] = sums[c] + jnp.sum(product.reshape(blk // 8, 8, LANES), axis=0)
        return f

    lax.fori_loop(0, blocks, step, 0, unroll=4)
    return jnp.sum(sums[...], axis=1)


def feeder_apply(values, table, field, sums, pieces, groups):
    blocks, blk = values.shape[:2]

    def step(j, carry):
        f, acc = carry
        fresh = j == table[blocks + f + 1]
        f = jnp.where(fresh, f + 1, f)
        keep = jnp.where(fresh, 0.0, 1.0).astype(F32)
        c = row_of_block(table[j], pieces, groups)
        acc = acc * keep + values[j] * field[pl.ds(c, 1), :]
        sums[f] = acc
        return f, acc

    lax.fori_loop(0, blocks, step, (0, jnp.zeros((blk, LANES), F32)), unroll=4)
    lane = lane_iota((blk, LANES))
    out = jnp.zeros((blk, LANES), F32)
    for f in range(sums.shape[0]):
        out = jnp.where(lane == f, jnp.sum(sums[f], axis=1, keepdims=True), out)
    return out


def pack_sums(primal, dual):
    lane = lane_iota(primal.shape)
    return jnp.where(
        lane < HALF, primal + pltpu.roll(primal, HALF, 1), dual + pltpu.roll(dual, HALF, 1)
    )


def next_weight(weight, parts):
    both = jnp.sum(parts, axis=0, keepdims=True)
    lane = lane_iota(both.shape)
    primal_sq = total(jnp.where(lane < HALF, both, 0.0))
    dual_sq = total(jnp.where(lane < HALF, 0.0, both))
    ratio = jnp.sqrt((dual_sq + EPS_NORM) / (primal_sq + EPS_NORM))
    return jnp.broadcast_to(jnp.sqrt(weight[:, :1] * ratio), (1, LANES))


def row_sum(value):
    return jnp.sum(value, axis=0, keepdims=True)


def first_duals_kernel(dims, duals, values, table, pushed, duals_t, limits_t, spread, sums):
    blk = values.shape[1]
    feeds = duals.shape[1]
    for i, target in enumerate((duals_t, limits_t)):
        padded = jnp.concatenate([duals[i], jnp.zeros((blk - feeds, LANES), F32)], axis=0)
        target[...] = jnp.transpose(padded)
    pushed[...] = feeder_adjoint(values, table, duals_t[...], spread, sums, *dims[:2])


def slots_kernel(dims, inputs, after, before, slots):
    pieces, groups, slot_rows = dims
    last = (groups - 1) * slot_rows
    for i in range(pieces):
        cut = slice(i * LANES, (i + 1) * LANES)
        for array in range(inputs.shape[0]):
            slots[pl.ds(array * pieces + i, groups, stride=slot_rows), :] = inputs[array, :, cut]
        slots[pl.ds(DYN_NEXT * pieces + i, groups - 1, stride=slot_rows), :] = inputs[DYN, 1:, cut]
        slots[last + DYN_NEXT * pieces + i, :] = after[0, cut]
        for array, source in ((DYN_PREV, DYN), (CHARGE_PREV, CHARGE)):
            slots[pl.ds(slot_rows + array * pieces + i, groups - 1, stride=slot_rows), :] = inputs[source, :-1, cut]
            slots[array * pieces + i, :] = before[source - CHARGE, cut]


def row_step(weight, first, power, charge, dyn, dyn_next, dyn_prev, charge_prev, pushed, price, inflow, limit, capacity):
    step_primal = ETA_STEP / weight[:, :1]
    step_dual = ETA_STEP * weight[:, :1]
    power_new = clip(power - step_primal * (price - dyn + pushed), -limit, limit)
    charge_new = clip(charge - step_primal * (dyn - dyn_next), 0.0, capacity)
    prev_new = clip(charge_prev - step_primal * (dyn_prev - dyn), 0.0, capacity)
    power_bar = 2.0 * power_new - power
    charge_bar = 2.0 * charge_new - charge
    prev_bar = jnp.where(first, 0.0, 2.0 * prev_new - charge_prev)
    dyn_new = dyn + step_dual * (charge_bar - prev_bar - power_bar - inflow)
    primal = row_sum((power_new - power) ** 2 + (charge_new - charge) ** 2)
    dual = row_sum((dyn_new - dyn) ** 2)
    return power_new, charge_new, dyn_new, prev_new, power_bar, primal, dual


def first_step():
    return (lax.axis_index("tm") == 0) & (lax.axis_index("bat") == 0)


def first_row_kernel(dims, slots, pushed, weight, power_out, charge_out, dyn_out, prev_out, bar_out, primal_out, dual_out):
    take = lambda array: take_row(slots, array, *dims)
    weight[...] = jnp.ones_like(weight)
    results = row_step(
        weight[...], first_step(), take(POWER), take(CHARGE), take(DYN), take(DYN_NEXT), take(DYN_PREV),
        take(CHARGE_PREV), pushed[...], take(PRICE), take(INFLOW), take(LIMIT), take(CAPACITY),
    )
    for ref, value in zip((power_out, charge_out, dyn_out, prev_out, bar_out, primal_out, dual_out), results):
        ref[...] = value


def row_kernel(dims, slots, parts, weight_in, power, charge, dyn, dyn_next, dyn_prev, charge_prev, pushed,
               weight, power_out, charge_out, dyn_out, prev_out, bar_out, primal_out, dual_out):
    take = lambda array: take_row(slots, array, *dims)
    weight[...] = next_weight(weight_in[...], parts[...])
    results = row_step(
        weight[...], first_step(), power[...], charge[...], dyn[...], dyn_next[...], dyn_prev[...],
        charge_prev[...], pushed[...], take(PRICE), take(INFLOW), take(LIMIT), take(CAPACITY),
    )
    for ref, value in zip((power_out, charge_out, dyn_out, prev_out, bar_out, primal_out, dual_out), results):
        ref[...] = value


def feeder_step(weight, coupled, duals_t, limits_t):
    step_dual = ETA_STEP * weight[:, :1]
    return jnp.maximum(0.0, duals_t + step_dual * (coupled - limits_t))


def feeder_kernel(dims, weight, bar, primal, dual, duals_t, limits_t, values, table,
                  pushed, duals_out, parts, spread, sums):
    pieces, groups = dims[:2]
    coupled = feeder_apply(values, table, bar, spread, pieces, groups)
    new = feeder_step(weight[...], coupled, duals_t[...], limits_t[...])
    duals_out[...] = new
    parts[...] = pack_sums(primal[...], dual[...] + row_sum((new - duals_t[...]) ** 2))
    pushed[...] = feeder_adjoint(values, table, new, spread, sums, pieces, groups)


def back_kernel(dims, back_rows, parts, *rest):
    pieces, groups = dims[:2]
    arrays, slots = rest[:-1], rest[-1]
    for array, ref in enumerate(arrays):
        put_row(slots, array, ref[...], pieces, groups, back_rows)
    slots[pl.ds(len(arrays) * pieces, groups, stride=back_rows), :] = jnp.broadcast_to(parts[...], (groups, LANES))


def relay_kernel(start, stride, received, parts):
    count = received.shape[0] // stride
    summed = jnp.sum(received[pl.ds(start, count, stride=stride), :], axis=0, keepdims=True)
    parts[...] = jnp.broadcast_to(summed, parts.shape)


def last_kernel(dims, back_rows, slots, parts, weight_in, power, dyn, pushed, duals_t, limits_t, values, table,
                back, inputs,
                power_out, charge_out, dyn_out, duals_out, bar, sums):
    pieces, groups, slot_rows = dims
    take = lambda array: take_row(slots, array, *dims)
    weight = next_weight(weight_in[...], parts[...])
    step_primal = ETA_STEP / weight[:, :1]
    row_limit = take(LIMIT)
    row_new = clip(power[...] - step_primal * (take(PRICE) - dyn[...] + pushed[...]), -row_limit, row_limit)
    bar[...] = 2.0 * row_new - power[...]
    first = (lax.axis_index("tm") == 0) & (lax.broadcasted_iota(jnp.int32, (groups, LANES), 0) == 0)
    for i in range(pieces):
        cut = slice(i * LANES, (i + 1) * LANES)
        state = [back[pl.ds(array * pieces + i, groups, stride=back_rows), :] for array in range(7)]
        results = row_step(
            weight, first, *state, *(inputs[array, :, cut] for array in (PRICE, INFLOW, LIMIT, CAPACITY))
        )
        for ref, value in zip((power_out, charge_out, dyn_out), results):
            ref[:, cut] = value
    coupled = feeder_apply(values, table, bar, sums, pieces, groups)
    new = feeder_step(weight, coupled, duals_t[...], limits_t[...])
    duals_out[...] = jnp.transpose(new)[: duals_out.shape[0]]


def shapes(*dims):
    return [jax.ShapeDtypeStruct(dim, F32) for dim in dims]


def call(kernel, name, in_specs, out_dims, scratch=(), flops=0, moved=0):
    return pl.pallas_call(
        kernel,
        name=name,
        in_specs=in_specs,
        out_specs=[VMEM] * len(out_dims),
        out_shape=shapes(*out_dims),
        scratch_shapes=[pltpu.VMEM(dim, F32) for dim in scratch],
        compiler_params=pltpu.CompilerParams(vmem_limit_bytes=16 * 1024 * 1024),
        cost_estimate=pl.CostEstimate(flops=flops, bytes_accessed=moved, transcendentals=0),
    )


def stacked(*arrays):
    shape = (len(arrays),) + arrays[0].shape
    index = lax.broadcasted_iota(jnp.int32, shape, 0)
    out = jnp.broadcast_to(arrays[-1], shape)
    for i, array in enumerate(arrays[:-1]):
        out = jnp.where(index == i, array, out)
    return out


def moved_to(value, axis, distance):
    count = lax.axis_size(axis)
    return lax.ppermute(value, axis, [(i, i + distance) for i in range(count) if 0 <= i + distance < count])


def exchange(value, axis):
    return lax.all_to_all(value, axis, 0, 0, tiled=True)


def shards(power0, charge0, dyn_dual0, feeder_dual0, price, inflow, power_limit, capacity, feeder_limit,
           block_values, block_cols, block_offsets):
    groups, local = power0.shape
    pieces = local // LANES
    blocks, blk = block_values.shape[:2]
    feeds = block_offsets.shape[0] - 1
    steps = lax.axis_size("tm")
    slot_rows = rows_up(10 * pieces)
    back_rows = rows_up(7 * pieces + 1)
    dims = (pieces, groups, slot_rows)
    row = (pieces * groups, LANES)
    line = (1, LANES)
    square = (blk, LANES)
    own = (groups, local)
    spread, sums = (feeds, blk, LANES), (pieces * groups, 8, LANES)
    matrix_specs = [VMEM, SMEM]
    work, moved = 2 * blocks * blk * LANES, 4 * blocks * blk * LANES
    inputs = stacked(power0, charge0, dyn_dual0, price, inflow, power_limit, capacity)
    duals = stacked(feeder_dual0.reshape(feeds, blk), feeder_limit.reshape(feeds, blk))
    matrix = (block_values, jnp.concatenate([block_cols, block_offsets]))

    after = moved_to(inputs[DYN, :1], "tm", -1)
    before = moved_to(inputs[CHARGE : DYN + 1, -1], "tm", 1)
    pushed, duals_t, limits_t = call(
        functools.partial(first_duals_kernel, dims), "first_duals",
        [VMEM] + matrix_specs, [row, square, square], [spread, sums], work, moved,
    )(duals, *matrix)
    pushed, after, before = lax.optimization_barrier((pushed, after, before))
    slots = call(
        functools.partial(slots_kernel, dims), "slots", [VMEM] * 3, [(groups * slot_rows, LANES)],
    )(inputs, after, before)[0]
    slots = exchange(slots.reshape(groups, slot_rows, LANES), "bat").reshape(groups * slot_rows, LANES)

    row_outs = [line] + [row] * 5 + [line] * 2
    weight, power, charge, dyn, charge_prev, bar, primal, dual = call(
        functools.partial(first_row_kernel, dims), "first_row", [VMEM] * 2, row_outs
    )(slots, pushed)

    for iteration in range(1, ITERS):
        dyn_next = moved_to(dyn, ("tm", "bat"), -1)
        dyn_prev = moved_to(dyn, ("tm", "bat"), 1)
        pushed, duals_t, parts = call(
            functools.partial(feeder_kernel, dims), "feeder",
            [VMEM] * 6 + matrix_specs, [row, square, line], [spread, sums], 2 * work, moved,
        )(weight, bar, primal, dual, duals_t, limits_t, *matrix)
        parts, dyn_next, dyn_prev = lax.optimization_barrier((parts, dyn_next, dyn_prev))
        if iteration + 1 < ITERS:
            received = exchange(jnp.broadcast_to(parts[None], (groups, 1, LANES)), "bat").reshape(groups, LANES)
            relay = functools.partial(relay_kernel, 0, 1)
        else:
            back = call(
                functools.partial(back_kernel, dims, back_rows), "back", [VMEM] * 8, [(groups * back_rows, LANES)]
            )(parts, power, charge, dyn, dyn_next, dyn_prev, charge_prev, pushed)[0]
            back = exchange(back.reshape(groups, back_rows, LANES), "bat").reshape(groups * back_rows, LANES)
            received = back
            relay = functools.partial(relay_kernel, 7 * pieces, back_rows)
        parts = call(relay, "relay", [VMEM], [(steps, LANES)])(received)[0]
        parts = exchange(parts.reshape(steps, 1, LANES), "tm").reshape(steps, LANES)
        if iteration + 1 < ITERS:
            weight, power, charge, dyn, charge_prev, bar, primal, dual = call(
                functools.partial(row_kernel, dims), "row", [VMEM] * 10, row_outs
            )(slots, parts, weight, power, charge, dyn, dyn_next, dyn_prev, charge_prev, pushed)

    power, charge, dyn_dual, feeder_dual = call(
        functools.partial(last_kernel, dims, back_rows), "last",
        [VMEM] * 8 + matrix_specs + [VMEM] * 2, [own] * 3 + [(feeds, blk)], [row, spread], work, moved,
    )(slots, parts, weight, power, dyn, pushed, duals_t, limits_t, *matrix,
      back, inputs)
    return power, charge, dyn_dual, feeder_dual.reshape(1, feeds * blk)


def solution(mesh):
    split = P("tm", "bat")
    steps = P(("tm", "bat"), None)
    return jax.shard_map(
        shards,
        mesh=mesh,
        in_specs=(split, split, split, steps, split, split, P("bat"), P("bat"), P(), P(), P(), P()),
        out_specs=(split, split, split, steps),
        check_vma=False,
    )
```

```python
import functools

import jax
import jax.numpy as jnp
from jax import lax
from jax.experimental import pallas as pl
from jax.experimental.pallas import tpu as pltpu
from jax.sharding import PartitionSpec as P

ITERS = 4
ETA_STEP = 0.4
EPS_NORM = 1e-06
LANES = 128
HALF = LANES // 2
F32 = jnp.float32

VMEM = pl.BlockSpec(memory_space=pltpu.VMEM)
SMEM = pl.BlockSpec(memory_space=pltpu.SMEM)

POWER, CHARGE, DYN, PRICE, INFLOW, LIMIT, CAPACITY = range(7)
SLOT_DYN, SLOT_PUSHED, SLOT_POWER, SLOT_PRICE, SLOT_LIMIT = range(5)


def rows_up(count):
    return -(-count // 8) * 8


def lane_iota(shape):
    return lax.broadcasted_iota(jnp.int32, shape, len(shape) - 1)


def clip(value, low, high):
    return jnp.minimum(jnp.maximum(value, low), high)


def total(value):
    return jnp.sum(jnp.sum(value, axis=0, keepdims=True), axis=1, keepdims=True)


def take_row(ref, array, pieces, groups, slot_rows):
    parts = [ref[pl.ds(array * pieces + i, groups, stride=slot_rows), :] for i in range(pieces)]
    return jnp.concatenate(parts, axis=0)


def put_row(ref, array, value, pieces, groups, slot_rows):
    for i in range(pieces):
        ref[pl.ds(array * pieces + i, groups, stride=slot_rows), :] = value[i * groups : (i + 1) * groups]


def row_of_block(block, pieces, groups):
    return (block % pieces) * groups + block // pieces


def feeder_adjoint(values, table, duals_t, spread, sums, pieces, groups):
    blocks, blk = values.shape[:2]
    for f in range(spread.shape[0]):
        spread[f] = jnp.broadcast_to(duals_t[:, f : f + 1], spread.shape[1:])
    sums[...] = jnp.zeros_like(sums)

    def step(j, f):
        f = jnp.where(j == table[blocks + f + 1], f + 1, f)
        product = values[j] * spread[f]
        c = row_of_block(table[j], pieces, groups)
        sums[c] = sums[c] + jnp.sum(product.reshape(blk // 8, 8, LANES), axis=0)
        return f

    lax.fori_loop(0, blocks, step, 0, unroll=4)
    return jnp.sum(sums[...], axis=1)


def feeder_apply(values, table, field, sums, pieces, groups):
    blocks, blk = values.shape[:2]

    def step(j, carry):
        f, acc = carry
        fresh = j == table[blocks + f + 1]
        f = jnp.where(fresh, f + 1, f)
        keep = jnp.where(fresh, 0.0, 1.0).astype(F32)
        c = row_of_block(table[j], pieces, groups)
        acc = acc * keep + values[j] * field[pl.ds(c, 1), :]
        sums[f] = acc
        return f, acc

    lax.fori_loop(0, blocks, step, (0, jnp.zeros((blk, LANES), F32)), unroll=4)
    lane = lane_iota((blk, LANES))
    out = jnp.zeros((blk, LANES), F32)
    for f in range(sums.shape[0]):
        out = jnp.where(lane == f, jnp.sum(sums[f], axis=1, keepdims=True), out)
    return out


def pack_sums(primal, dual):
    lane = lane_iota(primal.shape)
    return jnp.where(
        lane < HALF, primal + pltpu.roll(primal, HALF, 1), dual + pltpu.roll(dual, HALF, 1)
    )


def next_weight(weight, parts):
    both = jnp.sum(parts, axis=0, keepdims=True)
    lane = lane_iota(both.shape)
    primal_sq = total(jnp.where(lane < HALF, both, 0.0))
    dual_sq = total(jnp.where(lane < HALF, 0.0, both))
    ratio = jnp.sqrt((dual_sq + EPS_NORM) / (primal_sq + EPS_NORM))
    return jnp.broadcast_to(jnp.sqrt(weight[:, :1] * ratio), (1, LANES))


def row_sum(value):
    return jnp.sum(value, axis=0, keepdims=True)


def first_kernel(dims, first_rows, duals, inputs, values, table, slots, duals_t, limits_t, pushed_out, spread, sums):
    pieces, groups = dims
    blk = values.shape[1]
    feeds = duals.shape[1]
    for i, target in enumerate((duals_t, limits_t)):
        padded = jnp.concatenate([duals[i], jnp.zeros((blk - feeds, LANES), F32)], axis=0)
        target[...] = jnp.transpose(padded)
    sent = ((SLOT_DYN, DYN), (SLOT_POWER, POWER), (SLOT_PRICE, PRICE), (SLOT_LIMIT, LIMIT))
    for i in range(pieces):
        for slot, array in sent:
            slots[pl.ds(slot * pieces + i, groups, stride=first_rows), :] = inputs[array, :, i * LANES : (i + 1) * LANES]
    pushed = feeder_adjoint(values, table, duals_t[...], spread, sums, pieces, groups)
    pushed_out[...] = pushed
    put_row(slots, SLOT_PUSHED, pushed, pieces, groups, first_rows)


def local_step(dims, slot_rows, weight, received, inputs, state, edges, state_out, edge_out):
    pieces, groups = dims
    step_primal = ETA_STEP / weight[:, :1]
    step_dual = ETA_STEP * weight[:, :1]
    after, before_dyn, before_charge = edges
    begin = lax.axis_index("tm") == 0
    line = lax.broadcasted_iota(jnp.int32, (groups, LANES), 0)
    primal = jnp.zeros((1, LANES), F32)
    dual = jnp.zeros((1, LANES), F32)
    for i in range(pieces):
        cut = slice(i * LANES, (i + 1) * LANES)
        power, charge, dyn = (read(cut) for read in state)
        price, inflow, limit, capacity = (inputs[array, :, cut] for array in (PRICE, INFLOW, LIMIT, CAPACITY))
        pushed = received[pl.ds(SLOT_PUSHED * pieces + i, groups, stride=slot_rows), :]
        power_new = clip(power - step_primal * (price - dyn + pushed), -limit, limit)
        dyn_next = jnp.where(line == groups - 1, after(i), pltpu.roll(dyn, groups - 1, 0))
        charge_new = clip(charge - step_primal * (dyn - dyn_next), 0.0, capacity)
        power_bar = 2.0 * power_new - power
        charge_bar = 2.0 * charge_new - charge
        edge_charge = before_charge(i)
        edge_new = clip(edge_charge - step_primal * (before_dyn(i) - dyn[:1]), 0.0, capacity[:1])
        edge_bar = jnp.where(begin, 0.0, 2.0 * edge_new - edge_charge)
        prev_bar = jnp.where(line == 0, edge_bar, pltpu.roll(charge_bar, 1, 0))
        dyn_new = dyn + step_dual * (charge_bar - prev_bar - power_bar - inflow)
        for ref, value in zip(state_out, (power_new, charge_new, dyn_new)):
            ref[:, cut] = value
        if edge_out is not None:
            edge_out[:, cut] = edge_new
        primal = primal + row_sum((power_new - power) ** 2 + (charge_new - charge) ** 2)
        dual = dual + row_sum((dyn_new - dyn) ** 2)
    return primal, dual


def feeder_step(weight, coupled, duals_t, limits_t):
    step_dual = ETA_STEP * weight[:, :1]
    return jnp.maximum(0.0, duals_t + step_dual * (coupled - limits_t))


def row_power(dims, first_rows, weight, first, power, dyn, pushed, bar):
    pieces, groups = dims
    step_primal = ETA_STEP / weight[:, :1]
    price = take_row(first, SLOT_PRICE, pieces, groups, first_rows)
    limit = take_row(first, SLOT_LIMIT, pieces, groups, first_rows)
    new = clip(power - step_primal * (price - dyn + pushed), -limit, limit)
    bar[...] = 2.0 * new - power
    return new


def feeder_part(dims, slot_rows, weight, primal, dual, bar, dyn, duals_t, limits_t, values, table,
                duals_out, pushed_out, slots, spread, sums):
    pieces, groups = dims
    coupled = feeder_apply(values, table, bar, spread, pieces, groups)
    new = feeder_step(weight, coupled, duals_t[...], limits_t[...])
    duals_out[...] = new
    parts = pack_sums(primal, dual + row_sum((new - duals_t[...]) ** 2))
    slots[pl.ds(2 * pieces, groups, stride=slot_rows), :] = jnp.broadcast_to(parts, (groups, LANES))
    for i in range(pieces):
        slots[pl.ds(SLOT_DYN * pieces + i, groups, stride=slot_rows), :] = dyn[:, i * LANES : (i + 1) * LANES]
    pushed = feeder_adjoint(values, table, new, spread, sums, pieces, groups)
    pushed_out[...] = pushed
    put_row(slots, SLOT_PUSHED, pushed, pieces, groups, slot_rows)


def step_one_kernel(dims, first_rows, slot_rows, first, after, before, pushed_row, inputs, duals_t, limits_t, values,
                    table, weight, power_row, power_out, charge_out, dyn_out, edge_out, duals_out, pushed_out, slots,
                    bar, spread, sums):
    pieces, groups = dims
    weight[...] = jnp.ones_like(weight)
    state = [lambda cut, array=array: inputs[array, :, cut] for array in (POWER, CHARGE, DYN)]
    edges = [lambda i, ref=ref, k=k: ref[k : k + 1, i * LANES : (i + 1) * LANES]
             for ref, k in ((after, 0), (before, 1), (before, 0))]
    primal, dual = local_step(dims, first_rows, weight[...], first, inputs, state, edges,
                              (power_out, charge_out, dyn_out), edge_out)
    power_row[...] = row_power(dims, first_rows, weight[...], first,
                               take_row(first, SLOT_POWER, pieces, groups, first_rows),
                               take_row(first, SLOT_DYN, pieces, groups, first_rows), pushed_row[...], bar)
    feeder_part(dims, slot_rows, weight[...], primal, dual, bar, dyn_out, duals_t, limits_t, values, table,
                duals_out, pushed_out, slots, spread, sums)


def later_edges(parts, edge_in):
    steps = lax.axis_size("tm")
    here = lax.axis_index("tm")
    lines = parts.shape[0] // steps
    above, below = jnp.minimum(here + 1, steps - 1), jnp.maximum(here - 1, 0)
    after = lambda i: jnp.where(here == steps - 1, 0.0, parts[pl.ds(above * lines + 1 + i, 1), :])
    before_dyn = lambda i: parts[pl.ds(below * lines + 1 + i, 1), :]
    before_charge = lambda i: edge_in[:, i * LANES : (i + 1) * LANES]
    return after, before_dyn, before_charge


def later_weight(weight_in, parts):
    steps = lax.axis_size("tm")
    return next_weight(weight_in[...], parts[pl.ds(0, steps, stride=parts.shape[0] // steps), :])


def step_kernel(dims, first_rows, slot_rows, first, received, parts, weight_in, row_in, power, charge, dyn, edge_in,
                pushed_row, inputs, duals_t, limits_t, values, table, weight, power_row, power_out, charge_out,
                dyn_out, edge_out, duals_out, pushed_out, slots, bar, spread, sums):
    weight[...] = later_weight(weight_in, parts)
    state = [lambda cut, ref=ref: ref[:, cut] for ref in (power, charge, dyn)]
    primal, dual = local_step(dims, slot_rows, weight[...], received, inputs, state, later_edges(parts, edge_in),
                              (power_out, charge_out, dyn_out), edge_out)
    power_row[...] = row_power(dims, first_rows, weight[...], first, row_in[...],
                               take_row(received, SLOT_DYN, *dims, slot_rows), pushed_row[...], bar)
    feeder_part(dims, slot_rows, weight[...], primal, dual, bar, dyn_out, duals_t, limits_t, values, table,
                duals_out, pushed_out, slots, spread, sums)


def last_kernel(dims, first_rows, slot_rows, first, received, parts, weight_in, row_in, power, charge, dyn, edge_in,
                pushed_row, inputs, duals_t, limits_t, values, table, power_out, charge_out, dyn_out, duals_out,
                bar, spread):
    weight = later_weight(weight_in, parts)
    state = [lambda cut, ref=ref: ref[:, cut] for ref in (power, charge, dyn)]
    local_step(dims, slot_rows, weight, received, inputs, state, later_edges(parts, edge_in),
               (power_out, charge_out, dyn_out), None)
    row_power(dims, first_rows, weight, first, row_in[...], take_row(received, SLOT_DYN, *dims, slot_rows),
              pushed_row[...], bar)
    coupled = feeder_apply(values, table, bar, spread, *dims)
    new = feeder_step(weight, coupled, duals_t[...], limits_t[...])
    duals_out[...] = jnp.transpose(new)[: duals_out.shape[0]]


def relay_kernel(dims, slot_rows, received, dyn, parts):
    pieces, groups = dims
    steps = lax.axis_size("tm")
    here = lax.axis_index("tm")
    lines = parts.shape[0] // steps
    parts[...] = jnp.zeros_like(parts)
    summed = row_sum(received[pl.ds(2 * pieces, groups, stride=slot_rows), :])
    parts[pl.ds(0, steps, stride=lines), :] = jnp.broadcast_to(summed, (steps, LANES))

    @pl.when(here > 0)
    def _():
        for i in range(pieces):
            parts[pl.ds((here - 1) * lines + 1 + i, 1), :] = dyn[:1, i * LANES : (i + 1) * LANES]

    @pl.when(here < steps - 1)
    def _():
        for i in range(pieces):
            parts[pl.ds((here + 1) * lines + 1 + i, 1), :] = dyn[groups - 1 :, i * LANES : (i + 1) * LANES]


def shapes(*dims):
    return [jax.ShapeDtypeStruct(dim, F32) for dim in dims]


def call(kernel, name, in_specs, out_dims, scratch=(), flops=0, moved=0):
    return pl.pallas_call(
        kernel,
        name=name,
        in_specs=in_specs,
        out_specs=[VMEM] * len(out_dims),
        out_shape=shapes(*out_dims),
        scratch_shapes=[pltpu.VMEM(dim, F32) for dim in scratch],
        compiler_params=pltpu.CompilerParams(vmem_limit_bytes=16 * 1024 * 1024),
        cost_estimate=pl.CostEstimate(flops=flops, bytes_accessed=moved, transcendentals=0),
    )


def stacked(*arrays):
    shape = (len(arrays),) + arrays[0].shape
    index = lax.broadcasted_iota(jnp.int32, shape, 0)
    out = jnp.broadcast_to(arrays[-1], shape)
    for i, array in enumerate(arrays[:-1]):
        out = jnp.where(index == i, array, out)
    return out


def moved_to(value, axis, distance):
    count = lax.axis_size(axis)
    return lax.ppermute(value, axis, [(i, i + distance) for i in range(count) if 0 <= i + distance < count])


def exchange(value, axis):
    return lax.all_to_all(value, axis, 0, 0, tiled=True)


def shards(power0, charge0, dyn_dual0, feeder_dual0, price, inflow, power_limit, capacity, feeder_limit,
           block_values, block_cols, block_offsets):
    groups, local = power0.shape
    pieces = local // LANES
    blocks, blk = block_values.shape[:2]
    feeds = block_offsets.shape[0] - 1
    steps = lax.axis_size("tm")
    first_rows, slot_rows, lines = rows_up(5 * pieces), rows_up(2 * pieces + 1), 1 + pieces
    dims = (pieces, groups)
    row, line, square, own = (pieces * groups, LANES), (1, LANES), (blk, LANES), (groups, local)
    spread, sums = (feeds, blk, LANES), (pieces * groups, 8, LANES)
    matrix_specs = [VMEM, SMEM]
    work, moved = 2 * blocks * blk * LANES, 4 * blocks * blk * LANES

    inputs = stacked(power0, charge0, dyn_dual0, price, inflow, power_limit, capacity)
    duals = stacked(feeder_dual0.reshape(feeds, blk), feeder_limit.reshape(feeds, blk))
    matrix = (block_values, jnp.concatenate([block_cols, block_offsets]))

    after = moved_to(inputs[DYN, :1], "tm", -1)
    before = moved_to(inputs[CHARGE : DYN + 1, -1], "tm", 1)
    first, duals_t, limits_t, pushed = call(
        functools.partial(first_kernel, dims, first_rows), "first",
        [VMEM] * 2 + matrix_specs, [(groups * first_rows, LANES), square, square, row], [spread, sums], work, moved,
    )(duals, inputs, *matrix)
    first, after, before = lax.optimization_barrier((first, after, before))
    first = exchange(first.reshape(groups, first_rows, LANES), "bat").reshape(groups * first_rows, LANES)

    step_outs = [line, row] + [own] * 3 + [(1, local), square, row, (groups * slot_rows, LANES)]
    scratch = [row, spread, sums]
    for iteration in range(ITERS):
        last = iteration + 1 == ITERS
        outs = [own] * 3 + [(feeds, blk)] if last else step_outs
        sizes = (dims, first_rows, slot_rows)
        if iteration == 0:
            results = call(
                functools.partial(step_one_kernel, *sizes), "step_one", [VMEM] * 7 + matrix_specs, outs, scratch,
                2 * work, moved,
            )(first, after, before, pushed, inputs, duals_t, limits_t, *matrix)
        else:
            results = call(
                functools.partial(last_kernel if last else step_kernel, *sizes), "last" if last else "step",
                [VMEM] * 13 + matrix_specs, outs, scratch[:2] if last else scratch, 2 * work, moved,
            )(first, received, parts, weight, power_row, power, charge, dyn, edge, pushed, inputs, duals_t, limits_t,
              *matrix)
        if not last:
            weight, power_row, power, charge, dyn, edge, duals_t, pushed, slots = results
            received = exchange(slots.reshape(groups, slot_rows, LANES), "bat").reshape(groups * slot_rows, LANES)
            parts = call(
                functools.partial(relay_kernel, dims, slot_rows), "relay", [VMEM] * 2, [(steps * lines, LANES)]
            )(received, dyn)[0]
            parts = exchange(parts.reshape(steps, lines, LANES), "tm").reshape(steps * lines, LANES)
    power, charge, dyn_dual, feeder_dual = results
    return power, charge, dyn_dual, feeder_dual.reshape(1, feeds * blk)


def solution(mesh):
    split = P("tm", "bat")
    steps = P(("tm", "bat"), None)
    return jax.shard_map(
        shards,
        mesh=mesh,
        in_specs=(split, split, split, steps, split, split, P("bat"), P("bat"), P(), P(), P(), P()),
        out_specs=(split, split, split, steps),
        check_vma=False,
    )
```

```python
import functools

import jax
import jax.numpy as jnp
from jax import lax
from jax.experimental import pallas as pl
from jax.experimental.pallas import tpu as pltpu
from jax.sharding import PartitionSpec as P

ITERS = 4
ETA_STEP = 0.4
EPS_NORM = 1e-06
LANES = 128
HALF = LANES // 2
ADJOINT_UNROLL = 8
ADJOINT_PARTS = 4
APPLY_UNROLL = 8
CHUNKS = 4
STREAMING_LIMIT = 50 * 1024 * 1024
F32 = jnp.float32

VMEM = pl.BlockSpec(memory_space=pltpu.VMEM)
SMEM = pl.BlockSpec(memory_space=pltpu.SMEM)

POWER, CHARGE, DYN, PRICE, INFLOW, LIMIT, CAPACITY = range(7)
SLOT_DYN, SLOT_PUSHED, SLOT_POWER, SLOT_PRICE, SLOT_LIMIT = range(5)


def rows_up(count):
    return -(-count // 8) * 8


def lane_iota(shape):
    return lax.broadcasted_iota(jnp.int32, shape, len(shape) - 1)


def clip(value, low, high):
    return jnp.minimum(jnp.maximum(value, low), high)


def total(value):
    return jnp.sum(jnp.sum(value, axis=0, keepdims=True), axis=1, keepdims=True)


def take_row(ref, array, pieces, groups, slot_rows):
    parts = [ref[pl.ds(array * pieces + i, groups, stride=slot_rows), :] for i in range(pieces)]
    return jnp.concatenate(parts, axis=0)


def put_row(ref, array, value, pieces, groups, slot_rows):
    for i in range(pieces):
        ref[pl.ds(array * pieces + i, groups, stride=slot_rows), :] = value[i * groups : (i + 1) * groups]


def unrolled(count, most):
    return max(u for u in range(1, most + 1) if count % u == 0)


def adjoint_loop(values, table, spread, sums, begin, end):
    blocks, blk = values.shape[:2]
    ways = unrolled(end - begin, ADJOINT_UNROLL)

    def step(k, carry):
        for u in range(ways):
            j = begin + k * ways + u
            product = values[j] * spread[table[j]]
            c = table[blocks + j]
            part = sums[u % len(sums)]
            part[c] = part[c] + jnp.sum(product.reshape(blk // 8, 8, LANES), axis=0)
        return carry

    lax.fori_loop(0, (end - begin) // ways, step, 0)


def adjoint_start(sums):
    for part in sums:
        part[...] = jnp.zeros_like(part)


def adjoint_total(sums):
    return jnp.sum(sum(part[...] for part in sums), axis=1)


def feeder_adjoint(values, table, spread, sums):
    adjoint_start(sums)
    adjoint_loop(values, table, spread, sums, 0, values.shape[0])
    return adjoint_total(sums)


def feeder_duals(values, table, field, weight, duals_t, limits_t, spread):
    blocks, blk = values.shape[:2]
    feeds = spread.shape[0]
    ways = unrolled(blocks, APPLY_UNROLL)

    def step(k, acc):
        for u in range(ways):
            j = k * ways + u
            f = table[j]
            before = table[jnp.maximum(j - 1, 0)]
            keep = jnp.where(f == before, 1.0, 0.0).astype(F32)
            acc = acc * keep + values[j] * field[pl.ds(table[blocks + j], 1), :]
            spread[f] = acc
        return acc

    lax.fori_loop(0, blocks // ways, step, jnp.zeros((blk, LANES), F32))
    step_dual = ETA_STEP * weight[:, :1]
    shifted = duals_t - step_dual * limits_t
    lane = lane_iota((blk, LANES))
    new = jnp.zeros((blk, LANES), F32)
    for f in range(feeds):
        moved = spread[f] + jnp.where(lane == f, shifted, 0.0)
        dual = jnp.maximum(0.0, jnp.sum(moved, axis=1, keepdims=True))
        spread[f] = jnp.broadcast_to(dual, (blk, LANES))
        new = jnp.where(lane == f, dual, new)
    return new


def pack_sums(primal, dual):
    lane = lane_iota(primal.shape)
    return jnp.where(
        lane < HALF, primal + pltpu.roll(primal, HALF, 1), dual + pltpu.roll(dual, HALF, 1)
    )


def next_weight(weight, parts):
    both = jnp.sum(parts, axis=0, keepdims=True)
    lane = lane_iota(both.shape)
    primal_sq = total(jnp.where(lane < HALF, both, 0.0))
    dual_sq = total(jnp.where(lane < HALF, 0.0, both))
    ratio = jnp.sqrt((dual_sq + EPS_NORM) / (primal_sq + EPS_NORM))
    return jnp.broadcast_to(jnp.sqrt(weight[:, :1] * ratio), (1, LANES))


def row_sum(value):
    return jnp.sum(value, axis=0, keepdims=True)


def first_kernel(dims, first_rows, chunks, duals, inputs, values_in, table, slots, duals_t, limits_t, pushed_out,
                 values, spread, *rest):
    pieces, groups = dims
    sums, sems = rest[:-1], rest[-1]
    blocks, blk = values.shape[:2]
    feeds = duals.shape[1]
    size = blocks // chunks
    copies = [
        pltpu.make_async_copy(values_in.at[pl.ds(k * size, size)], values.at[pl.ds(k * size, size)], sems.at[k])
        for k in range(chunks)
    ]
    for copy in copies:
        copy.start()
    for i, target in enumerate((duals_t, limits_t)):
        padded = jnp.concatenate([duals[i], jnp.zeros((blk - feeds, LANES), F32)], axis=0)
        target[...] = jnp.transpose(padded)
    for f in range(feeds):
        spread[f] = jnp.broadcast_to(duals_t[:, f : f + 1], (blk, LANES))
    sent = ((SLOT_DYN, DYN), (SLOT_POWER, POWER), (SLOT_PRICE, PRICE), (SLOT_LIMIT, LIMIT))
    for i in range(pieces):
        for slot, array in sent:
            slots[pl.ds(slot * pieces + i, groups, stride=first_rows), :] = inputs[array, :, i * LANES : (i + 1) * LANES]
    adjoint_start(sums)
    for k, copy in enumerate(copies):
        copy.wait()
        adjoint_loop(values, table, spread, sums, k * size, (k + 1) * size)
    pushed = adjoint_total(sums)
    pushed_out[...] = pushed
    put_row(slots, SLOT_PUSHED, pushed, pieces, groups, first_rows)


def local_step(dims, slot_rows, weight, received, inputs, state, edges, state_out, edge_out):
    pieces, groups = dims
    step_primal = ETA_STEP / weight[:, :1]
    step_dual = ETA_STEP * weight[:, :1]
    after, before_dyn, before_charge = edges
    begin = lax.axis_index("tm") == 0
    line = lax.broadcasted_iota(jnp.int32, (groups, LANES), 0)
    primal = jnp.zeros((1, LANES), F32)
    dual = jnp.zeros((1, LANES), F32)
    for i in range(pieces):
        cut = slice(i * LANES, (i + 1) * LANES)
        power, charge, dyn = (read(cut) for read in state)
        price, inflow, limit, capacity = (inputs[array, :, cut] for array in (PRICE, INFLOW, LIMIT, CAPACITY))
        pushed = received[pl.ds(SLOT_PUSHED * pieces + i, groups, stride=slot_rows), :]
        power_new = clip(power - step_primal * (price - dyn + pushed), -limit, limit)
        dyn_next = jnp.where(line == groups - 1, after(i), pltpu.roll(dyn, groups - 1, 0))
        charge_new = clip(charge - step_primal * (dyn - dyn_next), 0.0, capacity)
        power_bar = 2.0 * power_new - power
        charge_bar = 2.0 * charge_new - charge
        edge_charge = before_charge(i)
        edge_new = clip(edge_charge - step_primal * (before_dyn(i) - dyn[:1]), 0.0, capacity[:1])
        edge_bar = jnp.where(begin, 0.0, 2.0 * edge_new - edge_charge)
        prev_bar = jnp.where(line == 0, edge_bar, pltpu.roll(charge_bar, 1, 0))
        dyn_new = dyn + step_dual * (charge_bar - prev_bar - power_bar - inflow)
        for ref, value in zip(state_out, (power_new, charge_new, dyn_new)):
            ref[:, cut] = value
        if edge_out is not None:
            edge_out[:, cut] = edge_new
        primal = primal + row_sum((power_new - power) ** 2 + (charge_new - charge) ** 2)
        dual = dual + row_sum((dyn_new - dyn) ** 2)
    return primal, dual


def row_power(dims, first_rows, weight, first, power, dyn, pushed, bar):
    pieces, groups = dims
    step_primal = ETA_STEP / weight[:, :1]
    price = take_row(first, SLOT_PRICE, pieces, groups, first_rows)
    limit = take_row(first, SLOT_LIMIT, pieces, groups, first_rows)
    new = clip(power - step_primal * (price - dyn + pushed), -limit, limit)
    bar[...] = (ETA_STEP * weight[:, :1]) * (2.0 * new - power)
    return new


def feeder_part(dims, slot_rows, weight, primal, dual, bar, dyn, duals_t, limits_t, values, table,
                duals_out, pushed_out, slots, spread, sums):
    pieces, groups = dims
    new = feeder_duals(values, table, bar, weight, duals_t[...], limits_t[...], spread)
    duals_out[...] = new
    parts = pack_sums(primal, dual + row_sum((new - duals_t[...]) ** 2))
    slots[pl.ds(2 * pieces, groups, stride=slot_rows), :] = jnp.broadcast_to(parts, (groups, LANES))
    for i in range(pieces):
        slots[pl.ds(SLOT_DYN * pieces + i, groups, stride=slot_rows), :] = dyn[:, i * LANES : (i + 1) * LANES]
    pushed = feeder_adjoint(values, table, spread, sums)
    pushed_out[...] = pushed
    put_row(slots, SLOT_PUSHED, pushed, pieces, groups, slot_rows)


def step_one_kernel(dims, first_rows, slot_rows, first, after, before, pushed_row, inputs, duals_t, limits_t, values,
                    table, weight, power_row, power_out, charge_out, dyn_out, edge_out, duals_out, pushed_out, slots,
                    bar, spread, *sums):
    pieces, groups = dims
    weight[...] = jnp.ones_like(weight)
    state = [lambda cut, array=array: inputs[array, :, cut] for array in (POWER, CHARGE, DYN)]
    edges = [lambda i, ref=ref, k=k: ref[k : k + 1, i * LANES : (i + 1) * LANES]
             for ref, k in ((after, 0), (before, 1), (before, 0))]
    primal, dual = local_step(dims, first_rows, weight[...], first, inputs, state, edges,
                              (power_out, charge_out, dyn_out), edge_out)
    power_row[...] = row_power(dims, first_rows, weight[...], first,
                               take_row(first, SLOT_POWER, pieces, groups, first_rows),
                               take_row(first, SLOT_DYN, pieces, groups, first_rows), pushed_row[...], bar)
    feeder_part(dims, slot_rows, weight[...], primal, dual, bar, dyn_out, duals_t, limits_t, values, table,
                duals_out, pushed_out, slots, spread, sums)


def later_edges(parts, edge_in):
    steps = lax.axis_size("tm")
    here = lax.axis_index("tm")
    lines = parts.shape[0] // steps
    above, below = jnp.minimum(here + 1, steps - 1), jnp.maximum(here - 1, 0)
    after = lambda i: jnp.where(here == steps - 1, 0.0, parts[pl.ds(above * lines + 1 + i, 1), :])
    before_dyn = lambda i: parts[pl.ds(below * lines + 1 + i, 1), :]
    before_charge = lambda i: edge_in[:, i * LANES : (i + 1) * LANES]
    return after, before_dyn, before_charge


def later_weight(weight_in, parts):
    steps = lax.axis_size("tm")
    return next_weight(weight_in[...], parts[pl.ds(0, steps, stride=parts.shape[0] // steps), :])


def step_kernel(dims, first_rows, slot_rows, first, received, parts, weight_in, row_in, power, charge, dyn, edge_in,
                pushed_row, inputs, duals_t, limits_t, values, table, weight, power_row, power_out, charge_out,
                dyn_out, edge_out, duals_out, pushed_out, slots, bar, spread, *sums):
    weight[...] = later_weight(weight_in, parts)
    state = [lambda cut, ref=ref: ref[:, cut] for ref in (power, charge, dyn)]
    primal, dual = local_step(dims, slot_rows, weight[...], received, inputs, state, later_edges(parts, edge_in),
                              (power_out, charge_out, dyn_out), edge_out)
    power_row[...] = row_power(dims, first_rows, weight[...], first, row_in[...],
                               take_row(received, SLOT_DYN, *dims, slot_rows), pushed_row[...], bar)
    feeder_part(dims, slot_rows, weight[...], primal, dual, bar, dyn_out, duals_t, limits_t, values, table,
                duals_out, pushed_out, slots, spread, sums)


def last_kernel(dims, first_rows, slot_rows, first, received, parts, weight_in, row_in, power, charge, dyn, edge_in,
                pushed_row, inputs, duals_t, limits_t, values, table, power_out, charge_out, dyn_out, duals_out,
                bar, spread):
    weight = later_weight(weight_in, parts)
    state = [lambda cut, ref=ref: ref[:, cut] for ref in (power, charge, dyn)]
    local_step(dims, slot_rows, weight, received, inputs, state, later_edges(parts, edge_in),
               (power_out, charge_out, dyn_out), None)
    row_power(dims, first_rows, weight, first, row_in[...], take_row(received, SLOT_DYN, *dims, slot_rows),
              pushed_row[...], bar)
    new = feeder_duals(values, table, bar, weight, duals_t[...], limits_t[...], spread)
    duals_out[...] = jnp.transpose(new)[: duals_out.shape[0]]


def relay_kernel(dims, slot_rows, received, dyn, parts):
    pieces, groups = dims
    steps = lax.axis_size("tm")
    here = lax.axis_index("tm")
    lines = parts.shape[0] // steps
    parts[...] = jnp.zeros_like(parts)
    summed = row_sum(received[pl.ds(2 * pieces, groups, stride=slot_rows), :])
    parts[pl.ds(0, steps, stride=lines), :] = jnp.broadcast_to(summed, (steps, LANES))

    @pl.when(here > 0)
    def _():
        for i in range(pieces):
            parts[pl.ds((here - 1) * lines + 1 + i, 1), :] = dyn[:1, i * LANES : (i + 1) * LANES]

    @pl.when(here < steps - 1)
    def _():
        for i in range(pieces):
            parts[pl.ds((here + 1) * lines + 1 + i, 1), :] = dyn[groups - 1 :, i * LANES : (i + 1) * LANES]


def shapes(*dims):
    return [jax.ShapeDtypeStruct(dim, F32) for dim in dims]


def call(kernel, name, in_specs, out_dims, scratch=(), flops=0, moved=0, limit=16 * 1024 * 1024, copies=0):
    semaphores = [pltpu.SemaphoreType.DMA((copies,))] if copies else []
    return pl.pallas_call(
        kernel,
        name=name,
        in_specs=in_specs,
        out_specs=[VMEM] * len(out_dims),
        out_shape=shapes(*out_dims),
        scratch_shapes=[pltpu.VMEM(dim, F32) for dim in scratch] + semaphores,
        compiler_params=pltpu.CompilerParams(vmem_limit_bytes=limit),
        cost_estimate=pl.CostEstimate(flops=flops, bytes_accessed=moved, transcendentals=0),
    )


def stacked(*arrays):
    shape = (len(arrays),) + arrays[0].shape
    index = lax.broadcasted_iota(jnp.int32, shape, 0)
    out = jnp.broadcast_to(arrays[-1], shape)
    for i, array in enumerate(arrays[:-1]):
        out = jnp.where(index == i, array, out)
    return out


def moved_to(value, axis, distance):
    count = lax.axis_size(axis)
    return lax.ppermute(value, axis, [(i, i + distance) for i in range(count) if 0 <= i + distance < count])


def exchange(value, axis):
    return lax.all_to_all(value, axis, 0, 0, tiled=True)


def shards(power0, charge0, dyn_dual0, feeder_dual0, price, inflow, power_limit, capacity, feeder_limit,
           block_values, block_cols, block_offsets):
    groups, local = power0.shape
    pieces = local // LANES
    blocks, blk = block_values.shape[:2]
    feeds = block_offsets.shape[0] - 1
    steps = lax.axis_size("tm")
    first_rows, slot_rows, lines = rows_up(5 * pieces), rows_up(2 * pieces + 1), 1 + pieces
    dims = (pieces, groups)
    row, line, square, own = (pieces * groups, LANES), (1, LANES), (blk, LANES), (groups, local)
    spread, sums = (feeds, blk, LANES), (pieces * groups, 8, LANES)
    matrix_specs = [VMEM, SMEM]
    chunks = unrolled(blocks, CHUNKS)
    work, moved = 2 * blocks * blk * LANES, 4 * blocks * blk * LANES

    inputs = stacked(power0, charge0, dyn_dual0, price, inflow, power_limit, capacity)
    duals = stacked(feeder_dual0.reshape(feeds, blk), feeder_limit.reshape(feeds, blk))
    index_all = lax.broadcasted_iota(jnp.int32, (blocks, feeds - 1), 0)
    row_of = jnp.sum((index_all >= block_offsets[None, 1:-1]).astype(jnp.int32), axis=1)
    matrix = (block_values, jnp.concatenate([row_of, (block_cols % pieces) * groups + block_cols // pieces]))

    after = moved_to(inputs[DYN, :1], "tm", -1)
    before = moved_to(inputs[CHARGE : DYN + 1, -1], "tm", 1)
    first, duals_t, limits_t, pushed = call(
        functools.partial(first_kernel, dims, first_rows, chunks), "first",
        [VMEM, VMEM, pl.BlockSpec(memory_space=pl.ANY), SMEM], [(groups * first_rows, LANES), square, square, row],
        [block_values.shape, spread] + [sums] * ADJOINT_PARTS, work, moved, STREAMING_LIMIT, chunks,
    )(duals, inputs, *matrix)
    first, after, before = lax.optimization_barrier((first, after, before))
    first = exchange(first.reshape(groups, first_rows, LANES), "bat").reshape(groups * first_rows, LANES)

    step_outs = [line, row] + [own] * 3 + [(1, local), square, row, (groups * slot_rows, LANES)]
    scratch = [row, spread] + [sums] * ADJOINT_PARTS
    for iteration in range(ITERS):
        last = iteration + 1 == ITERS
        outs = [own] * 3 + [(feeds, blk)] if last else step_outs
        sizes = (dims, first_rows, slot_rows)
        if iteration == 0:
            results = call(
                functools.partial(step_one_kernel, *sizes), "step_one", [VMEM] * 7 + matrix_specs, outs, scratch,
                2 * work, moved,
            )(first, after, before, pushed, inputs, duals_t, limits_t, *matrix)
        else:
            results = call(
                functools.partial(last_kernel if last else step_kernel, *sizes), "last" if last else "step",
                [VMEM] * 13 + matrix_specs, outs, scratch[:2] if last else scratch, 2 * work, moved,
            )(first, received, parts, weight, power_row, power, charge, dyn, edge, pushed, inputs, duals_t, limits_t,
              *matrix)
        if not last:
            weight, power_row, power, charge, dyn, edge, duals_t, pushed, slots = results
            received = exchange(slots.reshape(groups, slot_rows, LANES), "bat").reshape(groups * slot_rows, LANES)
            parts = call(
                functools.partial(relay_kernel, dims, slot_rows), "relay", [VMEM] * 2, [(steps * lines, LANES)]
            )(received, dyn)[0]
            parts = exchange(parts.reshape(steps, lines, LANES), "tm").reshape(steps * lines, LANES)
    power, charge, dyn_dual, feeder_dual = results
    return power, charge, dyn_dual, feeder_dual.reshape(1, feeds * blk)


def solution(mesh):
    split = P("tm", "bat")
    steps = P(("tm", "bat"), None)
    return jax.shard_map(
        shards,
        mesh=mesh,
        in_specs=(split, split, split, steps, split, split, P("bat"), P("bat"), P(), P(), P(), P()),
        out_specs=(split, split, split, steps),
        check_vma=False,
    )
```

```python
import functools

import jax
import jax.numpy as jnp
from jax import lax
from jax.experimental import pallas as pl
from jax.experimental.pallas import tpu as pltpu
from jax.sharding import PartitionSpec as P

ITERS = 4
ETA_STEP = 0.4
EPS_NORM = 1e-06
LANES = 128
HALF = LANES // 2
ADJOINT_UNROLL = 8
ADJOINT_PARTS = 4
APPLY_UNROLL = 8
CHUNKS = 4
STREAMING_LIMIT = 50 * 1024 * 1024
F32 = jnp.float32

VMEM = pl.BlockSpec(memory_space=pltpu.VMEM)

POWER, CHARGE, DYN, PRICE, INFLOW, LIMIT, CAPACITY = range(7)
SLOT_DYN, SLOT_PUSHED, SLOT_POWER, SLOT_PRICE, SLOT_LIMIT = range(5)


def places():
    return lax.axis_index("z"), lax.axis_index("core"), lax.axis_index("bat")


def rows_up(count):
    return -(-count // 8) * 8


def lane_iota(shape):
    return lax.broadcasted_iota(jnp.int32, shape, len(shape) - 1)


def clip(value, low, high):
    return jnp.minimum(jnp.maximum(value, low), high)


def total(value):
    return jnp.sum(jnp.sum(value, axis=0, keepdims=True), axis=1, keepdims=True)


def take_row(ref, array, pieces, groups, slot_rows):
    parts = [ref[pl.ds(array * pieces + i, groups, stride=slot_rows), :] for i in range(pieces)]
    return jnp.concatenate(parts, axis=0)


def put_row(ref, array, value, pieces, groups, slot_rows):
    for i in range(pieces):
        ref[pl.ds(array * pieces + i, groups, stride=slot_rows), :] = value[i * groups : (i + 1) * groups]


def unrolled(count, most):
    return max(u for u in range(1, most + 1) if count % u == 0)


def adjoint_loop(values, table, spread, sums, begin, end):
    blocks, blk = values.shape[:2]
    ways = unrolled(end - begin, ADJOINT_UNROLL)

    def step(k, carry):
        for u in range(ways):
            j = begin + k * ways + u
            product = values[j] * spread[table[j]]
            c = table[blocks + j]
            part = sums[u % len(sums)]
            part[c] = part[c] + jnp.sum(product.reshape(blk // 8, 8, LANES), axis=0)
        return carry

    lax.fori_loop(0, (end - begin) // ways, step, 0)


def adjoint_start(sums):
    for part in sums:
        part[...] = jnp.zeros_like(part)


def adjoint_total(sums):
    return jnp.sum(sum(part[...] for part in sums), axis=1)


def feeder_adjoint(values, table, spread, sums):
    adjoint_start(sums)
    adjoint_loop(values, table, spread, sums, 0, values.shape[0])
    return adjoint_total(sums)


def feeder_duals(values, table, field, weight, duals_t, limits_t, spread):
    blocks, blk = values.shape[:2]
    feeds = spread.shape[0]
    ways = unrolled(blocks, APPLY_UNROLL)

    def step(k, acc):
        for u in range(ways):
            j = k * ways + u
            f = table[j]
            before = table[jnp.maximum(j - 1, 0)]
            keep = jnp.where(f == before, 1.0, 0.0).astype(F32)
            acc = acc * keep + values[j] * field[pl.ds(table[blocks + j], 1), :]
            spread[f] = acc
        return acc

    lax.fori_loop(0, blocks // ways, step, jnp.zeros((blk, LANES), F32))
    step_dual = ETA_STEP * weight[:, :1]
    shifted = duals_t - step_dual * limits_t
    lane = lane_iota((blk, LANES))
    new = jnp.zeros((blk, LANES), F32)
    for f in range(feeds):
        moved = spread[f] + jnp.where(lane == f, shifted, 0.0)
        dual = jnp.maximum(0.0, jnp.sum(moved, axis=1, keepdims=True))
        spread[f] = jnp.broadcast_to(dual, (blk, LANES))
        new = jnp.where(lane == f, dual, new)
    return new


def pack_sums(primal, dual):
    lane = lane_iota(primal.shape)
    return jnp.where(
        lane < HALF, primal + pltpu.roll(primal, HALF, 1), dual + pltpu.roll(dual, HALF, 1)
    )


def next_weight(weight, parts):
    both = jnp.sum(parts, axis=0, keepdims=True)
    lane = lane_iota(both.shape)
    primal_sq = total(jnp.where(lane < HALF, both, 0.0))
    dual_sq = total(jnp.where(lane < HALF, 0.0, both))
    ratio = jnp.sqrt((dual_sq + EPS_NORM) / (primal_sq + EPS_NORM))
    return jnp.broadcast_to(jnp.sqrt(weight[:, :1] * ratio), (1, LANES))


def row_sum(value):
    return jnp.sum(value, axis=0, keepdims=True)


def table_load(table_in, table, sem):
    copy = pltpu.make_async_copy(table_in, table, sem)
    copy.start()
    return copy


def first_kernel(dims, first_rows, chunks, duals, inputs, values_in, table_in, slots, duals_t, limits_t, pushed_out,
                 values, spread, *rest):
    pieces, groups = dims
    *sums, sems, table, sem = rest
    load = table_load(table_in, table, sem)
    blocks, blk = values.shape[:2]
    feeds = duals.shape[1]
    size = blocks // chunks
    copies = [
        pltpu.make_async_copy(values_in.at[pl.ds(k * size, size)], values.at[pl.ds(k * size, size)], sems.at[k])
        for k in range(chunks)
    ]
    for copy in copies:
        copy.start()
    for i, target in enumerate((duals_t, limits_t)):
        padded = jnp.concatenate([duals[i], jnp.zeros((blk - feeds, LANES), F32)], axis=0)
        target[...] = jnp.transpose(padded)
    for f in range(feeds):
        spread[f] = jnp.broadcast_to(duals_t[:, f : f + 1], (blk, LANES))
    sent = ((SLOT_DYN, DYN), (SLOT_POWER, POWER), (SLOT_PRICE, PRICE), (SLOT_LIMIT, LIMIT))
    for i in range(pieces):
        for slot, array in sent:
            slots[pl.ds(slot * pieces + i, groups, stride=first_rows), :] = inputs[array, :, i * LANES : (i + 1) * LANES]
    adjoint_start(sums)
    load.wait()
    for k, copy in enumerate(copies):
        copy.wait()
        adjoint_loop(values, table, spread, sums, k * size, (k + 1) * size)
    pushed = adjoint_total(sums)
    pushed_out[...] = pushed
    put_row(slots, SLOT_PUSHED, pushed, pieces, groups, first_rows)


def local_step(dims, slot_rows, weight, received, inputs, state, edges, state_out, edge_out):
    pieces, groups = dims
    step_primal = ETA_STEP / weight[:, :1]
    step_dual = ETA_STEP * weight[:, :1]
    after, before_dyn, before_charge = edges
    z, core, _ = places()
    begin = (z == 0) & (core == 0)
    line = lax.broadcasted_iota(jnp.int32, (groups, LANES), 0)
    primal = jnp.zeros((1, LANES), F32)
    dual = jnp.zeros((1, LANES), F32)
    for i in range(pieces):
        cut = slice(i * LANES, (i + 1) * LANES)
        power, charge, dyn = (read(cut) for read in state)
        price, inflow, limit, capacity = (inputs[array, :, cut] for array in (PRICE, INFLOW, LIMIT, CAPACITY))
        pushed = received[pl.ds(SLOT_PUSHED * pieces + i, groups, stride=slot_rows), :]
        power_new = clip(power - step_primal * (price - dyn + pushed), -limit, limit)
        dyn_next = jnp.where(line == groups - 1, after(i), pltpu.roll(dyn, groups - 1, 0))
        charge_new = clip(charge - step_primal * (dyn - dyn_next), 0.0, capacity)
        power_bar = 2.0 * power_new - power
        charge_bar = 2.0 * charge_new - charge
        edge_charge = before_charge(i)
        edge_new = clip(edge_charge - step_primal * (before_dyn(i) - dyn[:1]), 0.0, capacity[:1])
        edge_bar = jnp.where(begin, 0.0, 2.0 * edge_new - edge_charge)
        prev_bar = jnp.where(line == 0, edge_bar, pltpu.roll(charge_bar, 1, 0))
        dyn_new = dyn + step_dual * (charge_bar - prev_bar - power_bar - inflow)
        for ref, value in zip(state_out, (power_new, charge_new, dyn_new)):
            ref[:, cut] = value
        if edge_out is not None:
            edge_out[:, cut] = edge_new
        primal = primal + row_sum((power_new - power) ** 2 + (charge_new - charge) ** 2)
        dual = dual + row_sum((dyn_new - dyn) ** 2)
    return primal, dual


def row_power(dims, first_rows, weight, first, power, dyn, pushed, bar):
    pieces, groups = dims
    step_primal = ETA_STEP / weight[:, :1]
    price = take_row(first, SLOT_PRICE, pieces, groups, first_rows)
    limit = take_row(first, SLOT_LIMIT, pieces, groups, first_rows)
    new = clip(power - step_primal * (price - dyn + pushed), -limit, limit)
    bar[...] = (ETA_STEP * weight[:, :1]) * (2.0 * new - power)
    return new


def feeder_part(dims, slot_rows, weight, primal, dual, bar, dyn, duals_t, limits_t, values, table,
                duals_out, pushed_out, slots, spread, sums):
    pieces, groups = dims
    _, core, bat = places()
    new = feeder_duals(values, table, bar, weight, duals_t[...], limits_t[...], spread)
    duals_out[...] = new
    parts = pack_sums(primal, dual + row_sum((new - duals_t[...]) ** 2))
    slots[...] = jnp.zeros_like(slots)
    own, other = slots.at[core], slots.at[1 - core]
    for side in (own, other):
        side[pl.ds(2 * pieces, groups, stride=slot_rows), :] = jnp.broadcast_to(parts, (groups, LANES))
    for i in range(pieces):
        cut = slice(i * LANES, (i + 1) * LANES)
        own[pl.ds(SLOT_DYN * pieces + i, groups, stride=slot_rows), :] = dyn[:, cut]
        other[pl.ds(bat * slot_rows + i, 1), :] = dyn[:1, cut]
        other[pl.ds(bat * slot_rows + pieces + i, 1), :] = dyn[groups - 1 :, cut]
    pushed = feeder_adjoint(values, table, spread, sums)
    pushed_out[...] = pushed
    put_row(own, SLOT_PUSHED, pushed, pieces, groups, slot_rows)


def step_one_kernel(dims, first_rows, slot_rows, first, after, before, pushed_row, inputs, duals_t, limits_t, values,
                    table_in, weight, power_row, power_out, charge_out, dyn_out, edge_out, duals_out, pushed_out, slots,
                    bar, spread, *rest):
    *sums, table, sem = rest
    pieces, groups = dims
    load = table_load(table_in, table, sem)
    weight[...] = jnp.ones_like(weight)
    state = [lambda cut, array=array: inputs[array, :, cut] for array in (POWER, CHARGE, DYN)]
    edges = [lambda i, ref=ref, k=k: ref[k : k + 1, i * LANES : (i + 1) * LANES]
             for ref, k in ((after, 0), (before, 1), (before, 0))]
    primal, dual = local_step(dims, first_rows, weight[...], first, inputs, state, edges,
                              (power_out, charge_out, dyn_out), edge_out)
    power_row[...] = row_power(dims, first_rows, weight[...], first,
                               take_row(first, SLOT_POWER, pieces, groups, first_rows),
                               take_row(first, SLOT_DYN, pieces, groups, first_rows), pushed_row[...], bar)
    load.wait()
    feeder_part(dims, slot_rows, weight[...], primal, dual, bar, dyn_out, duals_t, limits_t, values, table,
                duals_out, pushed_out, slots, spread, sums)


def later_edges(dims, slot_rows, received, parts, edge_in):
    pieces, _ = dims
    z, core, bat = places()
    chips = lax.axis_size("z")
    lines = parts.shape[0] // chips
    above, below = jnp.minimum(z + 1, chips - 1), jnp.maximum(z - 1, 0)
    end = jnp.where(z == chips - 1, 0.0, 1.0).astype(F32)
    after = lambda i: jnp.where(
        core == 0, received[1, pl.ds(bat * slot_rows + i, 1), :], end * parts[pl.ds(above * lines + 1 + i, 1), :]
    )
    before_dyn = lambda i: jnp.where(
        core == 0, parts[pl.ds(below * lines + 1 + i, 1), :], received[0, pl.ds(bat * slot_rows + pieces + i, 1), :]
    )
    before_charge = lambda i: edge_in[:, i * LANES : (i + 1) * LANES]
    return after, before_dyn, before_charge


def later_weight(weight_in, parts):
    chips = lax.axis_size("z")
    return next_weight(weight_in[...], parts[pl.ds(0, chips, stride=parts.shape[0] // chips), :])


def step_kernel(dims, first_rows, slot_rows, first, received, parts, weight_in, row_in, power, charge, dyn, edge_in,
                pushed_row, inputs, duals_t, limits_t, values, table_in, weight, power_row, power_out, charge_out,
                dyn_out, edge_out, duals_out, pushed_out, slots, bar, spread, *rest):
    *sums, table, sem = rest
    load = table_load(table_in, table, sem)
    weight[...] = later_weight(weight_in, parts)
    own = received.at[lax.axis_index("core")]
    state = [lambda cut, ref=ref: ref[:, cut] for ref in (power, charge, dyn)]
    primal, dual = local_step(dims, slot_rows, weight[...], own, inputs, state,
                              later_edges(dims, slot_rows, received, parts, edge_in),
                              (power_out, charge_out, dyn_out), edge_out)
    power_row[...] = row_power(dims, first_rows, weight[...], first, row_in[...],
                               take_row(own, SLOT_DYN, *dims, slot_rows), pushed_row[...], bar)
    load.wait()
    feeder_part(dims, slot_rows, weight[...], primal, dual, bar, dyn_out, duals_t, limits_t, values, table,
                duals_out, pushed_out, slots, spread, sums)


def last_kernel(dims, first_rows, slot_rows, first, received, parts, weight_in, row_in, power, charge, dyn, edge_in,
                pushed_row, inputs, duals_t, limits_t, values, table_in, power_out, charge_out, dyn_out, duals_out,
                bar, spread, table, sem):
    load = table_load(table_in, table, sem)
    weight = later_weight(weight_in, parts)
    own = received.at[lax.axis_index("core")]
    state = [lambda cut, ref=ref: ref[:, cut] for ref in (power, charge, dyn)]
    local_step(dims, slot_rows, weight, own, inputs, state, later_edges(dims, slot_rows, received, parts, edge_in),
               (power_out, charge_out, dyn_out), None)
    row_power(dims, first_rows, weight, first, row_in[...], take_row(own, SLOT_DYN, *dims, slot_rows),
              pushed_row[...], bar)
    load.wait()
    new = feeder_duals(values, table, bar, weight, duals_t[...], limits_t[...], spread)
    duals_out[...] = jnp.transpose(new)[: duals_out.shape[0]]


def relay_kernel(dims, slot_rows, received, parts):
    pieces, groups = dims
    z, core, bat = places()
    chips = lax.axis_size("z")
    lines = parts.shape[0] // chips
    parts[...] = jnp.zeros_like(parts)
    summed = sum(row_sum(received[k, pl.ds(2 * pieces, groups, stride=slot_rows), :]) for k in range(2))
    parts[pl.ds(0, chips, stride=lines), :] = jnp.broadcast_to(summed, (chips, LANES))

    @pl.when((core == 1) & (z > 0))
    def _():
        for i in range(pieces):
            parts[pl.ds((z - 1) * lines + 1 + i, 1), :] = received[0, pl.ds(bat * slot_rows + i, 1), :]

    @pl.when((core == 0) & (z < chips - 1))
    def _():
        for i in range(pieces):
            parts[pl.ds((z + 1) * lines + 1 + i, 1), :] = received[1, pl.ds(bat * slot_rows + pieces + i, 1), :]


def shapes(*dims):
    return [jax.ShapeDtypeStruct(dim, F32) for dim in dims]


def call(kernel, name, in_specs, out_dims, scratch=(), flops=0, moved=0, limit=16 * 1024 * 1024, copies=0, table=0):
    more = [pltpu.SemaphoreType.DMA((copies,))] if copies else []
    if table:
        more += [pltpu.SMEM((table,), jnp.int32), pltpu.SemaphoreType.DMA]
    return pl.pallas_call(
        kernel,
        name=name,
        in_specs=in_specs,
        out_specs=[VMEM] * len(out_dims),
        out_shape=shapes(*out_dims),
        scratch_shapes=[pltpu.VMEM(dim, F32) for dim in scratch] + more,
        compiler_params=pltpu.CompilerParams(vmem_limit_bytes=limit),
        cost_estimate=pl.CostEstimate(flops=flops, bytes_accessed=moved, transcendentals=0),
    )


def stacked(*arrays):
    shape = (len(arrays),) + arrays[0].shape
    index = lax.broadcasted_iota(jnp.int32, shape, 0)
    out = jnp.broadcast_to(arrays[-1], shape)
    for i, array in enumerate(arrays[:-1]):
        out = jnp.where(index == i, array, out)
    return out


def moved_to(value, axis, distance):
    count = lax.axis_size(axis)
    return lax.ppermute(value, axis, [(i, i + distance) for i in range(count) if 0 <= i + distance < count])


def exchange(value, axis):
    return lax.all_to_all(value, axis, 0, 0, tiled=True)


def shards(power0, charge0, dyn_dual0, feeder_dual0, price, inflow, power_limit, capacity, feeder_limit,
           block_values, block_cols, block_offsets):
    groups, local = power0.shape
    pieces = local // LANES
    blocks, blk = block_values.shape[:2]
    feeds = block_offsets.shape[0] - 1
    chips = lax.axis_size("z")
    first_rows, slot_rows, lines = rows_up(5 * pieces), rows_up(2 * pieces + 1), 1 + pieces
    dims = (pieces, groups)
    row, line, square, own = (pieces * groups, LANES), (1, LANES), (blk, LANES), (groups, local)
    spread, sums = (feeds, blk, LANES), (pieces * groups, 8, LANES)
    matrix_specs = [VMEM, VMEM]
    chunks = unrolled(blocks, CHUNKS)
    work, moved = 2 * blocks * blk * LANES, 4 * blocks * blk * LANES

    inputs = stacked(power0, charge0, dyn_dual0, price, inflow, power_limit, capacity)
    duals = stacked(feeder_dual0.reshape(feeds, blk), feeder_limit.reshape(feeds, blk))
    tables = lax.optimization_barrier(jnp.concatenate([block_cols, block_offsets]))
    block_cols, block_offsets = tables[:blocks], tables[blocks:]
    index_all = lax.broadcasted_iota(jnp.int32, (blocks, feeds - 1), 0)
    row_of = jnp.sum((index_all >= block_offsets[None, 1:-1]).astype(jnp.int32), axis=1)
    matrix = (block_values, jnp.concatenate([row_of, (block_cols % pieces) * groups + block_cols // pieces]))

    after = moved_to(inputs[DYN, :1], ("z", "core"), -1)
    before = moved_to(inputs[CHARGE : DYN + 1, -1], ("z", "core"), 1)
    first, duals_t, limits_t, pushed = call(
        functools.partial(first_kernel, dims, first_rows, chunks), "first",
        [VMEM, VMEM, pl.BlockSpec(memory_space=pl.ANY), VMEM], [(groups * first_rows, LANES), square, square, row],
        [block_values.shape, spread] + [sums] * ADJOINT_PARTS, work, moved, STREAMING_LIMIT, chunks, 2 * blocks,
    )(duals, inputs, *matrix)
    first, after, before = lax.optimization_barrier((first, after, before))
    first = exchange(first.reshape(groups, first_rows, LANES), "bat").reshape(groups * first_rows, LANES)

    both = (2, groups * slot_rows, LANES)
    step_outs = [line, row] + [own] * 3 + [(1, local), square, row, both]
    scratch = [row, spread] + [sums] * ADJOINT_PARTS
    for iteration in range(ITERS):
        last = iteration + 1 == ITERS
        outs = [own] * 3 + [(feeds, blk)] if last else step_outs
        sizes = (dims, first_rows, slot_rows)
        if iteration == 0:
            results = call(
                functools.partial(step_one_kernel, *sizes), "step_one", [VMEM] * 7 + matrix_specs, outs, scratch,
                2 * work, moved, table=2 * blocks,
            )(first, after, before, pushed, inputs, duals_t, limits_t, *matrix)
        else:
            results = call(
                functools.partial(last_kernel if last else step_kernel, *sizes), "last" if last else "step",
                [VMEM] * 13 + matrix_specs, outs, scratch[:2] if last else scratch, 2 * work, moved,
                table=2 * blocks,
            )(first, received, parts, weight, power_row, power, charge, dyn, edge, pushed, inputs, duals_t, limits_t,
              *matrix)
        if not last:
            weight, power_row, power, charge, dyn, edge, duals_t, pushed, slots = results
            received = exchange(slots.reshape(2 * groups, slot_rows, LANES), ("core", "bat")).reshape(both)
            parts = call(
                functools.partial(relay_kernel, dims, slot_rows), "relay", [VMEM], [(chips * lines, LANES)]
            )(received)[0]
            parts = exchange(parts.reshape(chips, lines, LANES), "z").reshape(chips * lines, LANES)
    power, charge, dyn_dual, feeder_dual = results
    return power, charge, dyn_dual, feeder_dual.reshape(1, feeds * blk)


def solution(mesh):
    fine = jax.sharding.Mesh(
        mesh.devices.reshape(mesh.shape["tm"] // 2, 2, mesh.shape["bat"]), ("z", "core", "bat")
    )
    split = P(("z", "core"), "bat")
    steps = P(("z", "core", "bat"), None)
    return jax.shard_map(
        shards,
        mesh=fine,
        in_specs=(split, split, split, steps, split, split, P("bat"), P("bat"), P(), P(), P(), P()),
        out_specs=(split, split, split, steps),
        check_vma=False,
    )
```

```python
import functools

import jax
import jax.numpy as jnp
from jax import lax
from jax.experimental import pallas as pl
from jax.experimental.pallas import tpu as pltpu
from jax.sharding import PartitionSpec as P

ITERS = 4
ETA_STEP = 0.4
EPS_NORM = 1e-06
LANES = 128
HALF = LANES // 2
ADJOINT_UNROLL = 8
ADJOINT_PARTS = 4
APPLY_UNROLL = 8
EARLY_COPY_FLOPS = 2 * 10**10
F32 = jnp.float32


VMEM = pl.BlockSpec(memory_space=pltpu.VMEM)

POWER, CHARGE, DYN, PRICE, INFLOW, LIMIT, CAPACITY = range(7)
SLOT_DYN, SLOT_PUSHED, SLOT_POWER, SLOT_PRICE, SLOT_LIMIT = range(5)


def places():
    return lax.axis_index("z"), lax.axis_index("core"), lax.axis_index("bat")


def rows_up(count):
    return -(-count // 8) * 8


def lane_iota(shape):
    return lax.broadcasted_iota(jnp.int32, shape, len(shape) - 1)


def clip(value, low, high):
    return jnp.minimum(jnp.maximum(value, low), high)


def total(value):
    return jnp.sum(jnp.sum(value, axis=0, keepdims=True), axis=1, keepdims=True)


def take_row(ref, array, pieces, groups, slot_rows):
    parts = [ref[pl.ds(array * pieces + i, groups, stride=slot_rows), :] for i in range(pieces)]
    return jnp.concatenate(parts, axis=0)


def put_row(ref, array, value, pieces, groups, slot_rows):
    for i in range(pieces):
        ref[pl.ds(array * pieces + i, groups, stride=slot_rows), :] = value[i * groups : (i + 1) * groups]


def unrolled(count, most):
    return max(u for u in range(1, most + 1) if count % u == 0)


def adjoint_loop(values, table, spread, sums, begin, end):
    blocks, blk = values.shape[:2]
    ways = unrolled(end - begin, ADJOINT_UNROLL)

    def step(k, carry):
        for u in range(ways):
            j = begin + k * ways + u
            product = values[j] * spread[table[j]]
            c = table[blocks + j]
            part = sums[u % len(sums)]
            part[c] = part[c] + jnp.sum(product.reshape(blk // 8, 8, LANES), axis=0)
        return carry

    lax.fori_loop(0, (end - begin) // ways, step, 0)


def adjoint_start(sums):
    for part in sums:
        part[...] = jnp.zeros_like(part)


def adjoint_total(sums):
    return jnp.sum(sum(part[...] for part in sums), axis=1)


def feeder_adjoint(values, table, spread, sums):
    adjoint_loop(values, table, spread, sums, 0, values.shape[0])
    return adjoint_total(sums)


def feeder_duals(values, table, field, weight, duals_t, limits_t, spread):
    blocks, blk = values.shape[:2]
    feeds = spread.shape[0]
    ways = unrolled(blocks, APPLY_UNROLL)

    def step(k, acc):
        for u in range(ways):
            j = k * ways + u
            f = table[j]
            before = table[jnp.maximum(j - 1, 0)]
            keep = jnp.where(f == before, 1.0, 0.0).astype(F32)
            acc = acc * keep + values[j] * field[pl.ds(table[blocks + j], 1), :]
            spread[f] = acc
        return acc

    lax.fori_loop(0, blocks // ways, step, jnp.zeros((blk, LANES), F32))
    step_dual = ETA_STEP * weight[:, :1]
    shifted = duals_t - step_dual * limits_t
    lane = lane_iota((blk, LANES))
    new = jnp.zeros((blk, LANES), F32)
    for f in range(feeds):
        moved = spread[f] + jnp.where(lane == f, shifted, 0.0)
        dual = jnp.maximum(0.0, jnp.sum(moved, axis=1, keepdims=True))
        spread[f] = jnp.broadcast_to(dual, (blk, LANES))
        new = jnp.where(lane == f, dual, new)
    return new


def pack_sums(primal, dual):
    lane = lane_iota(primal.shape)
    return jnp.where(
        lane < HALF, primal + pltpu.roll(primal, HALF, 1), dual + pltpu.roll(dual, HALF, 1)
    )


def next_weight(weight, parts):
    both = jnp.sum(parts, axis=0, keepdims=True)
    lane = lane_iota(both.shape)
    primal_sq = total(jnp.where(lane < HALF, both, 0.0))
    dual_sq = total(jnp.where(lane < HALF, 0.0, both))
    ratio = jnp.sqrt((dual_sq + EPS_NORM) / (primal_sq + EPS_NORM))
    return jnp.broadcast_to(jnp.sqrt(weight[:, :1] * ratio), (1, LANES))


def row_sum(value):
    return jnp.sum(value, axis=0, keepdims=True)


def table_load(table_in, table, sem):
    copy = pltpu.make_async_copy(table_in, table, sem)
    copy.start()
    return copy


def edges_kernel(inputs, top, bottom):
    last = inputs.shape[1] - 1
    top[...] = inputs[DYN, :1, :]
    bottom[:1, :] = inputs[CHARGE, last:, :]
    bottom[1:, :] = inputs[DYN, last:, :]


def first_kernel(dims, first_rows, duals, inputs, values, table_in, slots, duals_t, limits_t, pushed_out,
                 spread, *rest):
    pieces, groups = dims
    *sums, table, sem = rest
    load = table_load(table_in, table, sem)
    blocks, blk = values.shape[:2]
    feeds = duals.shape[1]
    for i, target in enumerate((duals_t, limits_t)):
        padded = jnp.concatenate([duals[i], jnp.zeros((blk - feeds, LANES), F32)], axis=0)
        target[...] = jnp.transpose(padded)
    for f in range(feeds):
        spread[f] = jnp.broadcast_to(duals_t[:, f : f + 1], (blk, LANES))
    sent = ((SLOT_DYN, DYN), (SLOT_POWER, POWER), (SLOT_PRICE, PRICE), (SLOT_LIMIT, LIMIT))
    for i in range(pieces):
        for slot, array in sent:
            slots[pl.ds(slot * pieces + i, groups, stride=first_rows), :] = inputs[array, :, i * LANES : (i + 1) * LANES]
    adjoint_start(sums)
    load.wait()
    adjoint_loop(values, table, spread, sums, 0, blocks)
    pushed = adjoint_total(sums)
    pushed_out[...] = pushed
    put_row(slots, SLOT_PUSHED, pushed, pieces, groups, first_rows)


def local_step(dims, slot_rows, weight, received, inputs, state, edges, state_out, edge_out):
    pieces, groups = dims
    step_primal = ETA_STEP / weight[:, :1]
    step_dual = ETA_STEP * weight[:, :1]
    after, before_dyn, before_charge = edges
    z, core, _ = places()
    begin = (z == 0) & (core == 0)
    line = lax.broadcasted_iota(jnp.int32, (groups, LANES), 0)
    primal = jnp.zeros((1, LANES), F32)
    dual = jnp.zeros((1, LANES), F32)
    for i in range(pieces):
        cut = slice(i * LANES, (i + 1) * LANES)
        power, charge, dyn = (read(cut) for read in state)
        price, inflow, limit, capacity = (inputs[array, :, cut] for array in (PRICE, INFLOW, LIMIT, CAPACITY))
        pushed = received[pl.ds(SLOT_PUSHED * pieces + i, groups, stride=slot_rows), :]
        power_new = clip(power - step_primal * (price - dyn + pushed), -limit, limit)
        dyn_next = jnp.where(line == groups - 1, after(i), pltpu.roll(dyn, groups - 1, 0))
        charge_new = clip(charge - step_primal * (dyn - dyn_next), 0.0, capacity)
        power_bar = 2.0 * power_new - power
        charge_bar = 2.0 * charge_new - charge
        edge_charge = before_charge(i)
        edge_new = clip(edge_charge - step_primal * (before_dyn(i) - dyn[:1]), 0.0, capacity[:1])
        edge_bar = jnp.where(begin, 0.0, 2.0 * edge_new - edge_charge)
        prev_bar = jnp.where(line == 0, edge_bar, pltpu.roll(charge_bar, 1, 0))
        dyn_new = dyn + step_dual * (charge_bar - prev_bar - power_bar - inflow)
        for ref, value in zip(state_out, (power_new, charge_new, dyn_new)):
            ref[:, cut] = value
        if edge_out is not None:
            edge_out[:, cut] = edge_new
        primal = primal + row_sum((power_new - power) ** 2 + (charge_new - charge) ** 2)
        dual = dual + row_sum((dyn_new - dyn) ** 2)
    return primal, dual


def row_power(dims, first_rows, weight, first, power, dyn, pushed, bar):
    pieces, groups = dims
    step_primal = ETA_STEP / weight[:, :1]
    price = take_row(first, SLOT_PRICE, pieces, groups, first_rows)
    limit = take_row(first, SLOT_LIMIT, pieces, groups, first_rows)
    new = clip(power - step_primal * (price - dyn + pushed), -limit, limit)
    bar[...] = (ETA_STEP * weight[:, :1]) * (2.0 * new - power)
    return new


def feeder_part(dims, slot_rows, load, weight, primal, dual, bar, dyn, duals_t, limits_t, values, table,
                duals_out, pushed_out, slots, spread, sums):
    pieces, groups = dims
    _, core, bat = places()
    load.wait()
    new = feeder_duals(values, table, bar, weight, duals_t[...], limits_t[...], spread)
    duals_out[...] = new
    parts = pack_sums(primal, dual + row_sum((new - duals_t[...]) ** 2))
    adjoint_start(sums)
    slots[...] = jnp.zeros_like(slots)
    own, other = slots.at[core], slots.at[1 - core]
    for side in (own, other):
        side[pl.ds(2 * pieces, groups, stride=slot_rows), :] = jnp.broadcast_to(parts, (groups, LANES))
    for i in range(pieces):
        cut = slice(i * LANES, (i + 1) * LANES)
        own[pl.ds(SLOT_DYN * pieces + i, groups, stride=slot_rows), :] = dyn[:, cut]
        other[pl.ds(bat * slot_rows + i, 1), :] = dyn[:1, cut]
        other[pl.ds(bat * slot_rows + pieces + i, 1), :] = dyn[groups - 1 :, cut]
    pushed = feeder_adjoint(values, table, spread, sums)
    pushed_out[...] = pushed
    put_row(own, SLOT_PUSHED, pushed, pieces, groups, slot_rows)


def step_one_kernel(dims, first_rows, slot_rows, first, after, before, pushed_row, inputs, duals_t, limits_t, values,
                    table_in, weight, power_row, power_out, charge_out, dyn_out, edge_out, duals_out, pushed_out, slots,
                    bar, spread, *rest):
    *sums, table, sem = rest
    pieces, groups = dims
    load = table_load(table_in, table, sem)
    weight[...] = jnp.ones_like(weight)
    state = [lambda cut, array=array: inputs[array, :, cut] for array in (POWER, CHARGE, DYN)]
    edges = [lambda i, ref=ref, k=k: ref[k : k + 1, i * LANES : (i + 1) * LANES]
             for ref, k in ((after, 0), (before, 1), (before, 0))]
    primal, dual = local_step(dims, first_rows, weight[...], first, inputs, state, edges,
                              (power_out, charge_out, dyn_out), edge_out)
    power_row[...] = row_power(dims, first_rows, weight[...], first,
                               take_row(first, SLOT_POWER, pieces, groups, first_rows),
                               take_row(first, SLOT_DYN, pieces, groups, first_rows), pushed_row[...], bar)
    feeder_part(dims, slot_rows, load, weight[...], primal, dual, bar, dyn_out, duals_t, limits_t, values, table,
                duals_out, pushed_out, slots, spread, sums)


def later_edges(dims, slot_rows, received, parts, edge_in):
    pieces, _ = dims
    z, core, bat = places()
    chips = lax.axis_size("z")
    lines = parts.shape[0] // chips
    above, below = jnp.minimum(z + 1, chips - 1), jnp.maximum(z - 1, 0)
    end = jnp.where(z == chips - 1, 0.0, 1.0).astype(F32)
    after = lambda i: jnp.where(
        core == 0, received[1, pl.ds(bat * slot_rows + i, 1), :], end * parts[pl.ds(above * lines + 1 + i, 1), :]
    )
    before_dyn = lambda i: jnp.where(
        core == 0, parts[pl.ds(below * lines + 1 + i, 1), :], received[0, pl.ds(bat * slot_rows + pieces + i, 1), :]
    )
    before_charge = lambda i: edge_in[:, i * LANES : (i + 1) * LANES]
    return after, before_dyn, before_charge


def later_weight(weight_in, parts):
    chips = lax.axis_size("z")
    return next_weight(weight_in[...], parts[pl.ds(0, chips, stride=parts.shape[0] // chips), :])


def step_kernel(dims, first_rows, slot_rows, first, received, parts, weight_in, row_in, power, charge, dyn, edge_in,
                pushed_row, inputs, duals_t, limits_t, values, table_in, weight, power_row, power_out, charge_out,
                dyn_out, edge_out, duals_out, pushed_out, slots, bar, spread, *rest):
    *sums, table, sem = rest
    load = table_load(table_in, table, sem)
    weight[...] = later_weight(weight_in, parts)
    own = received.at[lax.axis_index("core")]
    state = [lambda cut, ref=ref: ref[:, cut] for ref in (power, charge, dyn)]
    primal, dual = local_step(dims, slot_rows, weight[...], own, inputs, state,
                              later_edges(dims, slot_rows, received, parts, edge_in),
                              (power_out, charge_out, dyn_out), edge_out)
    power_row[...] = row_power(dims, first_rows, weight[...], first, row_in[...],
                               take_row(own, SLOT_DYN, *dims, slot_rows), pushed_row[...], bar)
    feeder_part(dims, slot_rows, load, weight[...], primal, dual, bar, dyn_out, duals_t, limits_t, values, table,
                duals_out, pushed_out, slots, spread, sums)


def last_kernel(dims, first_rows, slot_rows, first, received, parts, weight_in, row_in, power, charge, dyn, edge_in,
                pushed_row, inputs, duals_t, limits_t, values, table_in, power_out, charge_out, dyn_out, duals_out,
                bar, spread, table, sem):
    load = table_load(table_in, table, sem)
    weight = later_weight(weight_in, parts)
    own = received.at[lax.axis_index("core")]
    state = [lambda cut, ref=ref: ref[:, cut] for ref in (power, charge, dyn)]
    local_step(dims, slot_rows, weight, own, inputs, state, later_edges(dims, slot_rows, received, parts, edge_in),
               (power_out, charge_out, dyn_out), None)
    row_power(dims, first_rows, weight, first, row_in[...], take_row(own, SLOT_DYN, *dims, slot_rows),
              pushed_row[...], bar)
    load.wait()
    new = feeder_duals(values, table, bar, weight, duals_t[...], limits_t[...], spread)
    duals_out[...] = jnp.transpose(new)[: duals_out.shape[0]]


def relay_kernel(dims, slot_rows, received, parts):
    pieces, groups = dims
    z, core, bat = places()
    chips = lax.axis_size("z")
    lines = parts.shape[0] // chips
    parts[...] = jnp.zeros_like(parts)
    summed = sum(row_sum(received[k, pl.ds(2 * pieces, groups, stride=slot_rows), :]) for k in range(2))
    parts[pl.ds(0, chips, stride=lines), :] = jnp.broadcast_to(summed, (chips, LANES))

    @pl.when((core == 1) & (z > 0))
    def _():
        for i in range(pieces):
            parts[pl.ds((z - 1) * lines + 1 + i, 1), :] = received[0, pl.ds(bat * slot_rows + i, 1), :]

    @pl.when((core == 0) & (z < chips - 1))
    def _():
        for i in range(pieces):
            parts[pl.ds((z + 1) * lines + 1 + i, 1), :] = received[1, pl.ds(bat * slot_rows + pieces + i, 1), :]


def shapes(*dims):
    return [jax.ShapeDtypeStruct(dim, F32) for dim in dims]


def call(kernel, name, in_specs, out_dims, scratch=(), flops=0, moved=0, limit=16 * 1024 * 1024, copies=0, table=0):
    more = [pltpu.SemaphoreType.DMA((copies,))] if copies else []
    if table:
        more += [pltpu.SMEM((table,), jnp.int32), pltpu.SemaphoreType.DMA]
    return pl.pallas_call(
        kernel,
        name=name,
        in_specs=in_specs,
        out_specs=[VMEM] * len(out_dims),
        out_shape=shapes(*out_dims),
        scratch_shapes=[pltpu.VMEM(dim, F32) for dim in scratch] + more,
        compiler_params=pltpu.CompilerParams(vmem_limit_bytes=limit),
        cost_estimate=pl.CostEstimate(flops=flops, bytes_accessed=moved, transcendentals=0),
    )


def stacked(*arrays):
    shape = (len(arrays),) + arrays[0].shape
    index = lax.broadcasted_iota(jnp.int32, shape, 0)
    out = jnp.broadcast_to(arrays[-1], shape)
    for i, array in enumerate(arrays[:-1]):
        out = jnp.where(index == i, array, out)
    return out


def moved_to(value, axis, distance):
    count = lax.axis_size(axis)
    return lax.ppermute(value, axis, [(i, i + distance) for i in range(count) if 0 <= i + distance < count])


def exchange(value, axis):
    return lax.all_to_all(value, axis, 0, 0, tiled=True)


def shards(power0, charge0, dyn_dual0, feeder_dual0, price, inflow, power_limit, capacity, feeder_limit,
           block_values, block_cols, block_offsets):
    groups, local = power0.shape
    pieces = local // LANES
    blocks, blk = block_values.shape[:2]
    feeds = block_offsets.shape[0] - 1
    chips = lax.axis_size("z")
    first_rows, slot_rows, lines = rows_up(5 * pieces), rows_up(2 * pieces + 1), 1 + pieces
    dims = (pieces, groups)
    row, line, square, own = (pieces * groups, LANES), (1, LANES), (blk, LANES), (groups, local)
    spread, sums = (feeds, blk, LANES), (pieces * groups, 8, LANES)
    matrix_specs = [VMEM, VMEM]
    work, moved = 2 * blocks * blk * LANES, 4 * blocks * blk * LANES

    inputs = stacked(power0, charge0, dyn_dual0, price, inflow, power_limit, capacity)
    duals = stacked(feeder_dual0.reshape(feeds, blk), feeder_limit.reshape(feeds, blk))
    tables = lax.optimization_barrier(jnp.concatenate([block_cols, block_offsets]))
    block_cols, block_offsets = tables[:blocks], tables[blocks:]
    index_all = lax.broadcasted_iota(jnp.int32, (blocks, feeds - 1), 0)
    row_of = jnp.sum((index_all >= block_offsets[None, 1:-1]).astype(jnp.int32), axis=1)
    matrix = (block_values, jnp.concatenate([row_of, (block_cols % pieces) * groups + block_cols // pieces]))

    top, bottom = call(edges_kernel, "edges", [VMEM], [(1, local), (2, local)], flops=EARLY_COPY_FLOPS)(inputs)
    after = moved_to(top, ("z", "core"), -1)
    before = moved_to(bottom, ("z", "core"), 1)
    first, duals_t, limits_t, pushed = call(
        functools.partial(first_kernel, dims, first_rows), "first",
        [VMEM] * 4, [(groups * first_rows, LANES), square, square, row],
        [spread] + [sums] * ADJOINT_PARTS, work, moved, table=2 * blocks,
    )(duals, inputs, *matrix)
    first, after, before = lax.optimization_barrier((first, after, before))
    first = exchange(first.reshape(groups, first_rows, LANES), "bat").reshape(groups * first_rows, LANES)

    both = (2, groups * slot_rows, LANES)
    step_outs = [line, row] + [own] * 3 + [(1, local), square, row, both]
    scratch = [row, spread] + [sums] * ADJOINT_PARTS
    for iteration in range(ITERS):
        last = iteration + 1 == ITERS
        outs = [own] * 3 + [(feeds, blk)] if last else step_outs
        sizes = (dims, first_rows, slot_rows)
        if iteration == 0:
            results = call(
                functools.partial(step_one_kernel, *sizes), "step_one", [VMEM] * 7 + matrix_specs, outs, scratch,
                2 * work, moved, table=2 * blocks,
            )(first, after, before, pushed, inputs, duals_t, limits_t, *matrix)
        else:
            results = call(
                functools.partial(last_kernel if last else step_kernel, *sizes), "last" if last else "step",
                [VMEM] * 13 + matrix_specs, outs, scratch[:2] if last else scratch, 2 * work, moved,
                table=2 * blocks,
            )(first, received, parts, weight, power_row, power, charge, dyn, edge, pushed, inputs, duals_t, limits_t,
              *matrix)
        if not last:
            weight, power_row, power, charge, dyn, edge, duals_t, pushed, slots = results
            received = exchange(slots.reshape(2 * groups, slot_rows, LANES), ("core", "bat")).reshape(both)
            parts = call(
                functools.partial(relay_kernel, dims, slot_rows), "relay", [VMEM], [(chips * lines, LANES)]
            )(received)[0]
            parts = exchange(parts.reshape(chips, lines, LANES), "z").reshape(chips * lines, LANES)
    power, charge, dyn_dual, feeder_dual = results
    return power, charge, dyn_dual, feeder_dual.reshape(1, feeds * blk)


def solution(mesh):
    fine = jax.sharding.Mesh(
        mesh.devices.reshape(mesh.shape["tm"] // 2, 2, mesh.shape["bat"]), ("z", "core", "bat")
    )
    split = P(("z", "core"), "bat")
    steps = P(("z", "core", "bat"), None)
    return jax.shard_map(
        shards,
        mesh=fine,
        in_specs=(split, split, split, steps, split, split, P("bat"), P("bat"), P(), P(), P(), P()),
        out_specs=(split, split, split, steps),
        check_vma=False,
    )
```

```python
import functools

import jax
import jax.numpy as jnp
from jax import lax
from jax.experimental import pallas as pl
from jax.experimental.pallas import tpu as pltpu
from jax.sharding import PartitionSpec as P

ITERS = 4
ETA_STEP = 0.4
EPS_NORM = 1e-06
LANES = 128
HALF = LANES // 2
ADJOINT_UNROLL = 24
ADJOINT_PARTS = 4
APPLY_UNROLL = 8
EARLY_COPY_FLOPS = 2 * 10**10
F32 = jnp.float32


VMEM = pl.BlockSpec(memory_space=pltpu.VMEM)

POWER, CHARGE, DYN, PRICE, INFLOW, LIMIT, CAPACITY = range(7)
SLOT_DYN, SLOT_PUSHED, SLOT_POWER, SLOT_PRICE, SLOT_LIMIT = range(5)


def places():
    return lax.axis_index("z"), lax.axis_index("core"), lax.axis_index("bat")


def rows_up(count):
    return -(-count // 8) * 8


def lane_iota(shape):
    return lax.broadcasted_iota(jnp.int32, shape, len(shape) - 1)


def clip(value, low, high):
    return jnp.minimum(jnp.maximum(value, low), high)


def total(value):
    return jnp.sum(jnp.sum(value, axis=0, keepdims=True), axis=1, keepdims=True)


def take_row(ref, array, pieces, groups, slot_rows):
    parts = [ref[pl.ds(array * pieces + i, groups, stride=slot_rows), :] for i in range(pieces)]
    return jnp.concatenate(parts, axis=0)


def put_row(ref, array, value, pieces, groups, slot_rows):
    for i in range(pieces):
        ref[pl.ds(array * pieces + i, groups, stride=slot_rows), :] = value[i * groups : (i + 1) * groups]


def unrolled(count, most):
    return max(u for u in range(1, most + 1) if count % u == 0)


def adjoint_loop(values, table, spread, sums, begin, end):
    blocks, blk = values.shape[:2]
    ways = unrolled(end - begin, ADJOINT_UNROLL)

    def step(k, carry):
        for u in range(ways):
            j = begin + k * ways + u
            product = values[j] * spread[table[j]]
            c = table[blocks + j]
            part = sums[u % len(sums)]
            part[c] = part[c] + jnp.sum(product.reshape(blk // 8, 8, LANES), axis=0)
        return carry

    lax.fori_loop(0, (end - begin) // ways, step, 0)


def adjoint_start(sums):
    for part in sums:
        part[...] = jnp.zeros_like(part)


def adjoint_total(sums):
    return jnp.sum(sum(part[...] for part in sums), axis=1)


def feeder_adjoint(values, table, spread, sums):
    adjoint_loop(values, table, spread, sums, 0, values.shape[0])
    return adjoint_total(sums)


def feeder_duals(values, table, load, field, weight, duals_t, limits_t, spread):
    blocks, blk = values.shape[:2]
    feeds = spread.shape[0]
    ways = unrolled(blocks, APPLY_UNROLL)
    step_dual = ETA_STEP * weight[:, :1]
    shifted = duals_t - step_dual * limits_t
    lane = lane_iota((blk, LANES))
    for f in range(feeds):
        spread[f] = jnp.where(lane == f, shifted, 0.0)
    load.wait()

    def step(k, carry):
        for u in range(ways):
            j = k * ways + u
            f = table[j]
            spread[f] = spread[f] + values[j] * field[pl.ds(table[blocks + j], 1), :]
        return carry

    lax.fori_loop(0, blocks // ways, step, 0)
    new = jnp.zeros((blk, LANES), F32)
    for f in range(feeds):
        dual = jnp.maximum(0.0, jnp.sum(spread[f], axis=1, keepdims=True))
        spread[f] = jnp.broadcast_to(dual, (blk, LANES))
        new = jnp.where(lane == f, dual, new)
    return new


def pack_sums(primal, dual):
    lane = lane_iota(primal.shape)
    return jnp.where(
        lane < HALF, primal + pltpu.roll(primal, HALF, 1), dual + pltpu.roll(dual, HALF, 1)
    )


def next_weight(weight, parts):
    both = jnp.sum(parts, axis=0, keepdims=True)
    lane = lane_iota(both.shape)
    primal_sq = total(jnp.where(lane < HALF, both, 0.0))
    dual_sq = total(jnp.where(lane < HALF, 0.0, both))
    ratio = jnp.sqrt((dual_sq + EPS_NORM) / (primal_sq + EPS_NORM))
    return jnp.broadcast_to(jnp.sqrt(weight[:, :1] * ratio), (1, LANES))


def row_sum(value):
    return jnp.sum(value, axis=0, keepdims=True)


def table_load(table_in, table, sem):
    copy = pltpu.make_async_copy(table_in, table, sem)
    copy.start()
    return copy


def edges_kernel(inputs, edges):
    last = inputs.shape[1] - 1
    edges[:1, :] = jnp.where(lax.axis_index("core") == 0, inputs[DYN, :1, :], inputs[DYN, last:, :])
    edges[1:, :] = inputs[CHARGE, last:, :]


def first_kernel(dims, first_rows, duals, inputs, values, table_in, slots, duals_t, limits_t, pushed_out,
                 spread, *rest):
    pieces, groups = dims
    *sums, table, sem = rest
    load = table_load(table_in, table, sem)
    blocks, blk = values.shape[:2]
    feeds = duals.shape[1]
    for i, target in enumerate((duals_t, limits_t)):
        padded = jnp.concatenate([duals[i], jnp.zeros((blk - feeds, LANES), F32)], axis=0)
        target[...] = jnp.transpose(padded)
    for f in range(feeds):
        spread[f] = jnp.broadcast_to(duals_t[:, f : f + 1], (blk, LANES))
    sent = ((SLOT_DYN, DYN), (SLOT_POWER, POWER), (SLOT_PRICE, PRICE), (SLOT_LIMIT, LIMIT))
    _, core, bat = places()
    slots[...] = jnp.zeros_like(slots)
    own, other = slots.at[core], slots.at[1 - core]
    for i in range(pieces):
        cut = slice(i * LANES, (i + 1) * LANES)
        for slot, array in sent:
            own[pl.ds(slot * pieces + i, groups, stride=first_rows), :] = inputs[array, :, cut]
        for k, (array, line) in enumerate(((DYN, 0), (DYN, groups - 1), (CHARGE, groups - 1))):
            other[pl.ds(bat * first_rows + k * pieces + i, 1), :] = inputs[array, line : line + 1, cut]
    adjoint_start(sums)
    load.wait()
    adjoint_loop(values, table, spread, sums, 0, blocks)
    pushed = adjoint_total(sums)
    pushed_out[...] = pushed
    put_row(own, SLOT_PUSHED, pushed, pieces, groups, first_rows)


def local_step(dims, slot_rows, weight, received, inputs, state, edges, state_out, edge_out):
    pieces, groups = dims
    step_primal = ETA_STEP / weight[:, :1]
    step_dual = ETA_STEP * weight[:, :1]
    after, before_dyn, before_charge = edges
    z, core, _ = places()
    begin = (z == 0) & (core == 0)
    line = lax.broadcasted_iota(jnp.int32, (groups, LANES), 0)
    primal = jnp.zeros((1, LANES), F32)
    dual = jnp.zeros((1, LANES), F32)
    for i in range(pieces):
        cut = slice(i * LANES, (i + 1) * LANES)
        power, charge, dyn = (read(cut) for read in state)
        price, inflow, limit, capacity = (inputs[array, :, cut] for array in (PRICE, INFLOW, LIMIT, CAPACITY))
        pushed = received[pl.ds(SLOT_PUSHED * pieces + i, groups, stride=slot_rows), :]
        power_new = clip(power - step_primal * (price - dyn + pushed), -limit, limit)
        dyn_next = jnp.where(line == groups - 1, after(i), pltpu.roll(dyn, groups - 1, 0))
        charge_new = clip(charge - step_primal * (dyn - dyn_next), 0.0, capacity)
        power_bar = 2.0 * power_new - power
        charge_bar = 2.0 * charge_new - charge
        edge_charge = before_charge(i)
        edge_new = clip(edge_charge - step_primal * (before_dyn(i) - dyn[:1]), 0.0, capacity[:1])
        edge_bar = jnp.where(begin, 0.0, 2.0 * edge_new - edge_charge)
        prev_bar = jnp.where(line == 0, edge_bar, pltpu.roll(charge_bar, 1, 0))
        dyn_new = dyn + step_dual * (charge_bar - prev_bar - power_bar - inflow)
        for ref, value in zip(state_out, (power_new, charge_new, dyn_new)):
            ref[:, cut] = value
        if edge_out is not None:
            edge_out[:, cut] = edge_new
        primal = primal + row_sum((power_new - power) ** 2 + (charge_new - charge) ** 2)
        dual = dual + row_sum((dyn_new - dyn) ** 2)
    return primal, dual


def row_power(dims, first_rows, weight, first, power, dyn, pushed, bar):
    pieces, groups = dims
    step_primal = ETA_STEP / weight[:, :1]
    price = take_row(first, SLOT_PRICE, pieces, groups, first_rows)
    limit = take_row(first, SLOT_LIMIT, pieces, groups, first_rows)
    new = clip(power - step_primal * (price - dyn + pushed), -limit, limit)
    bar[...] = (ETA_STEP * weight[:, :1]) * (2.0 * new - power)
    return new


def feeder_part(dims, slot_rows, load, weight, primal, dual, bar, dyn, duals_t, limits_t, values, table,
                duals_out, pushed_out, slots, spread, sums):
    pieces, groups = dims
    _, core, bat = places()
    new = feeder_duals(values, table, load, bar, weight, duals_t[...], limits_t[...], spread)
    duals_out[...] = new
    parts = pack_sums(primal, dual + row_sum((new - duals_t[...]) ** 2))
    adjoint_start(sums)
    slots[...] = jnp.zeros_like(slots)
    own, other = slots.at[core], slots.at[1 - core]
    for side in (own, other):
        side[pl.ds(2 * pieces, groups, stride=slot_rows), :] = jnp.broadcast_to(parts, (groups, LANES))
    for i in range(pieces):
        cut = slice(i * LANES, (i + 1) * LANES)
        own[pl.ds(SLOT_DYN * pieces + i, groups, stride=slot_rows), :] = dyn[:, cut]
        other[pl.ds(bat * slot_rows + i, 1), :] = dyn[:1, cut]
        other[pl.ds(bat * slot_rows + pieces + i, 1), :] = dyn[groups - 1 :, cut]
    pushed = feeder_adjoint(values, table, spread, sums)
    pushed_out[...] = pushed
    put_row(own, SLOT_PUSHED, pushed, pieces, groups, slot_rows)


def step_one_kernel(dims, first_rows, slot_rows, first, across, pushed_row, inputs, duals_t, limits_t, values,
                    table_in, weight, power_row, power_out, charge_out, dyn_out, edge_out, duals_out, pushed_out, slots,
                    bar, spread, *rest):
    *sums, table, sem = rest
    pieces, groups = dims
    load = table_load(table_in, table, sem)
    weight[...] = jnp.ones_like(weight)
    state = [lambda cut, array=array: inputs[array, :, cut] for array in (POWER, CHARGE, DYN)]
    _, core, bat = places()
    own, other = first.at[core], first.at[1 - core]
    linked = lambda k, i: across[k : k + 1, i * LANES : (i + 1) * LANES]
    partner = lambda k, i: other[pl.ds(bat * first_rows + k * pieces + i, 1), :]
    edges = (
        lambda i: jnp.where(core == 0, partner(0, i), linked(0, i)),
        lambda i: jnp.where(core == 0, linked(0, i), partner(1, i)),
        lambda i: jnp.where(core == 0, linked(1, i), partner(2, i)),
    )
    primal, dual = local_step(dims, first_rows, weight[...], own, inputs, state, edges,
                              (power_out, charge_out, dyn_out), edge_out)
    power_row[...] = row_power(dims, first_rows, weight[...], own,
                               take_row(own, SLOT_POWER, pieces, groups, first_rows),
                               take_row(own, SLOT_DYN, pieces, groups, first_rows), pushed_row[...], bar)
    feeder_part(dims, slot_rows, load, weight[...], primal, dual, bar, dyn_out, duals_t, limits_t, values, table,
                duals_out, pushed_out, slots, spread, sums)


def later_edges(dims, slot_rows, received, parts, edge_in):
    pieces, _ = dims
    z, core, bat = places()
    chips = lax.axis_size("z")
    lines = parts.shape[0] // chips
    above, below = jnp.minimum(z + 1, chips - 1), jnp.maximum(z - 1, 0)
    end = jnp.where(z == chips - 1, 0.0, 1.0).astype(F32)
    after = lambda i: jnp.where(
        core == 0, received[1, pl.ds(bat * slot_rows + i, 1), :], end * parts[pl.ds(above * lines + 1 + i, 1), :]
    )
    before_dyn = lambda i: jnp.where(
        core == 0, parts[pl.ds(below * lines + 1 + i, 1), :], received[0, pl.ds(bat * slot_rows + pieces + i, 1), :]
    )
    before_charge = lambda i: edge_in[:, i * LANES : (i + 1) * LANES]
    return after, before_dyn, before_charge


def later_weight(weight_in, parts):
    chips = lax.axis_size("z")
    return next_weight(weight_in[...], parts[pl.ds(0, chips, stride=parts.shape[0] // chips), :])


def step_kernel(dims, first_rows, slot_rows, first, received, parts, weight_in, row_in, power, charge, dyn, edge_in,
                pushed_row, inputs, duals_t, limits_t, values, table_in, weight, power_row, power_out, charge_out,
                dyn_out, edge_out, duals_out, pushed_out, slots, bar, spread, *rest):
    *sums, table, sem = rest
    load = table_load(table_in, table, sem)
    weight[...] = later_weight(weight_in, parts)
    own = received.at[lax.axis_index("core")]
    state = [lambda cut, ref=ref: ref[:, cut] for ref in (power, charge, dyn)]
    primal, dual = local_step(dims, slot_rows, weight[...], own, inputs, state,
                              later_edges(dims, slot_rows, received, parts, edge_in),
                              (power_out, charge_out, dyn_out), edge_out)
    power_row[...] = row_power(dims, first_rows, weight[...], first.at[lax.axis_index("core")], row_in[...],
                               take_row(own, SLOT_DYN, *dims, slot_rows), pushed_row[...], bar)
    feeder_part(dims, slot_rows, load, weight[...], primal, dual, bar, dyn_out, duals_t, limits_t, values, table,
                duals_out, pushed_out, slots, spread, sums)


def last_kernel(dims, first_rows, slot_rows, first, received, parts, weight_in, row_in, power, charge, dyn, edge_in,
                pushed_row, inputs, duals_t, limits_t, values, table_in, power_out, charge_out, dyn_out, duals_out,
                bar, spread, table, sem):
    load = table_load(table_in, table, sem)
    weight = later_weight(weight_in, parts)
    own = received.at[lax.axis_index("core")]
    state = [lambda cut, ref=ref: ref[:, cut] for ref in (power, charge, dyn)]
    local_step(dims, slot_rows, weight, own, inputs, state, later_edges(dims, slot_rows, received, parts, edge_in),
               (power_out, charge_out, dyn_out), None)
    row_power(dims, first_rows, weight, first.at[lax.axis_index("core")], row_in[...], take_row(own, SLOT_DYN, *dims, slot_rows),
              pushed_row[...], bar)
    new = feeder_duals(values, table, load, bar, weight, duals_t[...], limits_t[...], spread)
    duals_out[...] = jnp.transpose(new)[: duals_out.shape[0]]


def relay_kernel(dims, slot_rows, received, parts):
    pieces, groups = dims
    z, core, bat = places()
    chips = lax.axis_size("z")
    lines = parts.shape[0] // chips
    parts[...] = jnp.zeros_like(parts)
    summed = sum(row_sum(received[k, pl.ds(2 * pieces, groups, stride=slot_rows), :]) for k in range(2))
    parts[pl.ds(0, chips, stride=lines), :] = jnp.broadcast_to(summed, (chips, LANES))

    @pl.when((core == 1) & (z > 0))
    def _():
        for i in range(pieces):
            parts[pl.ds((z - 1) * lines + 1 + i, 1), :] = received[0, pl.ds(bat * slot_rows + i, 1), :]

    @pl.when((core == 0) & (z < chips - 1))
    def _():
        for i in range(pieces):
            parts[pl.ds((z + 1) * lines + 1 + i, 1), :] = received[1, pl.ds(bat * slot_rows + pieces + i, 1), :]


def shapes(*dims):
    return [jax.ShapeDtypeStruct(dim, F32) for dim in dims]


def call(kernel, name, in_specs, out_dims, scratch=(), flops=0, moved=0, limit=16 * 1024 * 1024, copies=0, table=0):
    more = [pltpu.SemaphoreType.DMA((copies,))] if copies else []
    if table:
        more += [pltpu.SMEM((table,), jnp.int32), pltpu.SemaphoreType.DMA]
    return pl.pallas_call(
        kernel,
        name=name,
        in_specs=in_specs,
        out_specs=[VMEM] * len(out_dims),
        out_shape=shapes(*out_dims),
        scratch_shapes=[pltpu.VMEM(dim, F32) for dim in scratch] + more,
        compiler_params=pltpu.CompilerParams(vmem_limit_bytes=limit),
        cost_estimate=pl.CostEstimate(flops=flops, bytes_accessed=moved, transcendentals=0),
    )


def stacked(*arrays):
    shape = (len(arrays),) + arrays[0].shape
    index = lax.broadcasted_iota(jnp.int32, shape, 0)
    out = jnp.broadcast_to(arrays[-1], shape)
    for i, array in enumerate(arrays[:-1]):
        out = jnp.where(index == i, array, out)
    return out


def exchange(value, axis):
    return lax.all_to_all(value, axis, 0, 0, tiled=True)


def shards(power0, charge0, dyn_dual0, feeder_dual0, price, inflow, power_limit, capacity, feeder_limit,
           block_values, block_cols, block_offsets):
    groups, local = power0.shape
    pieces = local // LANES
    blocks, blk = block_values.shape[:2]
    feeds = block_offsets.shape[0] - 1
    chips = lax.axis_size("z")
    first_rows, slot_rows, lines = rows_up(5 * pieces), rows_up(2 * pieces + 1), 1 + pieces
    dims = (pieces, groups)
    row, line, square, own = (pieces * groups, LANES), (1, LANES), (blk, LANES), (groups, local)
    spread, sums = (feeds, blk, LANES), (pieces * groups, 8, LANES)
    matrix_specs = [VMEM, VMEM]
    work, moved = 2 * blocks * blk * LANES, 4 * blocks * blk * LANES

    inputs = stacked(power0, charge0, dyn_dual0, price, inflow, power_limit, capacity)
    duals = stacked(feeder_dual0.reshape(feeds, blk), feeder_limit.reshape(feeds, blk))
    tables = lax.optimization_barrier(jnp.concatenate([block_cols, block_offsets]))
    block_cols, block_offsets = tables[:blocks], tables[blocks:]
    index_all = lax.broadcasted_iota(jnp.int32, (blocks, feeds - 1), 0)
    row_of = jnp.sum((index_all >= block_offsets[None, 1:-1]).astype(jnp.int32), axis=1)
    matrix = (block_values, jnp.concatenate([row_of, (block_cols % pieces) * groups + block_cols // pieces]))

    edges = call(edges_kernel, "edges", [VMEM], [(2, local)], flops=EARLY_COPY_FLOPS)(inputs)[0]
    links = [(i, i + 1 if i % 2 else i - 1) for i in range(1, 2 * chips - 1)]
    across = lax.ppermute(edges, ("z", "core"), links)
    first, duals_t, limits_t, pushed = call(
        functools.partial(first_kernel, dims, first_rows), "first",
        [VMEM] * 4, [(2, groups * first_rows, LANES), square, square, row],
        [spread] + [sums] * ADJOINT_PARTS, work, moved, table=2 * blocks,
    )(duals, inputs, *matrix)
    first, across = lax.optimization_barrier((first, across))
    first = exchange(first.reshape(2 * groups, first_rows, LANES), ("core", "bat"))
    first = first.reshape(2, groups * first_rows, LANES)

    both = (2, groups * slot_rows, LANES)
    step_outs = [line, row] + [own] * 3 + [(1, local), square, row, both]
    scratch = [row, spread] + [sums] * ADJOINT_PARTS
    for iteration in range(ITERS):
        last = iteration + 1 == ITERS
        outs = [own] * 3 + [(feeds, blk)] if last else step_outs
        sizes = (dims, first_rows, slot_rows)
        if iteration == 0:
            results = call(
                functools.partial(step_one_kernel, *sizes), "step_one", [VMEM] * 6 + matrix_specs, outs, scratch,
                2 * work, moved, table=2 * blocks,
            )(first, across, pushed, inputs, duals_t, limits_t, *matrix)
        else:
            results = call(
                functools.partial(last_kernel if last else step_kernel, *sizes), "last" if last else "step",
                [VMEM] * 13 + matrix_specs, outs, scratch[:2] if last else scratch, 2 * work, moved,
                table=2 * blocks,
            )(first, received, parts, weight, power_row, power, charge, dyn, edge, pushed, inputs, duals_t, limits_t,
              *matrix)
        if not last:
            weight, power_row, power, charge, dyn, edge, duals_t, pushed, slots = results
            received = exchange(slots.reshape(2 * groups, slot_rows, LANES), ("core", "bat")).reshape(both)
            parts = call(
                functools.partial(relay_kernel, dims, slot_rows), "relay", [VMEM], [(chips * lines, LANES)]
            )(received)[0]
            parts = exchange(parts.reshape(chips, lines, LANES), "z").reshape(chips * lines, LANES)
    power, charge, dyn_dual, feeder_dual = results
    return power, charge, dyn_dual, feeder_dual.reshape(1, feeds * blk)


def solution(mesh):
    fine = jax.sharding.Mesh(
        mesh.devices.reshape(mesh.shape["tm"] // 2, 2, mesh.shape["bat"]), ("z", "core", "bat")
    )
    split = P(("z", "core"), "bat")
    steps = P(("z", "core", "bat"), None)
    return jax.shard_map(
        shards,
        mesh=fine,
        in_specs=(split, split, split, steps, split, split, P("bat"), P("bat"), P(), P(), P(), P()),
        out_specs=(split, split, split, steps),
        check_vma=False,
    )
```

```python
import functools

import jax
import jax.numpy as jnp
from jax import lax
from jax.experimental import pallas as pl
from jax.experimental.pallas import tpu as pltpu
from jax.sharding import PartitionSpec as P

ITERS = 4
ETA_STEP = 0.4
EPS_NORM = 1e-06
LANES = 128
HALF = LANES // 2
ADJOINT_UNROLL = 24
ADJOINT_PARTS = 4
APPLY_UNROLL = 8
EARLY_COPY_FLOPS = 2 * 10**10
F32 = jnp.float32


VMEM = pl.BlockSpec(memory_space=pltpu.VMEM)

POWER, CHARGE, DYN, PRICE, INFLOW, LIMIT, CAPACITY = range(7)
SLOT_DYN, SLOT_PUSHED, SLOT_POWER, SLOT_PRICE, SLOT_LIMIT = range(5)


def places():
    return lax.axis_index("z"), lax.axis_index("core"), lax.axis_index("bat")


def rows_up(count):
    return -(-count // 8) * 8


def lane_iota(shape):
    return lax.broadcasted_iota(jnp.int32, shape, len(shape) - 1)


def clip(value, low, high):
    return jnp.minimum(jnp.maximum(value, low), high)


def total(value):
    return jnp.sum(jnp.sum(value, axis=0, keepdims=True), axis=1, keepdims=True)


def take_row(ref, array, pieces, groups, slot_rows):
    parts = [ref[pl.ds(array * pieces + i, groups, stride=slot_rows), :] for i in range(pieces)]
    return jnp.concatenate(parts, axis=0)


def put_row(ref, array, value, pieces, groups, slot_rows):
    for i in range(pieces):
        ref[pl.ds(array * pieces + i, groups, stride=slot_rows), :] = value[i * groups : (i + 1) * groups]


def unrolled(count, most):
    return max(u for u in range(1, most + 1) if count % u == 0)


def adjoint_loop(values, table, spread, sums, begin, end):
    blocks, blk = values.shape[:2]
    ways = unrolled(end - begin, ADJOINT_UNROLL)

    def step(k, carry):
        for u in range(ways):
            j = begin + k * ways + u
            product = values[j] * spread[table[j]]
            c = table[blocks + j]
            part = sums[u % len(sums)]
            part[c] = part[c] + jnp.sum(product.reshape(blk // 8, 8, LANES), axis=0)
        return carry

    lax.fori_loop(0, (end - begin) // ways, step, 0)


def adjoint_start(sums):
    for part in sums:
        part[...] = jnp.zeros_like(part)


def adjoint_total(sums):
    return jnp.sum(sum(part[...] for part in sums), axis=1)


def feeder_adjoint(values, table, spread, sums):
    adjoint_loop(values, table, spread, sums, 0, values.shape[0])
    return adjoint_total(sums)


def feeder_duals(values, table, load, field, weight, duals_t, limits_t, spread):
    blocks, blk = values.shape[:2]
    feeds = spread.shape[0]
    ways = unrolled(blocks, APPLY_UNROLL)
    step_dual = ETA_STEP * weight[:, :1]
    shifted = duals_t - step_dual * limits_t
    lane = lane_iota((blk, LANES))
    for f in range(feeds):
        spread[f] = jnp.where(lane == f, shifted, 0.0)
    load.wait()

    def step(k, carry):
        for u in range(ways):
            j = k * ways + u
            f = table[j]
            spread[f] = spread[f] + values[j] * field[pl.ds(table[blocks + j], 1), :]
        return carry

    lax.fori_loop(0, blocks // ways, step, 0)
    new = jnp.zeros((blk, LANES), F32)
    for f in range(feeds):
        dual = jnp.maximum(0.0, jnp.sum(spread[f], axis=1, keepdims=True))
        spread[f] = jnp.broadcast_to(dual, (blk, LANES))
        new = jnp.where(lane == f, dual, new)
    return new


def pack_sums(primal, dual):
    lane = lane_iota(primal.shape)
    return jnp.where(
        lane < HALF, primal + pltpu.roll(primal, HALF, 1), dual + pltpu.roll(dual, HALF, 1)
    )


def next_weight(weight, parts):
    both = jnp.sum(parts, axis=0, keepdims=True)
    lane = lane_iota(both.shape)
    primal_sq = total(jnp.where(lane < HALF, both, 0.0))
    dual_sq = total(jnp.where(lane < HALF, 0.0, both))
    ratio = jnp.sqrt((dual_sq + EPS_NORM) / (primal_sq + EPS_NORM))
    return jnp.broadcast_to(jnp.sqrt(weight[:, :1] * ratio), (1, LANES))


def row_sum(value):
    return jnp.sum(value, axis=0, keepdims=True)


def table_load(table_in, table, sem):
    copy = pltpu.make_async_copy(table_in, table, sem)
    copy.start()
    return copy


def edges_kernel(inputs, edges, swapped):
    last = inputs.shape[1] - 1
    edges[:1, :] = jnp.where(lax.axis_index("core") == 0, inputs[DYN, :1, :], inputs[DYN, last:, :])
    edges[1:, :] = inputs[CHARGE, last:, :]
    for k, (array, line) in enumerate(((DYN, 0), (DYN, last), (CHARGE, last))):
        swapped[k : k + 1, :] = inputs[array, line : line + 1, :]


def first_kernel(dims, first_rows, duals, inputs, values, table_in, slots, duals_t, limits_t, pushed_out,
                 spread, *rest):
    pieces, groups = dims
    *sums, table, sem = rest
    load = table_load(table_in, table, sem)
    blocks, blk = values.shape[:2]
    feeds = duals.shape[1]
    for i, target in enumerate((duals_t, limits_t)):
        padded = jnp.concatenate([duals[i], jnp.zeros((blk - feeds, LANES), F32)], axis=0)
        target[...] = jnp.transpose(padded)
    for f in range(feeds):
        spread[f] = jnp.broadcast_to(duals_t[:, f : f + 1], (blk, LANES))
    sent = ((SLOT_DYN, DYN), (SLOT_POWER, POWER), (SLOT_PRICE, PRICE), (SLOT_LIMIT, LIMIT))
    for i in range(pieces):
        for slot, array in sent:
            slots[pl.ds(slot * pieces + i, groups, stride=first_rows), :] = inputs[array, :, i * LANES : (i + 1) * LANES]
    adjoint_start(sums)
    load.wait()
    adjoint_loop(values, table, spread, sums, 0, blocks)
    pushed = adjoint_total(sums)
    pushed_out[...] = pushed
    put_row(slots, SLOT_PUSHED, pushed, pieces, groups, first_rows)


def local_step(dims, slot_rows, weight, received, inputs, state, edges, state_out, edge_out):
    pieces, groups = dims
    step_primal = ETA_STEP / weight[:, :1]
    step_dual = ETA_STEP * weight[:, :1]
    after, before_dyn, before_charge = edges
    z, core, _ = places()
    begin = (z == 0) & (core == 0)
    line = lax.broadcasted_iota(jnp.int32, (groups, LANES), 0)
    primal = jnp.zeros((1, LANES), F32)
    dual = jnp.zeros((1, LANES), F32)
    for i in range(pieces):
        cut = slice(i * LANES, (i + 1) * LANES)
        power, charge, dyn = (read(cut) for read in state)
        price, inflow, limit, capacity = (inputs[array, :, cut] for array in (PRICE, INFLOW, LIMIT, CAPACITY))
        pushed = received[pl.ds(SLOT_PUSHED * pieces + i, groups, stride=slot_rows), :]
        power_new = clip(power - step_primal * (price - dyn + pushed), -limit, limit)
        dyn_next = jnp.where(line == groups - 1, after(i), pltpu.roll(dyn, groups - 1, 0))
        charge_new = clip(charge - step_primal * (dyn - dyn_next), 0.0, capacity)
        power_bar = 2.0 * power_new - power
        charge_bar = 2.0 * charge_new - charge
        edge_charge = before_charge(i)
        edge_new = clip(edge_charge - step_primal * (before_dyn(i) - dyn[:1]), 0.0, capacity[:1])
        edge_bar = jnp.where(begin, 0.0, 2.0 * edge_new - edge_charge)
        prev_bar = jnp.where(line == 0, edge_bar, pltpu.roll(charge_bar, 1, 0))
        dyn_new = dyn + step_dual * (charge_bar - prev_bar - power_bar - inflow)
        for ref, value in zip(state_out, (power_new, charge_new, dyn_new)):
            ref[:, cut] = value
        if edge_out is not None:
            edge_out[:, cut] = edge_new
        primal = primal + row_sum((power_new - power) ** 2 + (charge_new - charge) ** 2)
        dual = dual + row_sum((dyn_new - dyn) ** 2)
    return primal, dual


def row_power(dims, first_rows, weight, first, power, dyn, pushed, bar):
    pieces, groups = dims
    step_primal = ETA_STEP / weight[:, :1]
    price = take_row(first, SLOT_PRICE, pieces, groups, first_rows)
    limit = take_row(first, SLOT_LIMIT, pieces, groups, first_rows)
    new = clip(power - step_primal * (price - dyn + pushed), -limit, limit)
    bar[...] = (ETA_STEP * weight[:, :1]) * (2.0 * new - power)
    return new


def feeder_part(dims, slot_rows, load, weight, primal, dual, bar, dyn, duals_t, limits_t, values, table,
                duals_out, pushed_out, slots, spread, sums):
    pieces, groups = dims
    _, core, bat = places()
    new = feeder_duals(values, table, load, bar, weight, duals_t[...], limits_t[...], spread)
    duals_out[...] = new
    parts = pack_sums(primal, dual + row_sum((new - duals_t[...]) ** 2))
    adjoint_start(sums)
    slots[...] = jnp.zeros_like(slots)
    own, other = slots.at[core], slots.at[1 - core]
    for side in (own, other):
        side[pl.ds(2 * pieces, groups, stride=slot_rows), :] = jnp.broadcast_to(parts, (groups, LANES))
    for i in range(pieces):
        cut = slice(i * LANES, (i + 1) * LANES)
        own[pl.ds(SLOT_DYN * pieces + i, groups, stride=slot_rows), :] = dyn[:, cut]
        other[pl.ds(bat * slot_rows + i, 1), :] = dyn[:1, cut]
        other[pl.ds(bat * slot_rows + pieces + i, 1), :] = dyn[groups - 1 :, cut]
    pushed = feeder_adjoint(values, table, spread, sums)
    pushed_out[...] = pushed
    put_row(own, SLOT_PUSHED, pushed, pieces, groups, slot_rows)


def step_one_kernel(dims, first_rows, slot_rows, first, across, swapped, pushed_row, inputs, duals_t, limits_t, values,
                    table_in, weight, power_row, power_out, charge_out, dyn_out, edge_out, duals_out, pushed_out, slots,
                    bar, spread, *rest):
    *sums, table, sem = rest
    pieces, groups = dims
    load = table_load(table_in, table, sem)
    weight[...] = jnp.ones_like(weight)
    state = [lambda cut, array=array: inputs[array, :, cut] for array in (POWER, CHARGE, DYN)]
    core = lax.axis_index("core")
    linked = lambda k, i: across[k : k + 1, i * LANES : (i + 1) * LANES]
    partner = lambda k, i: swapped[k : k + 1, i * LANES : (i + 1) * LANES]
    edges = (
        lambda i: jnp.where(core == 0, partner(0, i), linked(0, i)),
        lambda i: jnp.where(core == 0, linked(0, i), partner(1, i)),
        lambda i: jnp.where(core == 0, linked(1, i), partner(2, i)),
    )
    primal, dual = local_step(dims, first_rows, weight[...], first, inputs, state, edges,
                              (power_out, charge_out, dyn_out), edge_out)
    power_row[...] = row_power(dims, first_rows, weight[...], first,
                               take_row(first, SLOT_POWER, pieces, groups, first_rows),
                               take_row(first, SLOT_DYN, pieces, groups, first_rows), pushed_row[...], bar)
    feeder_part(dims, slot_rows, load, weight[...], primal, dual, bar, dyn_out, duals_t, limits_t, values, table,
                duals_out, pushed_out, slots, spread, sums)


def later_edges(dims, slot_rows, received, parts, edge_in):
    pieces, _ = dims
    z, core, bat = places()
    chips = lax.axis_size("z")
    lines = parts.shape[0] // chips
    above, below = jnp.minimum(z + 1, chips - 1), jnp.maximum(z - 1, 0)
    end = jnp.where(z == chips - 1, 0.0, 1.0).astype(F32)
    after = lambda i: jnp.where(
        core == 0, received[1, pl.ds(bat * slot_rows + i, 1), :], end * parts[pl.ds(above * lines + 1 + i, 1), :]
    )
    before_dyn = lambda i: jnp.where(
        core == 0, parts[pl.ds(below * lines + 1 + i, 1), :], received[0, pl.ds(bat * slot_rows + pieces + i, 1), :]
    )
    before_charge = lambda i: edge_in[:, i * LANES : (i + 1) * LANES]
    return after, before_dyn, before_charge


def later_weight(weight_in, parts):
    chips = lax.axis_size("z")
    return next_weight(weight_in[...], parts[pl.ds(0, chips, stride=parts.shape[0] // chips), :])


def step_kernel(dims, first_rows, slot_rows, first, received, parts, weight_in, row_in, power, charge, dyn, edge_in,
                pushed_row, inputs, duals_t, limits_t, values, table_in, weight, power_row, power_out, charge_out,
                dyn_out, edge_out, duals_out, pushed_out, slots, bar, spread, *rest):
    *sums, table, sem = rest
    load = table_load(table_in, table, sem)
    weight[...] = later_weight(weight_in, parts)
    own = received.at[lax.axis_index("core")]
    state = [lambda cut, ref=ref: ref[:, cut] for ref in (power, charge, dyn)]
    primal, dual = local_step(dims, slot_rows, weight[...], own, inputs, state,
                              later_edges(dims, slot_rows, received, parts, edge_in),
                              (power_out, charge_out, dyn_out), edge_out)
    power_row[...] = row_power(dims, first_rows, weight[...], first, row_in[...],
                               take_row(own, SLOT_DYN, *dims, slot_rows), pushed_row[...], bar)
    feeder_part(dims, slot_rows, load, weight[...], primal, dual, bar, dyn_out, duals_t, limits_t, values, table,
                duals_out, pushed_out, slots, spread, sums)


def last_kernel(dims, first_rows, slot_rows, first, received, parts, weight_in, row_in, power, charge, dyn, edge_in,
                pushed_row, inputs, duals_t, limits_t, values, table_in, power_out, charge_out, dyn_out, duals_out,
                bar, spread, table, sem):
    load = table_load(table_in, table, sem)
    weight = later_weight(weight_in, parts)
    own = received.at[lax.axis_index("core")]
    state = [lambda cut, ref=ref: ref[:, cut] for ref in (power, charge, dyn)]
    local_step(dims, slot_rows, weight, own, inputs, state, later_edges(dims, slot_rows, received, parts, edge_in),
               (power_out, charge_out, dyn_out), None)
    row_power(dims, first_rows, weight, first, row_in[...], take_row(own, SLOT_DYN, *dims, slot_rows),
              pushed_row[...], bar)
    new = feeder_duals(values, table, load, bar, weight, duals_t[...], limits_t[...], spread)
    duals_out[...] = jnp.transpose(new)[: duals_out.shape[0]]


def relay_kernel(dims, slot_rows, received, parts):
    pieces, groups = dims
    z, core, bat = places()
    chips = lax.axis_size("z")
    lines = parts.shape[0] // chips
    parts[...] = jnp.zeros_like(parts)
    summed = sum(row_sum(received[k, pl.ds(2 * pieces, groups, stride=slot_rows), :]) for k in range(2))
    parts[pl.ds(0, chips, stride=lines), :] = jnp.broadcast_to(summed, (chips, LANES))

    @pl.when((core == 1) & (z > 0))
    def _():
        for i in range(pieces):
            parts[pl.ds((z - 1) * lines + 1 + i, 1), :] = received[0, pl.ds(bat * slot_rows + i, 1), :]

    @pl.when((core == 0) & (z < chips - 1))
    def _():
        for i in range(pieces):
            parts[pl.ds((z + 1) * lines + 1 + i, 1), :] = received[1, pl.ds(bat * slot_rows + pieces + i, 1), :]


def shapes(*dims):
    return [jax.ShapeDtypeStruct(dim, F32) for dim in dims]


def call(kernel, name, in_specs, out_dims, scratch=(), flops=0, moved=0, limit=16 * 1024 * 1024, copies=0, table=0):
    more = [pltpu.SemaphoreType.DMA((copies,))] if copies else []
    if table:
        more += [pltpu.SMEM((table,), jnp.int32), pltpu.SemaphoreType.DMA]
    return pl.pallas_call(
        kernel,
        name=name,
        in_specs=in_specs,
        out_specs=[VMEM] * len(out_dims),
        out_shape=shapes(*out_dims),
        scratch_shapes=[pltpu.VMEM(dim, F32) for dim in scratch] + more,
        compiler_params=pltpu.CompilerParams(vmem_limit_bytes=limit),
        cost_estimate=pl.CostEstimate(flops=flops, bytes_accessed=moved, transcendentals=0),
    )


def stacked(*arrays):
    shape = (len(arrays),) + arrays[0].shape
    index = lax.broadcasted_iota(jnp.int32, shape, 0)
    out = jnp.broadcast_to(arrays[-1], shape)
    for i, array in enumerate(arrays[:-1]):
        out = jnp.where(index == i, array, out)
    return out


def exchange(value, axis):
    return lax.all_to_all(value, axis, 0, 0, tiled=True)


def shards(power0, charge0, dyn_dual0, feeder_dual0, price, inflow, power_limit, capacity, feeder_limit,
           block_values, block_cols, block_offsets):
    groups, local = power0.shape
    pieces = local // LANES
    blocks, blk = block_values.shape[:2]
    feeds = block_offsets.shape[0] - 1
    chips = lax.axis_size("z")
    first_rows, slot_rows, lines = rows_up(5 * pieces), rows_up(2 * pieces + 1), 1 + pieces
    dims = (pieces, groups)
    row, line, square, own = (pieces * groups, LANES), (1, LANES), (blk, LANES), (groups, local)
    spread, sums = (feeds, blk, LANES), (pieces * groups, 8, LANES)
    matrix_specs = [VMEM, VMEM]
    work, moved = 2 * blocks * blk * LANES, 4 * blocks * blk * LANES

    inputs = stacked(power0, charge0, dyn_dual0, price, inflow, power_limit, capacity)
    duals = stacked(feeder_dual0.reshape(feeds, blk), feeder_limit.reshape(feeds, blk))
    tables = lax.optimization_barrier(jnp.concatenate([block_cols, block_offsets]))
    block_cols, block_offsets = tables[:blocks], tables[blocks:]
    index_all = lax.broadcasted_iota(jnp.int32, (blocks, feeds - 1), 0)
    row_of = jnp.sum((index_all >= block_offsets[None, 1:-1]).astype(jnp.int32), axis=1)
    matrix = (block_values, jnp.concatenate([row_of, (block_cols % pieces) * groups + block_cols // pieces]))

    edges, swapped = call(edges_kernel, "edges", [VMEM], [(2, local), (3, local)], flops=EARLY_COPY_FLOPS)(inputs)
    swapped = lax.ppermute(swapped, "core", [(0, 1), (1, 0)])
    links = [(i, i + 1 if i % 2 else i - 1) for i in range(1, 2 * chips - 1)]
    across = lax.ppermute(edges, ("z", "core"), links)
    first, duals_t, limits_t, pushed = call(
        functools.partial(first_kernel, dims, first_rows), "first",
        [VMEM] * 4, [(groups * first_rows, LANES), square, square, row],
        [spread] + [sums] * ADJOINT_PARTS, work, moved, table=2 * blocks,
    )(duals, inputs, *matrix)
    first, across, swapped = lax.optimization_barrier((first, across, swapped))
    first = exchange(first.reshape(groups, first_rows, LANES), "bat").reshape(groups * first_rows, LANES)

    both = (2, groups * slot_rows, LANES)
    step_outs = [line, row] + [own] * 3 + [(1, local), square, row, both]
    scratch = [row, spread] + [sums] * ADJOINT_PARTS
    for iteration in range(ITERS):
        last = iteration + 1 == ITERS
        outs = [own] * 3 + [(feeds, blk)] if last else step_outs
        sizes = (dims, first_rows, slot_rows)
        if iteration == 0:
            results = call(
                functools.partial(step_one_kernel, *sizes), "step_one", [VMEM] * 7 + matrix_specs, outs, scratch,
                2 * work, moved, table=2 * blocks,
            )(first, across, swapped, pushed, inputs, duals_t, limits_t, *matrix)
        else:
            results = call(
                functools.partial(last_kernel if last else step_kernel, *sizes), "last" if last else "step",
                [VMEM] * 13 + matrix_specs, outs, scratch[:2] if last else scratch, 2 * work, moved,
                table=2 * blocks,
            )(first, received, parts, weight, power_row, power, charge, dyn, edge, pushed, inputs, duals_t, limits_t,
              *matrix)
        if not last:
            weight, power_row, power, charge, dyn, edge, duals_t, pushed, slots = results
            received = exchange(slots.reshape(2 * groups, slot_rows, LANES), ("core", "bat")).reshape(both)
            parts = call(
                functools.partial(relay_kernel, dims, slot_rows), "relay", [VMEM], [(chips * lines, LANES)]
            )(received)[0]
            parts = exchange(parts.reshape(chips, lines, LANES), "z").reshape(chips * lines, LANES)
    power, charge, dyn_dual, feeder_dual = results
    return power, charge, dyn_dual, feeder_dual.reshape(1, feeds * blk)


def solution(mesh):
    fine = jax.sharding.Mesh(
        mesh.devices.reshape(mesh.shape["tm"] // 2, 2, mesh.shape["bat"]), ("z", "core", "bat")
    )
    split = P(("z", "core"), "bat")
    steps = P(("z", "core", "bat"), None)
    return jax.shard_map(
        shards,
        mesh=fine,
        in_specs=(split, split, split, steps, split, split, P("bat"), P("bat"), P(), P(), P(), P()),
        out_specs=(split, split, split, steps),
        check_vma=False,
    )
```

```python
import functools

import jax
import jax.numpy as jnp
from jax import lax
from jax.experimental import pallas as pl
from jax.experimental.pallas import tpu as pltpu
from jax.sharding import PartitionSpec as P

ITERS = 4
ETA_STEP = 0.4
EPS_NORM = 1e-06
LANES = 128
HALF = LANES // 2
ADJOINT_UNROLL = 24
ADJOINT_PARTS = 4
APPLY_UNROLL = 8
EARLY_COPY_FLOPS = 2 * 10**10
F32 = jnp.float32


VMEM = pl.BlockSpec(memory_space=pltpu.VMEM)

POWER, CHARGE, DYN, PRICE, INFLOW, LIMIT, CAPACITY = range(7)
SLOT_DYN, SLOT_PUSHED, SLOT_POWER, SLOT_PRICE, SLOT_LIMIT = range(5)


def places():
    return lax.axis_index("z"), lax.axis_index("core"), lax.axis_index("bat")


def rows_up(count):
    return -(-count // 8) * 8


def lane_iota(shape):
    return lax.broadcasted_iota(jnp.int32, shape, len(shape) - 1)


def clip(value, low, high):
    return jnp.minimum(jnp.maximum(value, low), high)


def total(value):
    return jnp.sum(jnp.sum(value, axis=0, keepdims=True), axis=1, keepdims=True)


def take_row(ref, array, pieces, groups, slot_rows):
    parts = [ref[pl.ds(array * pieces + i, groups, stride=slot_rows), :] for i in range(pieces)]
    return jnp.concatenate(parts, axis=0)


def put_row(ref, array, value, pieces, groups, slot_rows):
    for i in range(pieces):
        ref[pl.ds(array * pieces + i, groups, stride=slot_rows), :] = value[i * groups : (i + 1) * groups]


def unrolled(count, most):
    return max(u for u in range(1, most + 1) if count % u == 0)


def adjoint_loop(values, table, spread, sums, begin, end):
    blocks, blk = values.shape[:2]
    ways = unrolled(end - begin, ADJOINT_UNROLL)

    def step(k, carry):
        for u in range(ways):
            j = begin + k * ways + u
            product = values[j] * spread[table[j]]
            c = table[blocks + j]
            part = sums[u % len(sums)]
            part[c] = part[c] + jnp.sum(product.reshape(blk // 8, 8, LANES), axis=0)
        return carry

    lax.fori_loop(0, (end - begin) // ways, step, 0)


def adjoint_start(sums):
    for part in sums:
        part[...] = jnp.zeros_like(part)


def adjoint_total(sums):
    return jnp.sum(sum(part[...] for part in sums), axis=1)


def feeder_adjoint(values, table, spread, sums):
    adjoint_loop(values, table, spread, sums, 0, values.shape[0])
    return adjoint_total(sums)


def feeder_duals(values, table, load, field, weight, duals_t, limits_t, spread, local):
    blocks, blk = values.shape[:2]
    feeds = spread.shape[0]
    ways = unrolled(blocks, APPLY_UNROLL)
    step_dual = ETA_STEP * weight[:, :1]
    shifted = duals_t - step_dual * limits_t
    lane = lane_iota((blk, LANES))
    for f in range(feeds):
        spread[f] = jnp.where(lane == f, shifted, 0.0)
    load.wait()

    def step(k, carry):
        for u in range(ways):
            j = k * ways + u
            f = table[j]
            spread[f] = spread[f] + values[j] * field[pl.ds(table[blocks + j], 1), :]
        return carry

    lax.fori_loop(0, blocks // ways, step, 0)
    squares = local()
    new = jnp.zeros((blk, LANES), F32)
    for f in range(feeds):
        dual = jnp.maximum(0.0, jnp.sum(spread[f], axis=1, keepdims=True))
        spread[f] = jnp.broadcast_to(dual, (blk, LANES))
        new = jnp.where(lane == f, dual, new)
    return new, squares


def pack_sums(primal, dual):
    lane = lane_iota(primal.shape)
    return jnp.where(
        lane < HALF, primal + pltpu.roll(primal, HALF, 1), dual + pltpu.roll(dual, HALF, 1)
    )


def next_weight(weight, parts):
    both = jnp.sum(parts, axis=0, keepdims=True)
    lane = lane_iota(both.shape)
    primal_sq = total(jnp.where(lane < HALF, both, 0.0))
    dual_sq = total(jnp.where(lane < HALF, 0.0, both))
    ratio = jnp.sqrt((dual_sq + EPS_NORM) / (primal_sq + EPS_NORM))
    return jnp.broadcast_to(jnp.sqrt(weight[:, :1] * ratio), (1, LANES))


def row_sum(value):
    return jnp.sum(value, axis=0, keepdims=True)


def table_load(table_in, table, sem):
    copy = pltpu.make_async_copy(table_in, table, sem)
    copy.start()
    return copy


def edges_kernel(inputs, edges, swapped):
    last = inputs.shape[1] - 1
    edges[:1, :] = jnp.where(lax.axis_index("core") == 0, inputs[DYN, :1, :], inputs[DYN, last:, :])
    edges[1:, :] = inputs[CHARGE, last:, :]
    for k, (array, line) in enumerate(((DYN, 0), (DYN, last), (CHARGE, last))):
        swapped[k : k + 1, :] = inputs[array, line : line + 1, :]


def first_kernel(dims, first_rows, duals, inputs, values, table_in, slots, duals_t, limits_t, pushed_out,
                 spread, *rest):
    pieces, groups = dims
    *sums, table, sem = rest
    load = table_load(table_in, table, sem)
    blocks, blk = values.shape[:2]
    feeds = duals.shape[1]
    for i, target in enumerate((duals_t, limits_t)):
        padded = jnp.concatenate([duals[i], jnp.zeros((blk - feeds, LANES), F32)], axis=0)
        target[...] = jnp.transpose(padded)
    for f in range(feeds):
        spread[f] = jnp.broadcast_to(duals_t[:, f : f + 1], (blk, LANES))
    sent = ((SLOT_DYN, DYN), (SLOT_POWER, POWER), (SLOT_PRICE, PRICE), (SLOT_LIMIT, LIMIT))
    for i in range(pieces):
        for slot, array in sent:
            slots[pl.ds(slot * pieces + i, groups, stride=first_rows), :] = inputs[array, :, i * LANES : (i + 1) * LANES]
    adjoint_start(sums)
    load.wait()
    adjoint_loop(values, table, spread, sums, 0, blocks)
    pushed = adjoint_total(sums)
    pushed_out[...] = pushed
    put_row(slots, SLOT_PUSHED, pushed, pieces, groups, first_rows)


def local_step(dims, slot_rows, weight, received, inputs, state, edges, state_out, edge_out):
    pieces, groups = dims
    step_primal = ETA_STEP / weight[:, :1]
    step_dual = ETA_STEP * weight[:, :1]
    after, before_dyn, before_charge = edges
    z, core, _ = places()
    begin = (z == 0) & (core == 0)
    line = lax.broadcasted_iota(jnp.int32, (groups, LANES), 0)
    primal = jnp.zeros((1, LANES), F32)
    dual = jnp.zeros((1, LANES), F32)
    for i in range(pieces):
        cut = slice(i * LANES, (i + 1) * LANES)
        power, charge, dyn = (read(cut) for read in state)
        price, inflow, limit, capacity = (inputs[array, :, cut] for array in (PRICE, INFLOW, LIMIT, CAPACITY))
        pushed = received[pl.ds(SLOT_PUSHED * pieces + i, groups, stride=slot_rows), :]
        power_new = clip(power - step_primal * (price - dyn + pushed), -limit, limit)
        dyn_next = jnp.where(line == groups - 1, after(i), pltpu.roll(dyn, groups - 1, 0))
        charge_new = clip(charge - step_primal * (dyn - dyn_next), 0.0, capacity)
        power_bar = 2.0 * power_new - power
        charge_bar = 2.0 * charge_new - charge
        edge_charge = before_charge(i)
        edge_new = clip(edge_charge - step_primal * (before_dyn(i) - dyn[:1]), 0.0, capacity[:1])
        edge_bar = jnp.where(begin, 0.0, 2.0 * edge_new - edge_charge)
        prev_bar = jnp.where(line == 0, edge_bar, pltpu.roll(charge_bar, 1, 0))
        dyn_new = dyn + step_dual * (charge_bar - prev_bar - power_bar - inflow)
        for ref, value in zip(state_out, (power_new, charge_new, dyn_new)):
            ref[:, cut] = value
        if edge_out is not None:
            edge_out[:, cut] = edge_new
        primal = primal + row_sum((power_new - power) ** 2 + (charge_new - charge) ** 2)
        dual = dual + row_sum((dyn_new - dyn) ** 2)
    return primal, dual


def row_power(dims, first_rows, weight, first, power, dyn, pushed, bar):
    pieces, groups = dims
    step_primal = ETA_STEP / weight[:, :1]
    price = take_row(first, SLOT_PRICE, pieces, groups, first_rows)
    limit = take_row(first, SLOT_LIMIT, pieces, groups, first_rows)
    new = clip(power - step_primal * (price - dyn + pushed), -limit, limit)
    bar[...] = (ETA_STEP * weight[:, :1]) * (2.0 * new - power)
    return new


def feeder_part(dims, slot_rows, load, weight, local, bar, dyn, duals_t, limits_t, values, table,
                duals_out, pushed_out, slots, spread, sums):
    pieces, groups = dims
    _, core, bat = places()
    new, (primal, dual) = feeder_duals(values, table, load, bar, weight, duals_t[...], limits_t[...], spread, local)
    duals_out[...] = new
    parts = pack_sums(primal, dual + row_sum((new - duals_t[...]) ** 2))
    adjoint_start(sums)
    slots[...] = jnp.zeros_like(slots)
    own, other = slots.at[core], slots.at[1 - core]
    for side in (own, other):
        side[pl.ds(2 * pieces, groups, stride=slot_rows), :] = jnp.broadcast_to(parts, (groups, LANES))
    for i in range(pieces):
        cut = slice(i * LANES, (i + 1) * LANES)
        own[pl.ds(SLOT_DYN * pieces + i, groups, stride=slot_rows), :] = dyn[:, cut]
        other[pl.ds(bat * slot_rows + i, 1), :] = dyn[:1, cut]
        other[pl.ds(bat * slot_rows + pieces + i, 1), :] = dyn[groups - 1 :, cut]
    pushed = feeder_adjoint(values, table, spread, sums)
    pushed_out[...] = pushed
    put_row(own, SLOT_PUSHED, pushed, pieces, groups, slot_rows)


def step_one_kernel(dims, first_rows, slot_rows, first, across, swapped, pushed_row, inputs, duals_t, limits_t, values,
                    table_in, weight, power_row, power_out, charge_out, dyn_out, edge_out, duals_out, pushed_out, slots,
                    bar, spread, *rest):
    *sums, table, sem = rest
    pieces, groups = dims
    load = table_load(table_in, table, sem)
    weight[...] = jnp.ones_like(weight)
    state = [lambda cut, array=array: inputs[array, :, cut] for array in (POWER, CHARGE, DYN)]
    core = lax.axis_index("core")
    linked = lambda k, i: across[k : k + 1, i * LANES : (i + 1) * LANES]
    partner = lambda k, i: swapped[k : k + 1, i * LANES : (i + 1) * LANES]
    edges = (
        lambda i: jnp.where(core == 0, partner(0, i), linked(0, i)),
        lambda i: jnp.where(core == 0, linked(0, i), partner(1, i)),
        lambda i: jnp.where(core == 0, linked(1, i), partner(2, i)),
    )
    local = lambda: local_step(dims, first_rows, weight[...], first, inputs, state, edges,
                              (power_out, charge_out, dyn_out), edge_out)
    power_row[...] = row_power(dims, first_rows, weight[...], first,
                               take_row(first, SLOT_POWER, pieces, groups, first_rows),
                               take_row(first, SLOT_DYN, pieces, groups, first_rows), pushed_row[...], bar)
    feeder_part(dims, slot_rows, load, weight[...], local, bar, dyn_out, duals_t, limits_t, values, table,
                duals_out, pushed_out, slots, spread, sums)


def later_edges(dims, slot_rows, received, parts, edge_in):
    pieces, _ = dims
    z, core, bat = places()
    chips = lax.axis_size("z")
    lines = parts.shape[0] // chips
    above, below = jnp.minimum(z + 1, chips - 1), jnp.maximum(z - 1, 0)
    end = jnp.where(z == chips - 1, 0.0, 1.0).astype(F32)
    after = lambda i: jnp.where(
        core == 0, received[1, pl.ds(bat * slot_rows + i, 1), :], end * parts[pl.ds(above * lines + 1 + i, 1), :]
    )
    before_dyn = lambda i: jnp.where(
        core == 0, parts[pl.ds(below * lines + 1 + i, 1), :], received[0, pl.ds(bat * slot_rows + pieces + i, 1), :]
    )
    before_charge = lambda i: edge_in[:, i * LANES : (i + 1) * LANES]
    return after, before_dyn, before_charge


def later_weight(weight_in, parts):
    chips = lax.axis_size("z")
    return next_weight(weight_in[...], parts[pl.ds(0, chips, stride=parts.shape[0] // chips), :])


def step_kernel(dims, first_rows, slot_rows, first, received, parts, weight_in, row_in, power, charge, dyn, edge_in,
                pushed_row, inputs, duals_t, limits_t, values, table_in, weight, power_row, power_out, charge_out,
                dyn_out, edge_out, duals_out, pushed_out, slots, bar, spread, *rest):
    *sums, table, sem = rest
    load = table_load(table_in, table, sem)
    weight[...] = later_weight(weight_in, parts)
    own = received.at[lax.axis_index("core")]
    state = [lambda cut, ref=ref: ref[:, cut] for ref in (power, charge, dyn)]
    local = lambda: local_step(dims, slot_rows, weight[...], own, inputs, state,
                              later_edges(dims, slot_rows, received, parts, edge_in),
                              (power_out, charge_out, dyn_out), edge_out)
    power_row[...] = row_power(dims, first_rows, weight[...], first, row_in[...],
                               take_row(own, SLOT_DYN, *dims, slot_rows), pushed_row[...], bar)
    feeder_part(dims, slot_rows, load, weight[...], local, bar, dyn_out, duals_t, limits_t, values, table,
                duals_out, pushed_out, slots, spread, sums)


def last_kernel(dims, first_rows, slot_rows, first, received, parts, weight_in, row_in, power, charge, dyn, edge_in,
                pushed_row, inputs, duals_t, limits_t, values, table_in, power_out, charge_out, dyn_out, duals_out,
                bar, spread, table, sem):
    load = table_load(table_in, table, sem)
    weight = later_weight(weight_in, parts)
    own = received.at[lax.axis_index("core")]
    state = [lambda cut, ref=ref: ref[:, cut] for ref in (power, charge, dyn)]
    local = lambda: local_step(dims, slot_rows, weight, own, inputs, state, later_edges(dims, slot_rows, received, parts, edge_in),
               (power_out, charge_out, dyn_out), None)
    row_power(dims, first_rows, weight, first, row_in[...], take_row(own, SLOT_DYN, *dims, slot_rows),
              pushed_row[...], bar)
    new, _ = feeder_duals(values, table, load, bar, weight, duals_t[...], limits_t[...], spread, local)
    duals_out[...] = jnp.transpose(new)[: duals_out.shape[0]]


def relay_kernel(dims, slot_rows, received, parts):
    pieces, groups = dims
    z, core, bat = places()
    chips = lax.axis_size("z")
    lines = parts.shape[0] // chips
    parts[...] = jnp.zeros_like(parts)
    summed = sum(row_sum(received[k, pl.ds(2 * pieces, groups, stride=slot_rows), :]) for k in range(2))
    parts[pl.ds(0, chips, stride=lines), :] = jnp.broadcast_to(summed, (chips, LANES))

    @pl.when((core == 1) & (z > 0))
    def _():
        for i in range(pieces):
            parts[pl.ds((z - 1) * lines + 1 + i, 1), :] = received[0, pl.ds(bat * slot_rows + i, 1), :]

    @pl.when((core == 0) & (z < chips - 1))
    def _():
        for i in range(pieces):
            parts[pl.ds((z + 1) * lines + 1 + i, 1), :] = received[1, pl.ds(bat * slot_rows + pieces + i, 1), :]


def shapes(*dims):
    return [jax.ShapeDtypeStruct(dim, F32) for dim in dims]


def call(kernel, name, in_specs, out_dims, scratch=(), flops=0, moved=0, limit=16 * 1024 * 1024, copies=0, table=0):
    more = [pltpu.SemaphoreType.DMA((copies,))] if copies else []
    if table:
        more += [pltpu.SMEM((table,), jnp.int32), pltpu.SemaphoreType.DMA]
    return pl.pallas_call(
        kernel,
        name=name,
        in_specs=in_specs,
        out_specs=[VMEM] * len(out_dims),
        out_shape=shapes(*out_dims),
        scratch_shapes=[pltpu.VMEM(dim, F32) for dim in scratch] + more,
        compiler_params=pltpu.CompilerParams(vmem_limit_bytes=limit),
        cost_estimate=pl.CostEstimate(flops=flops, bytes_accessed=moved, transcendentals=0),
    )


def stacked(*arrays):
    shape = (len(arrays),) + arrays[0].shape
    index = lax.broadcasted_iota(jnp.int32, shape, 0)
    out = jnp.broadcast_to(arrays[-1], shape)
    for i, array in enumerate(arrays[:-1]):
        out = jnp.where(index == i, array, out)
    return out


def exchange(value, axis):
    return lax.all_to_all(value, axis, 0, 0, tiled=True)


def shards(power0, charge0, dyn_dual0, feeder_dual0, price, inflow, power_limit, capacity, feeder_limit,
           block_values, block_cols, block_offsets):
    groups, local = power0.shape
    pieces = local // LANES
    blocks, blk = block_values.shape[:2]
    feeds = block_offsets.shape[0] - 1
    chips = lax.axis_size("z")
    first_rows, slot_rows, lines = rows_up(5 * pieces), rows_up(2 * pieces + 1), 1 + pieces
    dims = (pieces, groups)
    row, line, square, own = (pieces * groups, LANES), (1, LANES), (blk, LANES), (groups, local)
    spread, sums = (feeds, blk, LANES), (pieces * groups, 8, LANES)
    matrix_specs = [VMEM, VMEM]
    work, moved = 2 * blocks * blk * LANES, 4 * blocks * blk * LANES

    inputs = stacked(power0, charge0, dyn_dual0, price, inflow, power_limit, capacity)
    duals = stacked(feeder_dual0.reshape(feeds, blk), feeder_limit.reshape(feeds, blk))
    tables = lax.optimization_barrier(jnp.concatenate([block_cols, block_offsets]))
    block_cols, block_offsets = tables[:blocks], tables[blocks:]
    index_all = lax.broadcasted_iota(jnp.int32, (blocks, feeds - 1), 0)
    row_of = jnp.sum((index_all >= block_offsets[None, 1:-1]).astype(jnp.int32), axis=1)
    matrix = (block_values, jnp.concatenate([row_of, (block_cols % pieces) * groups + block_cols // pieces]))

    edges, swapped = call(edges_kernel, "edges", [VMEM], [(2, local), (3, local)], flops=EARLY_COPY_FLOPS)(inputs)
    swapped = lax.ppermute(swapped, "core", [(0, 1), (1, 0)])
    links = [(i, i + 1 if i % 2 else i - 1) for i in range(1, 2 * chips - 1)]
    across = lax.ppermute(edges, ("z", "core"), links)
    first, duals_t, limits_t, pushed = call(
        functools.partial(first_kernel, dims, first_rows), "first",
        [VMEM] * 4, [(groups * first_rows, LANES), square, square, row],
        [spread] + [sums] * ADJOINT_PARTS, work, moved, table=2 * blocks,
    )(duals, inputs, *matrix)
    first, across, swapped = lax.optimization_barrier((first, across, swapped))
    first = exchange(first.reshape(groups, first_rows, LANES), "bat").reshape(groups * first_rows, LANES)

    both = (2, groups * slot_rows, LANES)
    step_outs = [line, row] + [own] * 3 + [(1, local), square, row, both]
    scratch = [row, spread] + [sums] * ADJOINT_PARTS
    for iteration in range(ITERS):
        last = iteration + 1 == ITERS
        outs = [own] * 3 + [(feeds, blk)] if last else step_outs
        sizes = (dims, first_rows, slot_rows)
        if iteration == 0:
            results = call(
                functools.partial(step_one_kernel, *sizes), "step_one", [VMEM] * 7 + matrix_specs, outs, scratch,
                2 * work, moved, table=2 * blocks,
            )(first, across, swapped, pushed, inputs, duals_t, limits_t, *matrix)
        else:
            results = call(
                functools.partial(last_kernel if last else step_kernel, *sizes), "last" if last else "step",
                [VMEM] * 13 + matrix_specs, outs, scratch[:2] if last else scratch, 2 * work, moved,
                table=2 * blocks,
            )(first, received, parts, weight, power_row, power, charge, dyn, edge, pushed, inputs, duals_t, limits_t,
              *matrix)
        if not last:
            weight, power_row, power, charge, dyn, edge, duals_t, pushed, slots = results
            received = exchange(slots.reshape(2 * groups, slot_rows, LANES), ("core", "bat")).reshape(both)
            parts = call(
                functools.partial(relay_kernel, dims, slot_rows), "relay", [VMEM], [(chips * lines, LANES)]
            )(received)[0]
            parts = exchange(parts.reshape(chips, lines, LANES), "z").reshape(chips * lines, LANES)
    power, charge, dyn_dual, feeder_dual = results
    return power, charge, dyn_dual, feeder_dual.reshape(1, feeds * blk)


def solution(mesh):
    fine = jax.sharding.Mesh(
        mesh.devices.reshape(mesh.shape["tm"] // 2, 2, mesh.shape["bat"]), ("z", "core", "bat")
    )
    split = P(("z", "core"), "bat")
    steps = P(("z", "core", "bat"), None)
    return jax.shard_map(
        shards,
        mesh=fine,
        in_specs=(split, split, split, steps, split, split, P("bat"), P("bat"), P(), P(), P(), P()),
        out_specs=(split, split, split, steps),
        check_vma=False,
    )
```

```python
import functools

import jax
import jax.numpy as jnp
from jax import lax
from jax.experimental import pallas as pl
from jax.experimental.pallas import tpu as pltpu
from jax.sharding import PartitionSpec as P

ITERS = 4
ETA_STEP = 0.4
EPS_NORM = 1e-06
LANES = 128
HALF = LANES // 2
ADJOINT_UNROLL = 24
ADJOINT_PARTS = 2
APPLY_UNROLL = 8
EARLY_COPY_FLOPS = 2 * 10**10
F32 = jnp.float32


VMEM = pl.BlockSpec(memory_space=pltpu.VMEM)

POWER, CHARGE, DYN, PRICE, INFLOW, LIMIT, CAPACITY = range(7)
SLOT_DYN, SLOT_PUSHED, SLOT_POWER, SLOT_PRICE, SLOT_LIMIT = range(5)


def places():
    return lax.axis_index("z"), lax.axis_index("core"), lax.axis_index("bat")


def rows_up(count):
    return -(-count // 8) * 8


def lane_iota(shape):
    return lax.broadcasted_iota(jnp.int32, shape, len(shape) - 1)


def clip(value, low, high):
    return jnp.minimum(jnp.maximum(value, low), high)


def total(value):
    return jnp.sum(jnp.sum(value, axis=0, keepdims=True), axis=1, keepdims=True)


def take_row(ref, array, pieces, groups, slot_rows):
    parts = [ref[pl.ds(array * pieces + i, groups, stride=slot_rows), :] for i in range(pieces)]
    return jnp.concatenate(parts, axis=0)


def put_row(ref, array, value, pieces, groups, slot_rows):
    for i in range(pieces):
        ref[pl.ds(array * pieces + i, groups, stride=slot_rows), :] = value[i * groups : (i + 1) * groups]


def unrolled(count, most):
    return max(u for u in range(1, most + 1) if count % u == 0)


def adjoint_loop(values, table, spread, sums, begin, end):
    blocks, blk = values.shape[:2]
    ways = unrolled(end - begin, ADJOINT_UNROLL)

    def step(k, carry):
        for u in range(ways):
            j = begin + k * ways + u
            product = values[j] * spread[table[j]]
            c = table[blocks + j]
            part = sums[u % len(sums)]
            part[c] = part[c] + jnp.sum(product.reshape(blk // 8, 8, LANES), axis=0)
        return carry

    lax.fori_loop(0, (end - begin) // ways, step, 0)


def adjoint_start(sums):
    for part in sums:
        part[...] = jnp.zeros_like(part)


def adjoint_total(sums):
    return jnp.sum(sum(part[...] for part in sums), axis=1)


def feeder_adjoint(values, table, spread, sums):
    adjoint_loop(values, table, spread, sums, 0, values.shape[0])
    return adjoint_total(sums)


def feeder_duals(values, table, load, field, weight, duals_t, limits_t, spread, local):
    blocks, blk = values.shape[:2]
    feeds = spread.shape[0]
    ways = unrolled(blocks, APPLY_UNROLL)
    step_dual = ETA_STEP * weight[:, :1]
    shifted = duals_t - step_dual * limits_t
    lane = lane_iota((blk, LANES))
    for f in range(feeds):
        spread[f] = jnp.where(lane == f, shifted, 0.0)
    load.wait()

    def step(k, carry):
        for u in range(ways):
            j = k * ways + u
            f = table[j]
            spread[f] = spread[f] + values[j] * field[pl.ds(table[blocks + j], 1), :]
        return carry

    lax.fori_loop(0, blocks // ways, step, 0)
    squares = local()
    new = jnp.zeros((blk, LANES), F32)
    for f in range(feeds):
        dual = jnp.maximum(0.0, jnp.sum(spread[f], axis=1, keepdims=True))
        spread[f] = jnp.broadcast_to(dual, (blk, LANES))
        new = jnp.where(lane == f, dual, new)
    return new, squares


def pack_sums(primal, dual):
    lane = lane_iota(primal.shape)
    return jnp.where(
        lane < HALF, primal + pltpu.roll(primal, HALF, 1), dual + pltpu.roll(dual, HALF, 1)
    )


def next_weight(weight, parts):
    both = jnp.sum(parts, axis=0, keepdims=True)
    lane = lane_iota(both.shape)
    primal_sq = total(jnp.where(lane < HALF, both, 0.0))
    dual_sq = total(jnp.where(lane < HALF, 0.0, both))
    ratio = jnp.sqrt((dual_sq + EPS_NORM) / (primal_sq + EPS_NORM))
    return jnp.broadcast_to(jnp.sqrt(weight[:, :1] * ratio), (1, LANES))


def row_sum(value):
    return jnp.sum(value, axis=0, keepdims=True)


def table_load(table_in, table, sem):
    copy = pltpu.make_async_copy(table_in, table, sem)
    copy.start()
    return copy


def edges_kernel(inputs, edges, swapped):
    last = inputs.shape[1] - 1
    edges[:1, :] = jnp.where(lax.axis_index("core") == 0, inputs[DYN, :1, :], inputs[DYN, last:, :])
    edges[1:, :] = inputs[CHARGE, last:, :]
    for k, (array, line) in enumerate(((DYN, 0), (DYN, last), (CHARGE, last))):
        swapped[k : k + 1, :] = inputs[array, line : line + 1, :]


def first_kernel(dims, first_rows, duals, inputs, values, table_in, slots, duals_t, limits_t, pushed_out,
                 spread, *rest):
    pieces, groups = dims
    *sums, table, sem = rest
    load = table_load(table_in, table, sem)
    blocks, blk = values.shape[:2]
    feeds = duals.shape[1]
    for i, target in enumerate((duals_t, limits_t)):
        padded = jnp.concatenate([duals[i], jnp.zeros((blk - feeds, LANES), F32)], axis=0)
        target[...] = jnp.transpose(padded)
    for f in range(feeds):
        spread[f] = jnp.broadcast_to(duals_t[:, f : f + 1], (blk, LANES))
    sent = ((SLOT_DYN, DYN), (SLOT_POWER, POWER), (SLOT_PRICE, PRICE), (SLOT_LIMIT, LIMIT))
    for i in range(pieces):
        for slot, array in sent:
            slots[pl.ds(slot * pieces + i, groups, stride=first_rows), :] = inputs[array, :, i * LANES : (i + 1) * LANES]
    adjoint_start(sums)
    load.wait()
    adjoint_loop(values, table, spread, sums, 0, blocks)
    pushed = adjoint_total(sums)
    pushed_out[...] = pushed
    put_row(slots, SLOT_PUSHED, pushed, pieces, groups, first_rows)


def local_step(dims, slot_rows, weight, received, inputs, state, edges, state_out, edge_out):
    pieces, groups = dims
    step_primal = ETA_STEP / weight[:, :1]
    step_dual = ETA_STEP * weight[:, :1]
    after, before_dyn, before_charge = edges
    z, core, _ = places()
    begin = (z == 0) & (core == 0)
    line = lax.broadcasted_iota(jnp.int32, (groups, LANES), 0)
    primal = jnp.zeros((1, LANES), F32)
    dual = jnp.zeros((1, LANES), F32)
    for i in range(pieces):
        cut = slice(i * LANES, (i + 1) * LANES)
        power, charge, dyn = (read(cut) for read in state)
        price, inflow, limit, capacity = (inputs[array, :, cut] for array in (PRICE, INFLOW, LIMIT, CAPACITY))
        pushed = received[pl.ds(SLOT_PUSHED * pieces + i, groups, stride=slot_rows), :]
        power_new = clip(power - step_primal * (price - dyn + pushed), -limit, limit)
        dyn_next = jnp.where(line == groups - 1, after(i), pltpu.roll(dyn, groups - 1, 0))
        charge_new = clip(charge - step_primal * (dyn - dyn_next), 0.0, capacity)
        power_bar = 2.0 * power_new - power
        charge_bar = 2.0 * charge_new - charge
        edge_charge = before_charge(i)
        edge_new = clip(edge_charge - step_primal * (before_dyn(i) - dyn[:1]), 0.0, capacity[:1])
        edge_bar = jnp.where(begin, 0.0, 2.0 * edge_new - edge_charge)
        prev_bar = jnp.where(line == 0, edge_bar, pltpu.roll(charge_bar, 1, 0))
        dyn_new = dyn + step_dual * (charge_bar - prev_bar - power_bar - inflow)
        for ref, value in zip(state_out, (power_new, charge_new, dyn_new)):
            ref[:, cut] = value
        if edge_out is not None:
            edge_out[:, cut] = edge_new
        primal = primal + row_sum((power_new - power) ** 2 + (charge_new - charge) ** 2)
        dual = dual + row_sum((dyn_new - dyn) ** 2)
    return primal, dual


def row_power(dims, first_rows, weight, first, power, dyn, pushed, bar):
    pieces, groups = dims
    step_primal = ETA_STEP / weight[:, :1]
    price = take_row(first, SLOT_PRICE, pieces, groups, first_rows)
    limit = take_row(first, SLOT_LIMIT, pieces, groups, first_rows)
    new = clip(power - step_primal * (price - dyn + pushed), -limit, limit)
    bar[...] = (ETA_STEP * weight[:, :1]) * (2.0 * new - power)
    return new


def feeder_part(dims, slot_rows, load, weight, local, bar, dyn, duals_t, limits_t, values, table,
                duals_out, pushed_out, slots, spread, sums):
    pieces, groups = dims
    _, core, bat = places()
    new, (primal, dual) = feeder_duals(values, table, load, bar, weight, duals_t[...], limits_t[...], spread, local)
    duals_out[...] = new
    parts = pack_sums(primal, dual + row_sum((new - duals_t[...]) ** 2))
    adjoint_start(sums)
    slots[...] = jnp.zeros_like(slots)
    own, other = slots.at[core], slots.at[1 - core]
    for side in (own, other):
        side[pl.ds(2 * pieces, groups, stride=slot_rows), :] = jnp.broadcast_to(parts, (groups, LANES))
    for i in range(pieces):
        cut = slice(i * LANES, (i + 1) * LANES)
        own[pl.ds(SLOT_DYN * pieces + i, groups, stride=slot_rows), :] = dyn[:, cut]
        other[pl.ds(bat * slot_rows + i, 1), :] = dyn[:1, cut]
        other[pl.ds(bat * slot_rows + pieces + i, 1), :] = dyn[groups - 1 :, cut]
    pushed = feeder_adjoint(values, table, spread, sums)
    pushed_out[...] = pushed
    put_row(own, SLOT_PUSHED, pushed, pieces, groups, slot_rows)


def step_one_kernel(dims, first_rows, slot_rows, first, across, swapped, pushed_row, inputs, duals_t, limits_t, values,
                    table_in, weight, power_row, power_out, charge_out, dyn_out, edge_out, duals_out, pushed_out, slots,
                    bar, spread, *rest):
    *sums, table, sem = rest
    pieces, groups = dims
    load = table_load(table_in, table, sem)
    weight[...] = jnp.ones_like(weight)
    state = [lambda cut, array=array: inputs[array, :, cut] for array in (POWER, CHARGE, DYN)]
    core = lax.axis_index("core")
    linked = lambda k, i: across[k : k + 1, i * LANES : (i + 1) * LANES]
    partner = lambda k, i: swapped[k : k + 1, i * LANES : (i + 1) * LANES]
    edges = (
        lambda i: jnp.where(core == 0, partner(0, i), linked(0, i)),
        lambda i: jnp.where(core == 0, linked(0, i), partner(1, i)),
        lambda i: jnp.where(core == 0, linked(1, i), partner(2, i)),
    )
    local = lambda: local_step(dims, first_rows, weight[...], first, inputs, state, edges,
                              (power_out, charge_out, dyn_out), edge_out)
    power_row[...] = row_power(dims, first_rows, weight[...], first,
                               take_row(first, SLOT_POWER, pieces, groups, first_rows),
                               take_row(first, SLOT_DYN, pieces, groups, first_rows), pushed_row[...], bar)
    feeder_part(dims, slot_rows, load, weight[...], local, bar, dyn_out, duals_t, limits_t, values, table,
                duals_out, pushed_out, slots, spread, sums)


def later_edges(dims, slot_rows, received, parts, edge_in):
    pieces, _ = dims
    z, core, bat = places()
    chips = lax.axis_size("z")
    lines = parts.shape[0] // chips
    above, below = jnp.minimum(z + 1, chips - 1), jnp.maximum(z - 1, 0)
    end = jnp.where(z == chips - 1, 0.0, 1.0).astype(F32)
    after = lambda i: jnp.where(
        core == 0, received[1, pl.ds(bat * slot_rows + i, 1), :], end * parts[pl.ds(above * lines + 1 + i, 1), :]
    )
    before_dyn = lambda i: jnp.where(
        core == 0, parts[pl.ds(below * lines + 1 + i, 1), :], received[0, pl.ds(bat * slot_rows + pieces + i, 1), :]
    )
    before_charge = lambda i: edge_in[:, i * LANES : (i + 1) * LANES]
    return after, before_dyn, before_charge


def later_weight(weight_in, parts):
    chips = lax.axis_size("z")
    return next_weight(weight_in[...], parts[pl.ds(0, chips, stride=parts.shape[0] // chips), :])


def step_kernel(dims, first_rows, slot_rows, first, received, parts, weight_in, row_in, power, charge, dyn, edge_in,
                pushed_row, inputs, duals_t, limits_t, values, table_in, weight, power_row, power_out, charge_out,
                dyn_out, edge_out, duals_out, pushed_out, slots, bar, spread, *rest):
    *sums, table, sem = rest
    load = table_load(table_in, table, sem)
    weight[...] = later_weight(weight_in, parts)
    own = received.at[lax.axis_index("core")]
    state = [lambda cut, ref=ref: ref[:, cut] for ref in (power, charge, dyn)]
    local = lambda: local_step(dims, slot_rows, weight[...], own, inputs, state,
                              later_edges(dims, slot_rows, received, parts, edge_in),
                              (power_out, charge_out, dyn_out), edge_out)
    power_row[...] = row_power(dims, first_rows, weight[...], first, row_in[...],
                               take_row(own, SLOT_DYN, *dims, slot_rows), pushed_row[...], bar)
    feeder_part(dims, slot_rows, load, weight[...], local, bar, dyn_out, duals_t, limits_t, values, table,
                duals_out, pushed_out, slots, spread, sums)


def last_kernel(dims, first_rows, slot_rows, first, received, parts, weight_in, row_in, power, charge, dyn, edge_in,
                pushed_row, inputs, duals_t, limits_t, values, table_in, power_out, charge_out, dyn_out, duals_out,
                bar, spread, table, sem):
    load = table_load(table_in, table, sem)
    weight = later_weight(weight_in, parts)
    own = received.at[lax.axis_index("core")]
    state = [lambda cut, ref=ref: ref[:, cut] for ref in (power, charge, dyn)]
    local = lambda: local_step(dims, slot_rows, weight, own, inputs, state, later_edges(dims, slot_rows, received, parts, edge_in),
               (power_out, charge_out, dyn_out), None)
    row_power(dims, first_rows, weight, first, row_in[...], take_row(own, SLOT_DYN, *dims, slot_rows),
              pushed_row[...], bar)
    new, _ = feeder_duals(values, table, load, bar, weight, duals_t[...], limits_t[...], spread, local)
    duals_out[...] = jnp.transpose(new)[: duals_out.shape[0]]


def relay_kernel(dims, slot_rows, received, parts):
    pieces, groups = dims
    z, core, bat = places()
    chips = lax.axis_size("z")
    lines = parts.shape[0] // chips
    parts[...] = jnp.zeros_like(parts)
    summed = sum(row_sum(received[k, pl.ds(2 * pieces, groups, stride=slot_rows), :]) for k in range(2))
    parts[pl.ds(0, chips, stride=lines), :] = jnp.broadcast_to(summed, (chips, LANES))

    @pl.when((core == 1) & (z > 0))
    def _():
        for i in range(pieces):
            parts[pl.ds((z - 1) * lines + 1 + i, 1), :] = received[0, pl.ds(bat * slot_rows + i, 1), :]

    @pl.when((core == 0) & (z < chips - 1))
    def _():
        for i in range(pieces):
            parts[pl.ds((z + 1) * lines + 1 + i, 1), :] = received[1, pl.ds(bat * slot_rows + pieces + i, 1), :]


def shapes(*dims):
    return [jax.ShapeDtypeStruct(dim, F32) for dim in dims]


def call(kernel, name, in_specs, out_dims, scratch=(), flops=0, moved=0, limit=16 * 1024 * 1024, copies=0, table=0):
    more = [pltpu.SemaphoreType.DMA((copies,))] if copies else []
    if table:
        more += [pltpu.SMEM((table,), jnp.int32), pltpu.SemaphoreType.DMA]
    return pl.pallas_call(
        kernel,
        name=name,
        in_specs=in_specs,
        out_specs=[VMEM] * len(out_dims),
        out_shape=shapes(*out_dims),
        scratch_shapes=[pltpu.VMEM(dim, F32) for dim in scratch] + more,
        compiler_params=pltpu.CompilerParams(vmem_limit_bytes=limit),
        cost_estimate=pl.CostEstimate(flops=flops, bytes_accessed=moved, transcendentals=0),
    )


def stacked(*arrays):
    shape = (len(arrays),) + arrays[0].shape
    index = lax.broadcasted_iota(jnp.int32, shape, 0)
    out = jnp.broadcast_to(arrays[-1], shape)
    for i, array in enumerate(arrays[:-1]):
        out = jnp.where(index == i, array, out)
    return out


def exchange(value, axis):
    return lax.all_to_all(value, axis, 0, 0, tiled=True)


def shards(power0, charge0, dyn_dual0, feeder_dual0, price, inflow, power_limit, capacity, feeder_limit,
           block_values, block_cols, block_offsets):
    groups, local = power0.shape
    pieces = local // LANES
    blocks, blk = block_values.shape[:2]
    feeds = block_offsets.shape[0] - 1
    chips = lax.axis_size("z")
    first_rows, slot_rows, lines = rows_up(5 * pieces), rows_up(2 * pieces + 1), 1 + pieces
    dims = (pieces, groups)
    row, line, square, own = (pieces * groups, LANES), (1, LANES), (blk, LANES), (groups, local)
    spread, sums = (feeds, blk, LANES), (pieces * groups, 8, LANES)
    matrix_specs = [VMEM, VMEM]
    work, moved = 2 * blocks * blk * LANES, 4 * blocks * blk * LANES

    inputs = stacked(power0, charge0, dyn_dual0, price, inflow, power_limit, capacity)
    duals = stacked(feeder_dual0.reshape(feeds, blk), feeder_limit.reshape(feeds, blk))
    tables = lax.optimization_barrier(jnp.concatenate([block_cols, block_offsets]))
    block_cols, block_offsets = tables[:blocks], tables[blocks:]
    index_all = lax.broadcasted_iota(jnp.int32, (blocks, feeds - 1), 0)
    row_of = jnp.sum((index_all >= block_offsets[None, 1:-1]).astype(jnp.int32), axis=1)
    matrix = (block_values, jnp.concatenate([row_of, (block_cols % pieces) * groups + block_cols // pieces]))

    edges, swapped = call(edges_kernel, "edges", [VMEM], [(2, local), (3, local)], flops=EARLY_COPY_FLOPS)(inputs)
    swapped = lax.ppermute(swapped, "core", [(0, 1), (1, 0)])
    links = [(i, i + 1 if i % 2 else i - 1) for i in range(1, 2 * chips - 1)]
    across = lax.ppermute(edges, ("z", "core"), links)
    first, duals_t, limits_t, pushed = call(
        functools.partial(first_kernel, dims, first_rows), "first",
        [VMEM] * 4, [(groups * first_rows, LANES), square, square, row],
        [spread] + [sums] * ADJOINT_PARTS, work, moved, table=2 * blocks,
    )(duals, inputs, *matrix)
    first, across, swapped = lax.optimization_barrier((first, across, swapped))
    first = exchange(first.reshape(groups, first_rows, LANES), "bat").reshape(groups * first_rows, LANES)

    both = (2, groups * slot_rows, LANES)
    step_outs = [line, row] + [own] * 3 + [(1, local), square, row, both]
    scratch = [row, spread] + [sums] * ADJOINT_PARTS
    for iteration in range(ITERS):
        last = iteration + 1 == ITERS
        outs = [own] * 3 + [(feeds, blk)] if last else step_outs
        sizes = (dims, first_rows, slot_rows)
        if iteration == 0:
            results = call(
                functools.partial(step_one_kernel, *sizes), "step_one", [VMEM] * 7 + matrix_specs, outs, scratch,
                2 * work, moved, table=2 * blocks,
            )(first, across, swapped, pushed, inputs, duals_t, limits_t, *matrix)
        else:
            results = call(
                functools.partial(last_kernel if last else step_kernel, *sizes), "last" if last else "step",
                [VMEM] * 13 + matrix_specs, outs, scratch[:2] if last else scratch, 2 * work, moved,
                table=2 * blocks,
            )(first, received, parts, weight, power_row, power, charge, dyn, edge, pushed, inputs, duals_t, limits_t,
              *matrix)
        if not last:
            weight, power_row, power, charge, dyn, edge, duals_t, pushed, slots = results
            received = exchange(slots.reshape(2 * groups, slot_rows, LANES), ("core", "bat")).reshape(both)
            parts = call(
                functools.partial(relay_kernel, dims, slot_rows), "relay", [VMEM], [(chips * lines, LANES)]
            )(received)[0]
            parts = exchange(parts.reshape(chips, lines, LANES), "z").reshape(chips * lines, LANES)
    power, charge, dyn_dual, feeder_dual = results
    return power, charge, dyn_dual, feeder_dual.reshape(1, feeds * blk)


def solution(mesh):
    fine = jax.sharding.Mesh(
        mesh.devices.reshape(mesh.shape["tm"] // 2, 2, mesh.shape["bat"]), ("z", "core", "bat")
    )
    split = P(("z", "core"), "bat")
    steps = P(("z", "core", "bat"), None)
    return jax.shard_map(
        shards,
        mesh=fine,
        in_specs=(split, split, split, steps, split, split, P("bat"), P("bat"), P(), P(), P(), P()),
        out_specs=(split, split, split, steps),
        check_vma=False,
    )
```
